32 devices in a mesh: groups: 2 (over y), seq: 4 (over z), chan: 2 (over x), sub: 2 (over core).
Axes of the slice: x: 2, y: 2, z: 4, core: 2. Of those that a mesh axis runs over, the one named last changes fastest.
Arguments:
- features: bfloat16 [3, 4096, 2048], P(None, ('chan', 'sub'), ('groups', 'seq')), parts along dimension 2, may hold values from -6 to 6
- dout: bfloat16 [4096, 2048], P(('chan', 'sub'), ('groups', 'seq')), parts along dimension 1, may hold values from -6 to 6
- filters: bfloat16 [4096, 1024], P(('chan', 'sub'), 'seq'), may hold values from -0.1875 to 0.1875
- taps: float32 [3, 3, 4096], P(None, None, ('chan', 'sub')), may hold values from -3.5 to 3.5
- skip: float32 [4096], P(('chan', 'sub')), may hold values from -4 to 4
- lengths: int32 [32], P('groups'), parts along dimension 0, may hold values from 1 to 256, 1024 in all
Outputs:
- out: bfloat16 [4096, 2048], P(('chan', 'sub'), ('groups', 'seq')), parts along dimension 1
- dfeatures: bfloat16 [3, 4096, 2048], P(None, ('chan', 'sub'), ('groups', 'seq')), parts along dimension 2
The draws below stay inside these ranges and needn't reach their ends.
There are 2 independent parts, one for each index of `groups`. The reference program is written for one: setup_inputs(seed, part) draws one part's arguments, and reference() takes and returns one part's arrays. A program takes and returns all parts, laid end to end along the dimension named above; an argument that names none is the same for every part. Nothing has to cross between parts.
Inputs may be any that keep to these rules, and one draw needn't show every extreme that they name: The lengths of one part sum to 1024, and the longest genome has exactly 256 positions.
All inputs are finite; a program needn't handle non-finite values.
Results may differ from the reference program's by a relative error of at most 0.01.
Values may be sent and summed in bfloat16 or wider, within the bound.
A program may use at most 64 MiB of HBM per device.

```python
import math
import jax
import jax.numpy as jnp
import numpy as np

D = 4096
TAPS = 3
GENOMES = 16
LEN = 1024
MOST = 256


def block_levels(own_key, shape, shards, low, high):
    def one(position, blocks):
        steps = jax.random.uniform(jax.random.fold_in(jax.random.fold_in(own_key, 6), position), (blocks,), jnp.float32, low / len(shards), high / len(shards))
        return jnp.repeat(jnp.exp(steps), shape[position] // blocks).reshape((-1,) + (1,) * (len(shape) - position - 1))

    loudness = one(*shards[0])
    for cut in shards[1:]:
        loudness = loudness * one(*cut)
    return loudness


def length_profile(amount, total, limit, slope):
    portions = [(1 << 20) // math.isqrt(standing ** slope) + 1 for standing in range(2, amount + 1)]
    surplus, counts = total - limit - (amount - 1), [1] * (amount - 1)
    while surplus > 0:
        free = [i for i in range(amount - 1) if counts[i] < limit]
        pool, budget = sum([portions[i] for i in free]), surplus
        for i in free:
            more = min(limit - counts[i], max(1, budget * portions[i] // pool), surplus)
            counts[i] = counts[i] + more
            surplus = surplus - more
    return np.array([limit] + counts)


def uneven(rng, amount, total, reach, skew):
    if amount == 2:
        one = jax.random.randint(rng, (), max(1, total - reach), min(reach, total - 1) + 1)
        return jnp.stack([one, total - one])
    tallies = jnp.asarray(length_profile(amount, total, reach, skew), jnp.int32)
    couples = (amount - 1) // 2
    source_of, sink = tallies[1:1 + 2 * couples:2], tallies[2:2 + 2 * couples:2]
    slack = jnp.minimum(source_of - 1, reach - sink)
    shifted = jax.random.randint(jax.random.fold_in(rng, 1), (couples,), 0, 1 << 20) % (slack + 1)
    tallies = tallies.at[1:1 + 2 * couples:2].set(source_of - shifted).at[2:2 + 2 * couples:2].set(sink + shifted)
    return tallies[jax.random.permutation(jax.random.fold_in(rng, 2), amount)]


def centred(own_key, extent, scale, reach, pieces=(), kind=jnp.bfloat16):
    array = jax.random.normal(own_key, extent, jnp.float32) * scale
    if len(pieces) > 0:
        array = block_levels(own_key, extent, pieces, -0.22, 0.18) * array
    return jnp.clip(array, min=-reach, max=reach).astype(kind)


def setup_inputs(seed: int = 0, part: int = 0) -> dict:
    key_of = jax.random.split(jax.random.key(seed), 7)
    part_keys = jax.random.split(jax.random.fold_in(key_of[6], part), 7)
    return {
        "features": centred(part_keys[0], (3, D, LEN), 1.0, 6.0, ((1, 4), (2, 4))),
        "dout": centred(part_keys[1], (D, LEN), 1.0, 6.0, ((0, 4), (1, 4))),
        "filters": centred(key_of[2], (D, LEN), LEN ** -0.5, 0.1875, ((0, 4), (1, 4))),
        "taps": centred(key_of[3], (3, TAPS, D), TAPS ** -0.5, 3.5, ((2, 4),), jnp.float32),
        "skip": centred(key_of[4], (D,), 1.0, 4.0, ((0, 4),), jnp.float32),
        "lengths": uneven(part_keys[5], GENOMES, LEN, MOST, 2).astype(jnp.int32),
    }


def genome_offsets(lengths, positions):
    ends_at = jnp.cumsum(lengths, dtype=jnp.int32)
    before = (ends_at[None, :] <= positions[:, None]).astype(jnp.int32)
    return positions - jnp.sum(before * lengths[None, :], axis=1, dtype=jnp.int32)


def short_forward(extended, taps_local, offsets):
    span_rows = offsets.shape[0]
    count = taps_local.shape[1]
    result = jnp.zeros(extended.shape[:2] + (span_rows,), jnp.float32)
    for tap_index in range(count):
        begin = count - 1 - tap_index
        window = extended[:, :, begin:begin + span_rows].astype(jnp.float32)
        keep_mask = (offsets >= tap_index).astype(jnp.float32)
        result = result + taps_local[:, tap_index, :, None] * window * keep_mask[None, None, :]
    return result


def short_backward(grads_ext, taps_local, offsets_ext):
    count = taps_local.shape[1]
    span_rows = offsets_ext.shape[0] - (count - 1)
    result = jnp.zeros(grads_ext.shape[:2] + (span_rows,), jnp.float32)
    for tap_index in range(count):
        window = grads_ext[:, :, tap_index:tap_index + span_rows]
        keep_mask = (offsets_ext[tap_index:tap_index + span_rows] >= tap_index).astype(jnp.float32)
        result = result + taps_local[:, tap_index, :, None] * window * keep_mask[None, None, :]
    return result


def reference(features, dout, filters, taps, skip, lengths):
    margin = TAPS - 1
    positions = jnp.arange(LEN, dtype=jnp.int32)
    offsets = genome_offsets(lengths, positions)
    extended = jnp.pad(features, ((0, 0), (0, 0), (margin, 0)))
    filtered = short_forward(extended, taps, offsets).astype(jnp.bfloat16)
    query_side = filtered[0].astype(jnp.float32)
    key_side = filtered[1].astype(jnp.float32)
    value_side = filtered[2].astype(jnp.float32)
    dout_f = dout.astype(jnp.float32)
    mixed = (key_side * value_side).astype(jnp.bfloat16).astype(jnp.float32)
    grad_in = (dout_f * query_side).astype(jnp.bfloat16).astype(jnp.float32)
    length_fft = 2 * LEN
    filt_spec = jnp.fft.rfft(filters.astype(jnp.float32), n=length_fft, axis=1)
    mixed_spec = jnp.fft.rfft(mixed, n=length_fft, axis=1)
    grad_spec = jnp.fft.rfft(grad_in, n=length_fft, axis=1)
    conv = jnp.fft.irfft(filt_spec * mixed_spec, n=length_fft, axis=1)[:, :LEN]
    corr = jnp.fft.irfft(jnp.conj(filt_spec) * grad_spec, n=length_fft, axis=1)[:, :LEN]
    conv = conv.astype(jnp.float32)
    corr = corr.astype(jnp.float32)
    y_out = (conv + skip[:, None] * mixed).astype(jnp.bfloat16).astype(jnp.float32)
    dmixed = (corr + skip[:, None] * grad_in).astype(jnp.bfloat16).astype(jnp.float32)
    out = (query_side * y_out).astype(jnp.bfloat16)
    grads = jnp.stack([dout_f * y_out, dmixed * value_side, dmixed * key_side])
    grads_ext = jnp.pad(grads, ((0, 0), (0, 0), (0, margin)))
    offsets_ext = genome_offsets(lengths, jnp.arange(LEN + margin, dtype=jnp.int32))
    dfeatures = short_backward(grads_ext, taps, offsets_ext).astype(jnp.bfloat16)
    return (out, dfeatures)
```

```python
import functools

import jax
import numpy as np
import jax.numpy as jnp
from jax import lax
from jax.experimental import pallas as pl
from jax.experimental.pallas import tpu as pltpu
from jax.sharding import PartitionSpec as P

HIGHEST = lax.Precision.HIGHEST
TWO_PI = 6.283185307179586


def shifted(value, axis, steps):
    count = lax.axis_size(axis)
    leading, last = (max(0, -steps), min(count, count - steps))
    return lax.ppermute(value, axis, [(source, source + steps) for source in range(leading, last)])


def genome_offsets(lengths, positions):
    order = jnp.arange(lengths.shape[0], dtype=jnp.int32)
    so_far = (order[None, :] <= order[:, None]).astype(jnp.int32)
    ends_at = jnp.sum(so_far * lengths[None, :], axis=1, dtype=jnp.int32)
    before = (ends_at[None, :] <= positions[:, None]).astype(jnp.int32)
    return positions - jnp.sum(before * lengths[None, :], axis=1, dtype=jnp.int32)


def short_forward(extended, taps_local, offsets):
    span_rows = offsets.shape[0]
    count = taps_local.shape[1]
    result = jnp.zeros(extended.shape[:2] + (span_rows,), jnp.float32)
    for tap_index in range(count):
        begin = count - 1 - tap_index
        window = extended[:, :, begin : begin + span_rows].astype(jnp.float32)
        keep_mask = (offsets >= tap_index).astype(jnp.float32)
        result = result + taps_local[:, tap_index, :, None] * window * keep_mask[None, None, :]
    return result


def short_backward(grads_ext, taps_local, offsets_ext):
    count = taps_local.shape[1]
    span_rows = offsets_ext.shape[0] - (count - 1)
    result = jnp.zeros(grads_ext.shape[:2] + (span_rows,), jnp.float32)
    for tap_index in range(count):
        window = grads_ext[:, :, tap_index : tap_index + span_rows]
        keep_mask = (offsets_ext[tap_index : tap_index + span_rows] >= tap_index).astype(
            jnp.float32
        )
        result = result + taps_local[:, tap_index, :, None] * window * keep_mask[None, None, :]
    return result


def dft_table(rows_n, cols_n, period):
    row_ids = jnp.arange(rows_n, dtype=jnp.int32)
    col_ids = jnp.arange(cols_n, dtype=jnp.int32)
    phase = row_ids[:, None] * col_ids[None, :] % period
    angles = phase.astype(jnp.float32) * (-TWO_PI / period)
    return (jnp.cos(angles), jnp.sin(angles))


def forward_transform(signal, tables):
    (row_re, row_im), (twid_re, twid_im), (col_re, col_im) = tables
    half_rows = signal.shape[1] // 128
    blocks_in = signal.reshape(signal.shape[0], half_rows, 128)
    part_re = jnp.einsum("kn,cnm->ckm", row_re[:, :half_rows], blocks_in, precision=HIGHEST)
    part_im = jnp.einsum("kn,cnm->ckm", row_im[:, :half_rows], blocks_in, precision=HIGHEST)
    turned_re = part_re * twid_re - part_im * twid_im
    turned_im = part_re * twid_im + part_im * twid_re
    spec_re = jnp.einsum("ckn,nm->ckm", turned_re, col_re, precision=HIGHEST) - jnp.einsum(
        "ckn,nm->ckm", turned_im, col_im, precision=HIGHEST
    )
    spec_im = jnp.einsum("ckn,nm->ckm", turned_re, col_im, precision=HIGHEST) + jnp.einsum(
        "ckn,nm->ckm", turned_im, col_re, precision=HIGHEST
    )
    return (spec_re, spec_im)


def inverse_transform(spec_re, spec_im, tables):
    (row_re, row_im), (twid_re, twid_im), (col_re, col_im) = tables
    rows_n = spec_re.shape[1]
    half_rows = rows_n // 2
    mid_re = jnp.einsum("ckn,nm->ckm", spec_re, col_re, precision=HIGHEST) + jnp.einsum(
        "ckn,nm->ckm", spec_im, col_im, precision=HIGHEST
    )
    mid_im = jnp.einsum("ckn,nm->ckm", spec_im, col_re, precision=HIGHEST) - jnp.einsum(
        "ckn,nm->ckm", spec_re, col_im, precision=HIGHEST
    )
    back_re = mid_re * twid_re + mid_im * twid_im
    back_im = mid_im * twid_re - mid_re * twid_im
    signal = jnp.einsum("nk,ckm->cnm", row_re[:half_rows], back_re, precision=HIGHEST) + jnp.einsum(
        "nk,ckm->cnm", row_im[:half_rows], back_im, precision=HIGHEST
    )
    return signal.reshape(signal.shape[0], half_rows * 128) * (1.0 / (rows_n * 128))


def long_filter(filt, mixed_in, grad_in, skip_part):
    rows_n = 2 * mixed_in.shape[1] // 128
    tables = (
        dft_table(rows_n, rows_n, rows_n),
        dft_table(rows_n, 128, rows_n * 128),
        dft_table(128, 128, 128),
    )
    mixed_f = mixed_in.astype(jnp.float32)
    grad_f = grad_in.astype(jnp.float32)
    filt_re, filt_im = forward_transform(filt.astype(jnp.float32), tables)
    mix_re, mix_im = forward_transform(mixed_f, tables)
    grad_re, grad_im = forward_transform(grad_f, tables)
    conv_out = inverse_transform(
        filt_re * mix_re - filt_im * mix_im, filt_re * mix_im + filt_im * mix_re, tables
    )
    corr_out = inverse_transform(
        filt_re * grad_re + filt_im * grad_im, filt_re * grad_im - filt_im * grad_re, tables
    )
    y_out = (conv_out + skip_part[:, None] * mixed_f).astype(jnp.bfloat16)
    dmixed = (corr_out + skip_part[:, None] * grad_f).astype(jnp.bfloat16)
    return (y_out, dmixed)


DENSE_MAX = 1024
FINE = 32


def angle_parts(length):
    base = np.arange(length, dtype=np.int64) * 4 + 1
    fine = np.arange(FINE, dtype=np.int64)[:, None] * base[None, :] % (4 * length)
    coarse = np.arange(0, length, FINE, dtype=np.int64)[:, None] * base[None, :] % (4 * length)
    scale = 2.0 * np.pi / (4 * length)
    return [
        func(part * scale).astype(np.float32)
        for part in (coarse, fine)
        for func in (np.cos, np.sin)
    ]


def dense_filter(filt, mixed_in, grad_in, skip_part):
    length = mixed_in.shape[1]
    cc, cs, fc, fs = [jnp.asarray(p)[:, None] if i < 2 else jnp.asarray(p)[None] for i, p in enumerate(angle_parts(length))]
    cos_t = (cc * fc - cs * fs).reshape(length, length)
    sin_t = (cs * fc + cc * fs).reshape(length, length)
    table = jnp.concatenate([cos_t, sin_t], axis=1).astype(jnp.bfloat16)

    def fwd(x):
        return jnp.dot(x, table, preferred_element_type=jnp.float32)

    def inv(x):
        return lax.dot_general(x.astype(jnp.bfloat16), table, (((1,), (1,)), ((), ())), preferred_element_type=jnp.float32) * (1.0 / length)

    h, m, g = fwd(filt), fwd(mixed_in), fwd(grad_in)
    hc, hs = h[:, :length], h[:, length:]
    mc, ms = m[:, :length], m[:, length:]
    gc, gs = g[:, :length], g[:, length:]
    conv_out = inv(jnp.concatenate([hc * mc - hs * ms, hc * ms + hs * mc], axis=1))
    corr_out = inv(jnp.concatenate([hc * gc + hs * gs, hc * gs - hs * gc], axis=1))
    y_out = (conv_out + skip_part[:, None] * mixed_in.astype(jnp.float32)).astype(jnp.bfloat16)
    dmixed = (corr_out + skip_part[:, None] * grad_in.astype(jnp.float32)).astype(jnp.bfloat16)
    return (y_out, dmixed)


def to_channels(stacked):
    return lax.all_to_all(stacked, "seq", split_axis=1, concat_axis=2, tiled=True)


def to_sequence(stacked):
    return lax.all_to_all(stacked, "seq", split_axis=2, concat_axis=1, tiled=True)


def local_general(features, dout, filters, taps, skip, lengths):
    blocks = lax.axis_size("seq")
    seq_rank = lax.axis_index("seq")
    span_rows = features.shape[2]
    channels_here = features.shape[1]
    chan_part = channels_here // blocks
    count = taps.shape[1]
    margin = count - 1
    rim = shifted(features[:, :, span_rows - margin :], "seq", 1)
    extended = jnp.concatenate([rim, features], axis=2)
    first_pos = seq_rank * span_rows
    offsets = genome_offsets(lengths, first_pos + jnp.arange(span_rows, dtype=jnp.int32))
    filtered = short_forward(extended, taps, offsets).astype(jnp.bfloat16)
    query_side = filtered[0].astype(jnp.float32)
    key_side = filtered[1].astype(jnp.float32)
    value_side = filtered[2].astype(jnp.float32)
    dout_f = dout.astype(jnp.float32)
    mixed = (key_side * value_side).astype(jnp.bfloat16)
    grad_in = (dout_f * query_side).astype(jnp.bfloat16)
    moved = to_channels(jnp.stack([mixed, grad_in, filters]))
    skip_part = lax.dynamic_slice_in_dim(skip, seq_rank * chan_part, chan_part, 0)
    run = dense_filter if moved.shape[2] <= DENSE_MAX else long_filter
    y_out, dmixed = run(moved[2], moved[0], moved[1], skip_part)
    returned = to_sequence(jnp.stack([y_out, dmixed]))
    y_here = returned[0].astype(jnp.float32)
    dmixed_here = returned[1].astype(jnp.float32)
    out = (query_side * y_here).astype(jnp.bfloat16)
    grads = jnp.stack([dout_f * y_here, dmixed_here * value_side, dmixed_here * key_side])
    ahead = shifted(grads[:, :, :margin], "seq", -1)
    grads_ext = jnp.concatenate([grads, ahead], axis=2)
    offsets_ext = genome_offsets(
        lengths, first_pos + jnp.arange(span_rows + margin, dtype=jnp.int32)
    )
    dfeatures = short_backward(grads_ext, taps, offsets_ext).astype(jnp.bfloat16)
    return (out, dfeatures)


CH = 128
LAG = 3
BACK = 1
NN = (((1,), (0,)), ((), ()))
NT = (((1,), (1,)), ((), ()))
TN = (((0,), (0,)), ((), ()))
MESH = pl.DeviceIdType.MESH


def mm(a, b, dims=NN):
    return lax.dot_general(a, b, dims, preferred_element_type=jnp.float32)


def block_tables(size):
    place = np.arange(size, dtype=np.int64)
    phase = place[:, None] * (4 * place[None, :] + 1) % (4 * size)
    angle = phase * (2.0 * np.pi / (4 * size))
    cos, sin = np.cos(angle), np.sin(angle)
    there = np.stack([np.concatenate([cos, s * sin], axis=1) for s in (1, -1)])
    back = np.stack([np.concatenate([cos.T, s * sin.T], axis=0) for s in (1, -1)]) / size
    return there.astype(jnp.bfloat16), back.astype(jnp.bfloat16)


def mixer_kernel(
    lengths_ref, feat_hbm, dout_hbm, filt_hbm, taps_hbm, skip_hbm, there_hbm, back_hbm,
    out_ref, df_ref,
    xf, xd, taps_v, skip_v, par, wh, wsig, winv, keep_f, keep_b,
    rim_src, rim, h_all, sig, q_s, k_s, v_s, yd, c_src, c_in, hal_src, hal, spec_s, spec_h, prod,
    ld, rim_ss, rim_rs, h_zs, h_ys, h_bs, h_rs, u_ss, uf_ss, s_rs, c_ss, c_rs, hal_ss, hal_rs,
):
    rank = lax.axis_index("seq")
    group = lax.axis_index("groups")
    channels, span = xd.shape
    count = channels // CH
    half = count // 2
    mir = rank // 2
    inn = lax.rem(rank + mir, 2)
    inner = inn == 1
    inward = rank + 1 - 2 * mir
    outward = rank - 1 + 2 * mir
    far = 3 - 3 * mir
    bf = jnp.bfloat16
    f32 = jnp.float32

    loads = [
        pltpu.make_async_copy(feat_hbm, xf, ld.at[0]),
        pltpu.make_async_copy(taps_hbm, taps_v, ld.at[1]),
        pltpu.make_async_copy(skip_hbm, skip_v, ld.at[2]),
        pltpu.make_async_copy(dout_hbm, xd, ld.at[3]),
        pltpu.make_async_copy(filt_hbm, h_all.at[rank], ld.at[4]),
        pltpu.make_async_copy(there_hbm.at[0], wh, ld.at[5]),
        pltpu.make_async_copy(there_hbm.at[mir], wsig, ld.at[6]),
        pltpu.make_async_copy(back_hbm.at[mir], winv, ld.at[7]),
    ]
    for load in loads:
        load.start()

    barrier = pltpu.get_barrier_semaphore()
    pl.semaphore_signal(barrier, inc=1, device_id={"seq": inward}, device_id_type=MESH)
    pl.semaphore_signal(barrier, inc=1, device_id={"groups": 1 - group}, device_id_type=MESH)

    @pl.when(inner)
    def _():
        pl.semaphore_signal(barrier, inc=1, device_id={"seq": outward}, device_id_type=MESH)

    def rows_of(i):
        c = lax.rem(half * group + i, count)
        return c, pl.ds(pl.multiple_of(c * CH, CH), CH)

    def remote(src, dst, ss, rs, where):
        return pltpu.make_async_remote_copy(
            src_ref=src, dst_ref=dst, send_sem=ss, recv_sem=rs, device_id=where, device_id_type=MESH
        )

    def h_own_copy(i):
        c, rows = rows_of(i)
        return remote(filt_hbm.at[rows], h_all.at[rank, rows], h_zs.at[0, i], h_rs.at[rank, c], {"seq": inward})

    def h_on_copy(i):
        c, rows = rows_of(i)
        return remote(h_all.at[outward, rows], h_all.at[outward, rows], h_zs.at[1, i], h_rs.at[outward, c], {"seq": inward})

    def h_back_copy(i):
        c, rows = rows_of(i)
        return remote(h_all.at[0, rows], h_all.at[0, rows], h_bs.at[i], h_rs.at[0, c], {"seq": 3})

    def h_over_copy(which, slot, i):
        c, rows = rows_of(i)
        return remote(
            h_all.at[slot, rows], h_all.at[slot, rows], h_ys.at[which, i], h_rs.at[slot, c], {"groups": 1 - group}
        )

    def h_arrival(slot, i):
        c, rows = rows_of(i)
        return remote(h_all.at[slot, rows], h_all.at[slot, rows], h_zs.at[0, 0], h_rs.at[slot, c], {"seq": inward})

    def u_copy(i):
        c, rows = rows_of(i)
        return remote(sig.at[0, rows], sig.at[2 + inn, rows], u_ss.at[i], s_rs.at[inn, c], {"seq": inward})

    def u_on_copy(i):
        c, rows = rows_of(i)
        return remote(sig.at[2, rows], sig.at[4, rows], uf_ss.at[i], s_rs.at[2, c], {"seq": inward})

    def sig_arrival(which, i):
        c, rows = rows_of(i)
        return remote(sig.at[2 + which, rows], sig.at[2 + which, rows], u_ss.at[0], s_rs.at[which, c], {"seq": inward})

    def c_copy(i):
        c, rows = rows_of(i)
        return remote(c_src.at[rows], c_in.at[rows], c_ss.at[i], c_rs.at[c], {"seq": outward})

    def rim_copy():
        return remote(rim_src, rim, rim_ss, rim_rs, {"seq": rank + 1})

    def hal_copy(i):
        c, _ = rows_of(i)
        return remote(hal_src.at[c], hal.at[c], hal_ss.at[i], hal_rs.at[c], {"seq": rank - 1})

    @pl.when(rank == 0)
    def _():
        rim[...] = jnp.zeros_like(rim)

    @pl.when(rank == 3)
    def _():
        hal[...] = jnp.zeros_like(hal)

    pl.semaphore_wait(barrier, 2 + inn)

    h_own_copy(0).start()

    loads[0].wait()
    r_id = lax.broadcasted_iota(jnp.int32, (16, 128), 0)
    p_id = lax.broadcasted_iota(jnp.int32, (16, 128), 1)
    total = None
    for a in range(3):
        hit = ((r_id == 2 * a) & (p_id == 126)) | ((r_id == 2 * a + 1) & (p_id == 127))
        term = mm(jnp.where(hit, 1.0, 0.0).astype(bf), xf[a, :, span - 128 :], NT)
        total = term if total is None else total + term
    rim_src[...] = total.astype(bf)

    @pl.when(rank < 3)
    def _():
        rim_copy().start()

    for i in range(1, half):
        h_own_copy(i).start()

    def keeps(ahead, least):
        position = rank * span + ahead + lax.broadcasted_iota(jnp.int32, (8, span), 1)
        offset = position
        end = jnp.int32(0)
        for g in range(lengths_ref.shape[0]):
            one = lengths_ref[g]
            end = end + one
            offset = offset - jnp.where(end <= position, one, 0)
        return jnp.where(offset >= least, 1.0, 0.0)

    for j in (1, 2):
        keep_f[j - 1] = keeps(0, j)
        keep_b[j - 1] = keeps(j, j)

    loads[1].wait()
    loads[2].wait()
    flat = jnp.concatenate(
        [taps_v[0], taps_v[1], taps_v[2], skip_v[...], jnp.zeros((6, channels), f32)], axis=0
    )
    for c in range(count):
        par[c * CH : (c + 1) * CH, 0:16] = flat[:, c * CH : (c + 1) * CH].T
    for load in loads[3:]:
        load.wait()

    @pl.when(rank > 0)
    def _():
        rim_copy().wait_recv()

    rr = lax.broadcasted_iota(jnp.int32, (16, 384), 0)
    cc = lax.broadcasted_iota(jnp.int32, (16, 384), 1)

    def spread(first):
        hit = None
        for a in range(3):
            one = ((rr == 2 * a) & (cc == 128 * a + first)) | ((rr == 2 * a + 1) & (cc == 128 * a + first + 1))
            hit = one if hit is None else hit | one
        return jnp.where(hit, 1.0, 0.0).astype(bf)

    def prepare(i):
        c, rows = rows_of(i)
        edge = mm(rim[:, rows], spread(126), TN)
        tap = par[rows, :]
        result = []
        for a in range(3):
            here = xf[a, rows, :].astype(f32)
            wide = jnp.concatenate([edge[:, 128 * a : 128 * a + 128], here], axis=1)
            acc = tap[:, 3 * a : 3 * a + 1] * here
            for j in (1, 2):
                moved = pltpu.roll(wide, j, 1)[:, 128:]
                acc = acc + tap[:, 3 * a + j : 3 * a + j + 1] * (moved * keep_f[j - 1, 0:1, :])
            result.append(acc.astype(bf))
        q, k, v = result
        q_s[rows, :] = q
        k_s[rows, :] = k
        v_s[rows, :] = v
        sig[mir, rows, :] = (k.astype(f32) * v.astype(f32)).astype(bf)
        sig[1 - mir, rows, :] = (xd[rows, :].astype(f32) * q.astype(f32)).astype(bf)
        u_copy(i).start()

    def pass_on(i):
        sig_arrival(0, i).wait_recv()
        u_on_copy(i).start()

        @pl.when(i < half)
        def _():
            h_arrival(outward, i).wait_recv()
            h_on_copy(i).start()
            h_over_copy(0, outward, i).start()

    def products(terms_of):
        def block(b, carry):
            first = pl.multiple_of(b * 16, 16)

            def pair(ref, k):
                at = pl.ds(k * CH + first, 16)
                return ref[at, 0:span], ref[at, span:]

            for k, terms in enumerate(terms_of(lambda n: pair(spec_h, n), lambda n: pair(spec_s, n))):
                re = im = None
                for (tc, ts), (xc, xs), sign in terms:
                    if sign > 0:
                        new_re, new_im = tc * xc - ts * xs, tc * xs + ts * xc
                    else:
                        new_re, new_im = tc * xc + ts * xs, tc * xs - ts * xc
                    re = new_re if re is None else re + new_re
                    im = new_im if im is None else im + new_im
                at = pl.ds(k * CH + first, 16)
                prod[at, 0:span] = re.astype(bf)
                prod[at, span:] = im.astype(bf)
            return carry

        lax.fori_loop(0, CH // 16, block, 0)

    def inner_terms(h, s):
        hs = [h(k) for k in range(4)]
        t = [hs[0]] + [(hs[k][0] + hs[k - 1][1], hs[k][1] - hs[k - 1][0]) for k in (1, 2, 3)]
        own, other, near, mid, end = [s(k) for k in range(5)]
        return [
            [(t[0], own, 1), (t[1], near, 1)],
            [(t[0], other, -1), (t[1], mid, -1), (t[2], end, -1)],
            [(t[1], other, -1), (t[2], mid, -1), (t[3], end, -1)],
        ]

    def outer_terms(h, s):
        return [[(h(0), s(0), 1)], [(h(0), s(1), -1)]]

    def main_inner(i):
        c, rows = rows_of(i)

        @pl.when(i < half)
        def _():
            h_arrival(inward, i).wait_recv()
            h_over_copy(1, inward, i).start()
            h_arrival(far, i).wait_recv()
            h_over_copy(2, far, i).start()

            @pl.when(rank == 2)
            def _():
                h_back_copy(i).start()

        @pl.when(i >= half)
        def _():
            h_arrival(outward, i).wait_recv()
            h_arrival(inward, i).wait_recv()
            h_arrival(far, i).wait_recv()

        sig_arrival(1, i).wait_recv()
        sig_arrival(2, i).wait_recv()
        spec_h[...] = mm(h_all[:, rows, :].reshape(4 * CH, span), wh[...])
        spec_s[...] = mm(sig[:, rows, :].reshape(5 * CH, span), wsig[...])
        products(inner_terms)
        value = mm(prod[...], winv[...])
        skip = par[rows, 9:10]
        yd[0, rows, :] = (value[0:CH] + skip * sig[0, rows, :].astype(f32)).astype(bf)
        yd[1, rows, :] = (value[CH : 2 * CH] + skip * sig[1, rows, :].astype(f32)).astype(bf)
        c_src[rows, :] = value[2 * CH :].astype(bf)
        c_copy(i).start()

    def main_outer(i):
        c, rows = rows_of(i)

        @pl.when(rank == 3)
        def _():
            h_arrival(0, i).wait_recv()

            @pl.when(i < half)
            def _():
                h_over_copy(0, 0, i).start()

        spec_h[0:CH] = mm(h_all[0, rows, :], wh[...])
        spec_s[0 : 2 * CH] = mm(sig[0:2, rows, :].reshape(2 * CH, span), wsig[...])
        products(outer_terms)
        value = mm(prod[0 : 2 * CH], winv[...])
        skip = par[rows, 9:10]
        yd[0, rows, :] = (value[0:CH] + skip * sig[0, rows, :].astype(f32)).astype(bf)
        base = value[CH:] + skip * sig[1, rows, :].astype(f32)
        c_copy(i).wait_recv()
        yd[1, rows, :] = (base + c_in[rows, :].astype(f32)).astype(bf)

    def grads_of(rows, lanes):
        y = yd[mir, rows, lanes].astype(f32)
        dm = yd[1 - mir, rows, lanes].astype(f32)
        return [
            xd[rows, lanes].astype(f32) * y,
            dm * v_s[rows, lanes].astype(f32),
            dm * k_s[rows, lanes].astype(f32),
        ]

    def halo(i):
        c, rows = rows_of(i)
        edge = None
        for a, grad in enumerate(grads_of(rows, slice(0, 128))):
            hit = ((r_id == 2 * a) & (p_id == 0)) | ((r_id == 2 * a + 1) & (p_id == 1))
            term = mm(jnp.where(hit, 1.0, 0.0).astype(bf), grad.astype(bf), NT)
            edge = term if edge is None else edge + term
        hal_src[c] = edge.astype(bf)
        hal_copy(i).start()

    def finish(i):
        c, rows = rows_of(i)

        @pl.when(rank < 3)
        def _():
            hal_copy(i).wait_recv()

        tap = par[rows, :]
        edge = mm(hal[c], spread(0), TN)
        y = yd[mir, rows, :].astype(f32)
        out_ref[rows, :] = (q_s[rows, :].astype(f32) * y).astype(bf)
        for a, grad in enumerate(grads_of(rows, slice(None))):
            wide = jnp.concatenate([grad, edge[:, 128 * a : 128 * a + 128]], axis=1)
            acc = tap[:, 3 * a : 3 * a + 1] * grad
            for j in (1, 2):
                moved = pltpu.roll(wide, span + 128 - j, 1)[:, :span]
                acc = acc + tap[:, 3 * a + j : 3 * a + j + 1] * (moved * keep_b[j - 1, 0:1, :])
            df_ref[a, rows, :] = acc.astype(bf)

    def step(s, carry):
        @pl.when(s < count)
        def _():
            prepare(s)

        @pl.when(inner & (s >= 1) & (s < count + 1))
        def _():
            pass_on(s - 1)

        main = (s >= LAG) & (s < count + LAG)

        @pl.when(inner & main)
        def _():
            main_inner(s - LAG)

        @pl.when((inn == 0) & main)
        def _():
            main_outer(s - LAG)

        @pl.when((rank > 0) & main)
        def _():
            halo(s - LAG)

        @pl.when(s >= LAG + BACK)
        def _():
            finish(s - LAG - BACK)

        return carry

    lax.fori_loop(0, count + LAG + BACK, step, 0)

    @pl.when(rank < 3)
    def _():
        rim_copy().wait_send()

    def drain(i, carry):
        u_copy(i).wait_send()

        @pl.when(rank > 0)
        def _():
            hal_copy(i).wait_send()

        @pl.when(inner)
        def _():
            u_on_copy(i).wait_send()
            c_copy(i).wait_send()

        @pl.when(i < half)
        def _():
            h_own_copy(i).wait_send()

            @pl.when(inner)
            def _():
                h_on_copy(i).wait_send()
                h_over_copy(0, outward, i).wait_send()
                h_over_copy(1, inward, i).wait_send()
                h_over_copy(2, far, i).wait_send()

            @pl.when(rank == 2)
            def _():
                h_back_copy(i).wait_send()

            @pl.when(rank == 3)
            def _():
                h_over_copy(0, 0, i).wait_send()

        return carry

    lax.fori_loop(0, count, drain, 0)


def local_kernel(features, dout, filters, taps, skip, lengths):
    channels, span = dout.shape
    count = channels // CH
    bf = jnp.bfloat16
    f32 = jnp.float32
    there, back = block_tables(span)
    vmem = pl.BlockSpec(memory_space=pltpu.VMEM)
    smem = pl.BlockSpec(memory_space=pltpu.SMEM)
    hbm = pl.BlockSpec(memory_space=pl.ANY)
    dma = pltpu.SemaphoreType.DMA
    return pl.pallas_call(
        mixer_kernel,
        out_shape=(
            jax.ShapeDtypeStruct(dout.shape, bf),
            jax.ShapeDtypeStruct(features.shape, bf),
        ),
        in_specs=[smem] + [hbm] * 7,
        out_specs=(vmem, vmem),
        scratch_shapes=[
            pltpu.VMEM((3, channels, span), bf),
            pltpu.VMEM((channels, span), bf),
            pltpu.VMEM((3, 3, channels), f32),
            pltpu.VMEM((1, channels), f32),
            pltpu.VMEM((channels, 128), f32),
            pltpu.VMEM((span, 2 * span), bf),
            pltpu.VMEM((span, 2 * span), bf),
            pltpu.VMEM((2 * span, span), bf),
            pltpu.VMEM((2, 8, span), f32),
            pltpu.VMEM((2, 8, span), f32),
            pltpu.VMEM((16, channels), bf),
            pltpu.VMEM((16, channels), bf),
            pltpu.VMEM((4, channels, span), bf),
            pltpu.VMEM((5, channels, span), bf),
            pltpu.VMEM((channels, span), bf),
            pltpu.VMEM((channels, span), bf),
            pltpu.VMEM((channels, span), bf),
            pltpu.VMEM((2, channels, span), bf),
            pltpu.VMEM((channels, span), bf),
            pltpu.VMEM((channels, span), bf),
            pltpu.VMEM((count, 16, CH), bf),
            pltpu.VMEM((count, 16, CH), bf),
            pltpu.VMEM((5 * CH, 2 * span), f32),
            pltpu.VMEM((4 * CH, 2 * span), f32),
            pltpu.VMEM((3 * CH, 2 * span), bf),
            dma((8,)), dma, dma,
            dma((2, count)), dma((3, count)), dma((count,)), dma((4, count)),
            dma((count,)), dma((count,)), dma((3, count)),
            dma((count,)), dma((count,)), dma((count,)), dma((count,)),
        ],
        compiler_params=pltpu.CompilerParams(
            collective_id=0, has_side_effects=True, vmem_limit_bytes=28 * 1024 * 1024
        ),
    )(lengths, features, dout, filters, taps, skip[None], jnp.asarray(there), jnp.asarray(back))


def local(features, dout, filters, taps, skip, lengths):
    channels, span = dout.shape
    fits = lax.axis_size("seq") == 4 and lax.axis_size("groups") == 2 and taps.shape[:2] == (3, 3)
    if fits and span == 256 and channels % (2 * CH) == 0:
        return local_kernel(features, dout, filters, taps, skip, lengths)
    return local_general(features, dout, filters, taps, skip, lengths)


def solution(mesh):
    in_specs = (
        P(None, ("chan", "sub"), ("groups", "seq")),
        P(("chan", "sub"), ("groups", "seq")),
        P(("chan", "sub"), "seq"),
        P(None, None, ("chan", "sub")),
        P(("chan", "sub")),
        P("groups"),
    )
    out_specs = (P(("chan", "sub"), ("groups", "seq")), P(None, ("chan", "sub"), ("groups", "seq")))
    return jax.shard_map(local, mesh=mesh, in_specs=in_specs, out_specs=out_specs, check_vma=False)
```

```python
import functools

import jax
import numpy as np
import jax.numpy as jnp
from jax import lax
from jax.experimental import pallas as pl
from jax.experimental.pallas import tpu as pltpu
from jax.sharding import PartitionSpec as P

HIGHEST = lax.Precision.HIGHEST
TWO_PI = 6.283185307179586


def shifted(value, axis, steps):
    count = lax.axis_size(axis)
    leading, last = (max(0, -steps), min(count, count - steps))
    return lax.ppermute(value, axis, [(source, source + steps) for source in range(leading, last)])


def genome_offsets(lengths, positions):
    order = jnp.arange(lengths.shape[0], dtype=jnp.int32)
    so_far = (order[None, :] <= order[:, None]).astype(jnp.int32)
    ends_at = jnp.sum(so_far * lengths[None, :], axis=1, dtype=jnp.int32)
    before = (ends_at[None, :] <= positions[:, None]).astype(jnp.int32)
    return positions - jnp.sum(before * lengths[None, :], axis=1, dtype=jnp.int32)


def short_forward(extended, taps_local, offsets):
    span_rows = offsets.shape[0]
    count = taps_local.shape[1]
    result = jnp.zeros(extended.shape[:2] + (span_rows,), jnp.float32)
    for tap_index in range(count):
        begin = count - 1 - tap_index
        window = extended[:, :, begin : begin + span_rows].astype(jnp.float32)
        keep_mask = (offsets >= tap_index).astype(jnp.float32)
        result = result + taps_local[:, tap_index, :, None] * window * keep_mask[None, None, :]
    return result


def short_backward(grads_ext, taps_local, offsets_ext):
    count = taps_local.shape[1]
    span_rows = offsets_ext.shape[0] - (count - 1)
    result = jnp.zeros(grads_ext.shape[:2] + (span_rows,), jnp.float32)
    for tap_index in range(count):
        window = grads_ext[:, :, tap_index : tap_index + span_rows]
        keep_mask = (offsets_ext[tap_index : tap_index + span_rows] >= tap_index).astype(
            jnp.float32
        )
        result = result + taps_local[:, tap_index, :, None] * window * keep_mask[None, None, :]
    return result


def dft_table(rows_n, cols_n, period):
    row_ids = jnp.arange(rows_n, dtype=jnp.int32)
    col_ids = jnp.arange(cols_n, dtype=jnp.int32)
    phase = row_ids[:, None] * col_ids[None, :] % period
    angles = phase.astype(jnp.float32) * (-TWO_PI / period)
    return (jnp.cos(angles), jnp.sin(angles))


def forward_transform(signal, tables):
    (row_re, row_im), (twid_re, twid_im), (col_re, col_im) = tables
    half_rows = signal.shape[1] // 128
    blocks_in = signal.reshape(signal.shape[0], half_rows, 128)
    part_re = jnp.einsum("kn,cnm->ckm", row_re[:, :half_rows], blocks_in, precision=HIGHEST)
    part_im = jnp.einsum("kn,cnm->ckm", row_im[:, :half_rows], blocks_in, precision=HIGHEST)
    turned_re = part_re * twid_re - part_im * twid_im
    turned_im = part_re * twid_im + part_im * twid_re
    spec_re = jnp.einsum("ckn,nm->ckm", turned_re, col_re, precision=HIGHEST) - jnp.einsum(
        "ckn,nm->ckm", turned_im, col_im, precision=HIGHEST
    )
    spec_im = jnp.einsum("ckn,nm->ckm", turned_re, col_im, precision=HIGHEST) + jnp.einsum(
        "ckn,nm->ckm", turned_im, col_re, precision=HIGHEST
    )
    return (spec_re, spec_im)


def inverse_transform(spec_re, spec_im, tables):
    (row_re, row_im), (twid_re, twid_im), (col_re, col_im) = tables
    rows_n = spec_re.shape[1]
    half_rows = rows_n // 2
    mid_re = jnp.einsum("ckn,nm->ckm", spec_re, col_re, precision=HIGHEST) + jnp.einsum(
        "ckn,nm->ckm", spec_im, col_im, precision=HIGHEST
    )
    mid_im = jnp.einsum("ckn,nm->ckm", spec_im, col_re, precision=HIGHEST) - jnp.einsum(
        "ckn,nm->ckm", spec_re, col_im, precision=HIGHEST
    )
    back_re = mid_re * twid_re + mid_im * twid_im
    back_im = mid_im * twid_re - mid_re * twid_im
    signal = jnp.einsum("nk,ckm->cnm", row_re[:half_rows], back_re, precision=HIGHEST) + jnp.einsum(
        "nk,ckm->cnm", row_im[:half_rows], back_im, precision=HIGHEST
    )
    return signal.reshape(signal.shape[0], half_rows * 128) * (1.0 / (rows_n * 128))


def long_filter(filt, mixed_in, grad_in, skip_part):
    rows_n = 2 * mixed_in.shape[1] // 128
    tables = (
        dft_table(rows_n, rows_n, rows_n),
        dft_table(rows_n, 128, rows_n * 128),
        dft_table(128, 128, 128),
    )
    mixed_f = mixed_in.astype(jnp.float32)
    grad_f = grad_in.astype(jnp.float32)
    filt_re, filt_im = forward_transform(filt.astype(jnp.float32), tables)
    mix_re, mix_im = forward_transform(mixed_f, tables)
    grad_re, grad_im = forward_transform(grad_f, tables)
    conv_out = inverse_transform(
        filt_re * mix_re - filt_im * mix_im, filt_re * mix_im + filt_im * mix_re, tables
    )
    corr_out = inverse_transform(
        filt_re * grad_re + filt_im * grad_im, filt_re * grad_im - filt_im * grad_re, tables
    )
    y_out = (conv_out + skip_part[:, None] * mixed_f).astype(jnp.bfloat16)
    dmixed = (corr_out + skip_part[:, None] * grad_f).astype(jnp.bfloat16)
    return (y_out, dmixed)


DENSE_MAX = 1024
FINE = 32


def angle_parts(length):
    base = np.arange(length, dtype=np.int64) * 4 + 1
    fine = np.arange(FINE, dtype=np.int64)[:, None] * base[None, :] % (4 * length)
    coarse = np.arange(0, length, FINE, dtype=np.int64)[:, None] * base[None, :] % (4 * length)
    scale = 2.0 * np.pi / (4 * length)
    return [
        func(part * scale).astype(np.float32)
        for part in (coarse, fine)
        for func in (np.cos, np.sin)
    ]


def dense_filter(filt, mixed_in, grad_in, skip_part):
    length = mixed_in.shape[1]
    cc, cs, fc, fs = [jnp.asarray(p)[:, None] if i < 2 else jnp.asarray(p)[None] for i, p in enumerate(angle_parts(length))]
    cos_t = (cc * fc - cs * fs).reshape(length, length)
    sin_t = (cs * fc + cc * fs).reshape(length, length)
    table = jnp.concatenate([cos_t, sin_t], axis=1).astype(jnp.bfloat16)

    def fwd(x):
        return jnp.dot(x, table, preferred_element_type=jnp.float32)

    def inv(x):
        return lax.dot_general(x.astype(jnp.bfloat16), table, (((1,), (1,)), ((), ())), preferred_element_type=jnp.float32) * (1.0 / length)

    h, m, g = fwd(filt), fwd(mixed_in), fwd(grad_in)
    hc, hs = h[:, :length], h[:, length:]
    mc, ms = m[:, :length], m[:, length:]
    gc, gs = g[:, :length], g[:, length:]
    conv_out = inv(jnp.concatenate([hc * mc - hs * ms, hc * ms + hs * mc], axis=1))
    corr_out = inv(jnp.concatenate([hc * gc + hs * gs, hc * gs - hs * gc], axis=1))
    y_out = (conv_out + skip_part[:, None] * mixed_in.astype(jnp.float32)).astype(jnp.bfloat16)
    dmixed = (corr_out + skip_part[:, None] * grad_in.astype(jnp.float32)).astype(jnp.bfloat16)
    return (y_out, dmixed)


def to_channels(stacked):
    return lax.all_to_all(stacked, "seq", split_axis=1, concat_axis=2, tiled=True)


def to_sequence(stacked):
    return lax.all_to_all(stacked, "seq", split_axis=2, concat_axis=1, tiled=True)


def local_general(features, dout, filters, taps, skip, lengths):
    blocks = lax.axis_size("seq")
    seq_rank = lax.axis_index("seq")
    span_rows = features.shape[2]
    channels_here = features.shape[1]
    chan_part = channels_here // blocks
    count = taps.shape[1]
    margin = count - 1
    rim = shifted(features[:, :, span_rows - margin :], "seq", 1)
    extended = jnp.concatenate([rim, features], axis=2)
    first_pos = seq_rank * span_rows
    offsets = genome_offsets(lengths, first_pos + jnp.arange(span_rows, dtype=jnp.int32))
    filtered = short_forward(extended, taps, offsets).astype(jnp.bfloat16)
    query_side = filtered[0].astype(jnp.float32)
    key_side = filtered[1].astype(jnp.float32)
    value_side = filtered[2].astype(jnp.float32)
    dout_f = dout.astype(jnp.float32)
    mixed = (key_side * value_side).astype(jnp.bfloat16)
    grad_in = (dout_f * query_side).astype(jnp.bfloat16)
    moved = to_channels(jnp.stack([mixed, grad_in, filters]))
    skip_part = lax.dynamic_slice_in_dim(skip, seq_rank * chan_part, chan_part, 0)
    run = dense_filter if moved.shape[2] <= DENSE_MAX else long_filter
    y_out, dmixed = run(moved[2], moved[0], moved[1], skip_part)
    returned = to_sequence(jnp.stack([y_out, dmixed]))
    y_here = returned[0].astype(jnp.float32)
    dmixed_here = returned[1].astype(jnp.float32)
    out = (query_side * y_here).astype(jnp.bfloat16)
    grads = jnp.stack([dout_f * y_here, dmixed_here * value_side, dmixed_here * key_side])
    ahead = shifted(grads[:, :, :margin], "seq", -1)
    grads_ext = jnp.concatenate([grads, ahead], axis=2)
    offsets_ext = genome_offsets(
        lengths, first_pos + jnp.arange(span_rows + margin, dtype=jnp.int32)
    )
    dfeatures = short_backward(grads_ext, taps, offsets_ext).astype(jnp.bfloat16)
    return (out, dfeatures)


CH = 128
LAG = 5
BACK = 2
NN = (((1,), (0,)), ((), ()))
NT = (((1,), (1,)), ((), ()))
TN = (((0,), (0,)), ((), ()))
MESH = pl.DeviceIdType.MESH


def mm(a, b, dims=NN):
    return lax.dot_general(a, b, dims, preferred_element_type=jnp.float32)


def block_tables(size):
    place = np.arange(size, dtype=np.int64)
    phase = place[:, None] * (4 * place[None, :] + 1) % (4 * size)
    angle = phase * (2.0 * np.pi / (4 * size))
    cos, sin = np.cos(angle), np.sin(angle)
    there = np.stack([np.concatenate([cos, s * sin], axis=1) for s in (1, -1)])
    back = np.stack([np.concatenate([cos.T, s * sin.T], axis=0) for s in (1, -1)]) / size
    return there.astype(jnp.bfloat16), back.astype(jnp.bfloat16)


def mixer_kernel(
    lengths_hbm, feat_hbm, dout_hbm, filt_hbm, taps_hbm, skip_hbm, there_hbm, back_hbm,
    out_ref, df_ref,
    lengths_ref, xf, xd, taps_v, skip_v, par, wh, wsig, winv, keep_f, keep_b,
    rim_src, rim, h_all, sig, q_s, k_s, v_s, yd, c_src, c_in, hal_src, hal, spec_s, spec_h, prod,
    ld, rim_ss, rim_rs, h_zs, h_ys, h_bs, h_rs, u_ss, uf_ss, s_rs, c_ss, c_rs, hal_ss, hal_rs,
):
    rank = lax.axis_index("seq")
    group = lax.axis_index("groups")
    channels, span = xd.shape
    count = channels // CH
    half = count // 2
    mir = rank // 2
    inn = lax.rem(rank + mir, 2)
    inner = inn == 1
    inward = rank + 1 - 2 * mir
    outward = rank - 1 + 2 * mir
    far = 3 - 3 * mir
    bf = jnp.bfloat16
    f32 = jnp.float32

    loads = [
        pltpu.make_async_copy(feat_hbm, xf, ld.at[0]),
        pltpu.make_async_copy(taps_hbm, taps_v, ld.at[1]),
        pltpu.make_async_copy(skip_hbm, skip_v, ld.at[2]),
        pltpu.make_async_copy(dout_hbm, xd, ld.at[3]),
        pltpu.make_async_copy(filt_hbm, h_all.at[rank], ld.at[4]),
        pltpu.make_async_copy(there_hbm.at[0], wh, ld.at[5]),
        pltpu.make_async_copy(there_hbm.at[mir], wsig, ld.at[6]),
        pltpu.make_async_copy(back_hbm.at[mir], winv, ld.at[7]),
        pltpu.make_async_copy(lengths_hbm, lengths_ref, ld.at[8]),
    ]
    for load in loads:
        load.start()

    barrier = pltpu.get_barrier_semaphore()
    pl.semaphore_signal(barrier, inc=1, device_id={"seq": inward}, device_id_type=MESH)
    pl.semaphore_signal(barrier, inc=1, device_id={"groups": 1 - group}, device_id_type=MESH)

    @pl.when(inner)
    def _():
        pl.semaphore_signal(barrier, inc=1, device_id={"seq": outward}, device_id_type=MESH)

    def rows_of(i):
        c = lax.rem(half * group + i, count)
        return c, pl.ds(pl.multiple_of(c * CH, CH), CH)

    def remote(src, dst, ss, rs, where):
        return pltpu.make_async_remote_copy(
            src_ref=src, dst_ref=dst, send_sem=ss, recv_sem=rs, device_id=where, device_id_type=MESH
        )

    def h_own_copy(i):
        c, rows = rows_of(i)
        return remote(filt_hbm.at[rows], h_all.at[rank, rows], h_zs.at[0, i], h_rs.at[rank, c], {"seq": inward})

    def h_on_copy(i):
        c, rows = rows_of(i)
        return remote(h_all.at[outward, rows], h_all.at[outward, rows], h_zs.at[1, i], h_rs.at[outward, c], {"seq": inward})

    def h_back_copy(i):
        c, rows = rows_of(i)
        return remote(h_all.at[0, rows], h_all.at[0, rows], h_bs.at[i], h_rs.at[0, c], {"seq": 3})

    def h_over_copy(which, slot, i):
        c, rows = rows_of(i)
        return remote(
            h_all.at[slot, rows], h_all.at[slot, rows], h_ys.at[which, i], h_rs.at[slot, c], {"groups": 1 - group}
        )

    def h_arrival(slot, i):
        c, rows = rows_of(i)
        return remote(h_all.at[slot, rows], h_all.at[slot, rows], h_zs.at[0, 0], h_rs.at[slot, c], {"seq": inward})

    def u_copy(i):
        c, rows = rows_of(i)
        return remote(sig.at[0, rows], sig.at[2 + inn, rows], u_ss.at[i], s_rs.at[inn, c], {"seq": inward})

    def u_on_copy(i):
        c, rows = rows_of(i)
        return remote(sig.at[2, rows], sig.at[4, rows], uf_ss.at[i], s_rs.at[2, c], {"seq": inward})

    def sig_arrival(which, i):
        c, rows = rows_of(i)
        return remote(sig.at[2 + which, rows], sig.at[2 + which, rows], u_ss.at[0], s_rs.at[which, c], {"seq": inward})

    def c_copy(i):
        c, rows = rows_of(i)
        return remote(c_src.at[rows], c_in.at[rows], c_ss.at[i], c_rs.at[c], {"seq": outward})

    def rim_copy():
        return remote(rim_src, rim, rim_ss, rim_rs, {"seq": rank + 1})

    def hal_copy(i):
        c, _ = rows_of(i)
        return remote(hal_src.at[c], hal.at[c], hal_ss.at[i], hal_rs.at[c], {"seq": rank - 1})

    @pl.when(rank == 0)
    def _():
        rim[...] = jnp.zeros_like(rim)

    @pl.when(rank == 3)
    def _():
        hal[...] = jnp.zeros_like(hal)

    pl.semaphore_wait(barrier, 2 + inn)

    h_own_copy(0).start()

    loads[0].wait()
    r_id = lax.broadcasted_iota(jnp.int32, (16, 128), 0)
    p_id = lax.broadcasted_iota(jnp.int32, (16, 128), 1)
    total = None
    for a in range(3):
        hit = ((r_id == 2 * a) & (p_id == 126)) | ((r_id == 2 * a + 1) & (p_id == 127))
        term = mm(jnp.where(hit, 1.0, 0.0).astype(bf), xf[a, :, span - 128 :], NT)
        total = term if total is None else total + term
    rim_src[...] = total.astype(bf)

    @pl.when(rank < 3)
    def _():
        rim_copy().start()

    for i in range(1, half):
        h_own_copy(i).start()

    loads[8].wait()

    def keeps(ahead, least):
        position = rank * span + ahead + lax.broadcasted_iota(jnp.int32, (8, span), 1)
        offset = position
        end = jnp.int32(0)
        for g in range(lengths_ref.shape[0]):
            one = lengths_ref[g]
            end = end + one
            offset = offset - jnp.where(end <= position, one, 0)
        return jnp.where(offset >= least, 1.0, 0.0)

    for j in (1, 2):
        keep_f[j - 1] = keeps(0, j)
        keep_b[j - 1] = keeps(j, j)

    loads[1].wait()
    loads[2].wait()
    flat = jnp.concatenate(
        [taps_v[0], taps_v[1], taps_v[2], skip_v[...], jnp.zeros((6, channels), f32)], axis=0
    )
    for c in range(count):
        par[c * CH : (c + 1) * CH, 0:16] = flat[:, c * CH : (c + 1) * CH].T
    for load in loads[3:8]:
        load.wait()

    @pl.when(rank > 0)
    def _():
        rim_copy().wait_recv()

    rr = lax.broadcasted_iota(jnp.int32, (16, 384), 0)
    cc = lax.broadcasted_iota(jnp.int32, (16, 384), 1)

    def spread(first):
        hit = None
        for a in range(3):
            one = ((rr == 2 * a) & (cc == 128 * a + first)) | ((rr == 2 * a + 1) & (cc == 128 * a + first + 1))
            hit = one if hit is None else hit | one
        return jnp.where(hit, 1.0, 0.0).astype(bf)

    def prepare(i):
        c, rows = rows_of(i)
        edge = mm(rim[:, rows], spread(126), TN)
        tap = par[rows, :]
        result = []
        for a in range(3):
            here = xf[a, rows, :].astype(f32)
            wide = jnp.concatenate([edge[:, 128 * a : 128 * a + 128], here], axis=1)
            acc = tap[:, 3 * a : 3 * a + 1] * here
            for j in (1, 2):
                moved = pltpu.roll(wide, j, 1)[:, 128:]
                acc = acc + tap[:, 3 * a + j : 3 * a + j + 1] * (moved * keep_f[j - 1, 0:1, :])
            result.append(acc.astype(bf))
        q, k, v = result
        q_s[rows, :] = q
        k_s[rows, :] = k
        v_s[rows, :] = v
        sig[mir, rows, :] = (k.astype(f32) * v.astype(f32)).astype(bf)
        sig[1 - mir, rows, :] = (xd[rows, :].astype(f32) * q.astype(f32)).astype(bf)
        u_copy(i).start()

    def pass_on(i):
        sig_arrival(0, i).wait_recv()
        u_on_copy(i).start()

        @pl.when(i < half)
        def _():
            h_arrival(outward, i).wait_recv()
            h_on_copy(i).start()
            h_over_copy(0, outward, i).start()

    def products(terms_of):
        def block(b, carry):
            first = pl.multiple_of(b * 16, 16)

            def pair(ref, k):
                at = pl.ds(k * CH + first, 16)
                return ref[at, 0:span], ref[at, span:]

            for k, terms in enumerate(terms_of(lambda n: pair(spec_h, n), lambda n: pair(spec_s, n))):
                re = im = None
                for (tc, ts), (xc, xs), sign in terms:
                    if sign > 0:
                        new_re, new_im = tc * xc - ts * xs, tc * xs + ts * xc
                    else:
                        new_re, new_im = tc * xc + ts * xs, tc * xs - ts * xc
                    re = new_re if re is None else re + new_re
                    im = new_im if im is None else im + new_im
                at = pl.ds(k * CH + first, 16)
                prod[at, 0:span] = re.astype(bf)
                prod[at, span:] = im.astype(bf)
            return carry

        lax.fori_loop(0, CH // 16, block, 0)

    def inner_terms(h, s):
        hs = [h(k) for k in range(4)]
        t = [hs[0]] + [(hs[k][0] + hs[k - 1][1], hs[k][1] - hs[k - 1][0]) for k in (1, 2, 3)]
        own, other, near, mid, end = [s(k) for k in range(5)]
        return [
            [(t[0], own, 1), (t[1], near, 1)],
            [(t[0], other, -1), (t[1], mid, -1), (t[2], end, -1)],
            [(t[1], other, -1), (t[2], mid, -1), (t[3], end, -1)],
        ]

    def outer_terms(h, s):
        return [[(h(0), s(0), 1)], [(h(0), s(1), -1)]]

    def main_inner(i):
        c, rows = rows_of(i)

        @pl.when(i < half)
        def _():
            h_arrival(inward, i).wait_recv()
            h_over_copy(1, inward, i).start()
            h_arrival(far, i).wait_recv()
            h_over_copy(2, far, i).start()

            @pl.when(rank == 2)
            def _():
                h_back_copy(i).start()

        @pl.when(i >= half)
        def _():
            h_arrival(outward, i).wait_recv()
            h_arrival(inward, i).wait_recv()
            h_arrival(far, i).wait_recv()

        sig_arrival(1, i).wait_recv()
        sig_arrival(2, i).wait_recv()
        spec_h[...] = mm(h_all[:, rows, :].reshape(4 * CH, span), wh[...])
        spec_s[...] = mm(sig[:, rows, :].reshape(5 * CH, span), wsig[...])
        products(inner_terms)
        value = mm(prod[...], winv[...])
        skip = par[rows, 9:10]
        yd[0, rows, :] = (value[0:CH] + skip * sig[0, rows, :].astype(f32)).astype(bf)
        yd[1, rows, :] = (value[CH : 2 * CH] + skip * sig[1, rows, :].astype(f32)).astype(bf)
        c_src[rows, :] = value[2 * CH :].astype(bf)
        c_copy(i).start()

    def main_outer(i):
        c, rows = rows_of(i)

        @pl.when(rank == 3)
        def _():
            h_arrival(0, i).wait_recv()

            @pl.when(i < half)
            def _():
                h_over_copy(0, 0, i).start()

        spec_h[0:CH] = mm(h_all[0, rows, :], wh[...])
        spec_s[0 : 2 * CH] = mm(sig[0:2, rows, :].reshape(2 * CH, span), wsig[...])
        products(outer_terms)
        value = mm(prod[0 : 2 * CH], winv[...])
        skip = par[rows, 9:10]
        yd[0, rows, :] = (value[0:CH] + skip * sig[0, rows, :].astype(f32)).astype(bf)
        base = value[CH:] + skip * sig[1, rows, :].astype(f32)
        c_copy(i).wait_recv()
        yd[1, rows, :] = (base + c_in[rows, :].astype(f32)).astype(bf)

    def grads_of(rows, lanes):
        y = yd[mir, rows, lanes].astype(f32)
        dm = yd[1 - mir, rows, lanes].astype(f32)
        return [
            xd[rows, lanes].astype(f32) * y,
            dm * v_s[rows, lanes].astype(f32),
            dm * k_s[rows, lanes].astype(f32),
        ]

    def halo(i):
        c, rows = rows_of(i)
        edge = None
        for a, grad in enumerate(grads_of(rows, slice(0, 128))):
            hit = ((r_id == 2 * a) & (p_id == 0)) | ((r_id == 2 * a + 1) & (p_id == 1))
            term = mm(jnp.where(hit, 1.0, 0.0).astype(bf), grad.astype(bf), NT)
            edge = term if edge is None else edge + term
        hal_src[c] = edge.astype(bf)
        hal_copy(i).start()

    def finish(i):
        c, rows = rows_of(i)

        @pl.when(rank < 3)
        def _():
            hal_copy(i).wait_recv()

        tap = par[rows, :]
        edge = mm(hal[c], spread(0), TN)
        y = yd[mir, rows, :].astype(f32)
        out_ref[rows, :] = (q_s[rows, :].astype(f32) * y).astype(bf)
        for a, grad in enumerate(grads_of(rows, slice(None))):
            wide = jnp.concatenate([grad, edge[:, 128 * a : 128 * a + 128]], axis=1)
            acc = tap[:, 3 * a : 3 * a + 1] * grad
            for j in (1, 2):
                moved = pltpu.roll(wide, span + 128 - j, 1)[:, :span]
                acc = acc + tap[:, 3 * a + j : 3 * a + j + 1] * (moved * keep_b[j - 1, 0:1, :])
            df_ref[a, rows, :] = acc.astype(bf)

    def step(s, carry):
        @pl.when(s < count)
        def _():
            prepare(s)

        @pl.when(inner & (s >= 1) & (s < count + 1))
        def _():
            pass_on(s - 1)

        main = (s >= LAG) & (s < count + LAG)

        @pl.when(inner & main)
        def _():
            main_inner(s - LAG)

        @pl.when((inn == 0) & main)
        def _():
            main_outer(s - LAG)

        @pl.when((rank > 0) & main)
        def _():
            halo(s - LAG)

        @pl.when(s >= LAG + BACK)
        def _():
            finish(s - LAG - BACK)

        return carry

    lax.fori_loop(0, count + LAG + BACK, step, 0)

    @pl.when(rank < 3)
    def _():
        rim_copy().wait_send()

    def drain(i, carry):
        u_copy(i).wait_send()

        @pl.when(rank > 0)
        def _():
            hal_copy(i).wait_send()

        @pl.when(inner)
        def _():
            u_on_copy(i).wait_send()
            c_copy(i).wait_send()

        @pl.when(i < half)
        def _():
            h_own_copy(i).wait_send()

            @pl.when(inner)
            def _():
                h_on_copy(i).wait_send()
                h_over_copy(0, outward, i).wait_send()
                h_over_copy(1, inward, i).wait_send()
                h_over_copy(2, far, i).wait_send()

            @pl.when(rank == 2)
            def _():
                h_back_copy(i).wait_send()

            @pl.when(rank == 3)
            def _():
                h_over_copy(0, 0, i).wait_send()

        return carry

    lax.fori_loop(0, count, drain, 0)


def local_kernel(features, dout, filters, taps, skip, lengths):
    channels, span = dout.shape
    count = channels // CH
    bf = jnp.bfloat16
    f32 = jnp.float32
    there, back = block_tables(span)
    operands = [lengths, features, dout, filters, taps, skip[None], jnp.asarray(there), jnp.asarray(back)]
    vmem = pl.BlockSpec(memory_space=pltpu.VMEM)
    hbm = pl.BlockSpec(memory_space=pltpu.HBM)
    dma = pltpu.SemaphoreType.DMA
    return pl.pallas_call(
        mixer_kernel,
        out_shape=(pltpu.VMEM(dout.shape, bf), pltpu.VMEM(features.shape, bf)),
        in_specs=[hbm] * 8,
        out_specs=(vmem, vmem),
        scratch_shapes=[
            pltpu.SMEM(lengths.shape, jnp.int32),
            pltpu.VMEM((3, channels, span), bf),
            pltpu.VMEM((channels, span), bf),
            pltpu.VMEM((3, 3, channels), f32),
            pltpu.VMEM((1, channels), f32),
            pltpu.VMEM((channels, 128), f32),
            pltpu.VMEM((span, 2 * span), bf),
            pltpu.VMEM((span, 2 * span), bf),
            pltpu.VMEM((2 * span, span), bf),
            pltpu.VMEM((2, 8, span), f32),
            pltpu.VMEM((2, 8, span), f32),
            pltpu.VMEM((16, channels), bf),
            pltpu.VMEM((16, channels), bf),
            pltpu.VMEM((4, channels, span), bf),
            pltpu.VMEM((5, channels, span), bf),
            pltpu.VMEM((channels, span), bf),
            pltpu.VMEM((channels, span), bf),
            pltpu.VMEM((channels, span), bf),
            pltpu.VMEM((2, channels, span), bf),
            pltpu.VMEM((channels, span), bf),
            pltpu.VMEM((channels, span), bf),
            pltpu.VMEM((count, 16, CH), bf),
            pltpu.VMEM((count, 16, CH), bf),
            pltpu.VMEM((5 * CH, 2 * span), f32),
            pltpu.VMEM((4 * CH, 2 * span), f32),
            pltpu.VMEM((3 * CH, 2 * span), bf),
            dma((9,)), dma, dma,
            dma((2, count)), dma((3, count)), dma((count,)), dma((4, count)),
            dma((count,)), dma((count,)), dma((3, count)),
            dma((count,)), dma((count,)), dma((count,)), dma((count,)),
        ],
        compiler_params=pltpu.CompilerParams(
            collective_id=0, has_side_effects=True, vmem_limit_bytes=32 * 1024 * 1024
        ),
    )(*[pltpu.with_memory_space_constraint(x, pltpu.HBM) for x in operands])


def local(features, dout, filters, taps, skip, lengths):
    channels, span = dout.shape
    fits = lax.axis_size("seq") == 4 and lax.axis_size("groups") == 2 and taps.shape[:2] == (3, 3)
    if fits and span == 256 and channels % (2 * CH) == 0:
        return local_kernel(features, dout, filters, taps, skip, lengths)
    return local_general(features, dout, filters, taps, skip, lengths)


def solution(mesh):
    in_specs = (
        P(None, ("chan", "sub"), ("groups", "seq")),
        P(("chan", "sub"), ("groups", "seq")),
        P(("chan", "sub"), "seq"),
        P(None, None, ("chan", "sub")),
        P(("chan", "sub")),
        P("groups"),
    )
    out_specs = (P(("chan", "sub"), ("groups", "seq")), P(None, ("chan", "sub"), ("groups", "seq")))
    return jax.shard_map(local, mesh=mesh, in_specs=in_specs, out_specs=out_specs, check_vma=False)
```

```python
import functools

import jax
import numpy as np
import jax.numpy as jnp
from jax import lax
from jax.experimental import pallas as pl
from jax.experimental.pallas import tpu as pltpu
from jax.sharding import PartitionSpec as P

HIGHEST = lax.Precision.HIGHEST
TWO_PI = 6.283185307179586


def shifted(value, axis, steps):
    count = lax.axis_size(axis)
    leading, last = (max(0, -steps), min(count, count - steps))
    return lax.ppermute(value, axis, [(source, source + steps) for source in range(leading, last)])


def genome_offsets(lengths, positions):
    order = jnp.arange(lengths.shape[0], dtype=jnp.int32)
    so_far = (order[None, :] <= order[:, None]).astype(jnp.int32)
    ends_at = jnp.sum(so_far * lengths[None, :], axis=1, dtype=jnp.int32)
    before = (ends_at[None, :] <= positions[:, None]).astype(jnp.int32)
    return positions - jnp.sum(before * lengths[None, :], axis=1, dtype=jnp.int32)


def short_forward(extended, taps_local, offsets):
    span_rows = offsets.shape[0]
    count = taps_local.shape[1]
    result = jnp.zeros(extended.shape[:2] + (span_rows,), jnp.float32)
    for tap_index in range(count):
        begin = count - 1 - tap_index
        window = extended[:, :, begin : begin + span_rows].astype(jnp.float32)
        keep_mask = (offsets >= tap_index).astype(jnp.float32)
        result = result + taps_local[:, tap_index, :, None] * window * keep_mask[None, None, :]
    return result


def short_backward(grads_ext, taps_local, offsets_ext):
    count = taps_local.shape[1]
    span_rows = offsets_ext.shape[0] - (count - 1)
    result = jnp.zeros(grads_ext.shape[:2] + (span_rows,), jnp.float32)
    for tap_index in range(count):
        window = grads_ext[:, :, tap_index : tap_index + span_rows]
        keep_mask = (offsets_ext[tap_index : tap_index + span_rows] >= tap_index).astype(
            jnp.float32
        )
        result = result + taps_local[:, tap_index, :, None] * window * keep_mask[None, None, :]
    return result


def dft_table(rows_n, cols_n, period):
    row_ids = jnp.arange(rows_n, dtype=jnp.int32)
    col_ids = jnp.arange(cols_n, dtype=jnp.int32)
    phase = row_ids[:, None] * col_ids[None, :] % period
    angles = phase.astype(jnp.float32) * (-TWO_PI / period)
    return (jnp.cos(angles), jnp.sin(angles))


def forward_transform(signal, tables):
    (row_re, row_im), (twid_re, twid_im), (col_re, col_im) = tables
    half_rows = signal.shape[1] // 128
    blocks_in = signal.reshape(signal.shape[0], half_rows, 128)
    part_re = jnp.einsum("kn,cnm->ckm", row_re[:, :half_rows], blocks_in, precision=HIGHEST)
    part_im = jnp.einsum("kn,cnm->ckm", row_im[:, :half_rows], blocks_in, precision=HIGHEST)
    turned_re = part_re * twid_re - part_im * twid_im
    turned_im = part_re * twid_im + part_im * twid_re
    spec_re = jnp.einsum("ckn,nm->ckm", turned_re, col_re, precision=HIGHEST) - jnp.einsum(
        "ckn,nm->ckm", turned_im, col_im, precision=HIGHEST
    )
    spec_im = jnp.einsum("ckn,nm->ckm", turned_re, col_im, precision=HIGHEST) + jnp.einsum(
        "ckn,nm->ckm", turned_im, col_re, precision=HIGHEST
    )
    return (spec_re, spec_im)


def inverse_transform(spec_re, spec_im, tables):
    (row_re, row_im), (twid_re, twid_im), (col_re, col_im) = tables
    rows_n = spec_re.shape[1]
    half_rows = rows_n // 2
    mid_re = jnp.einsum("ckn,nm->ckm", spec_re, col_re, precision=HIGHEST) + jnp.einsum(
        "ckn,nm->ckm", spec_im, col_im, precision=HIGHEST
    )
    mid_im = jnp.einsum("ckn,nm->ckm", spec_im, col_re, precision=HIGHEST) - jnp.einsum(
        "ckn,nm->ckm", spec_re, col_im, precision=HIGHEST
    )
    back_re = mid_re * twid_re + mid_im * twid_im
    back_im = mid_im * twid_re - mid_re * twid_im
    signal = jnp.einsum("nk,ckm->cnm", row_re[:half_rows], back_re, precision=HIGHEST) + jnp.einsum(
        "nk,ckm->cnm", row_im[:half_rows], back_im, precision=HIGHEST
    )
    return signal.reshape(signal.shape[0], half_rows * 128) * (1.0 / (rows_n * 128))


def long_filter(filt, mixed_in, grad_in, skip_part):
    rows_n = 2 * mixed_in.shape[1] // 128
    tables = (
        dft_table(rows_n, rows_n, rows_n),
        dft_table(rows_n, 128, rows_n * 128),
        dft_table(128, 128, 128),
    )
    mixed_f = mixed_in.astype(jnp.float32)
    grad_f = grad_in.astype(jnp.float32)
    filt_re, filt_im = forward_transform(filt.astype(jnp.float32), tables)
    mix_re, mix_im = forward_transform(mixed_f, tables)
    grad_re, grad_im = forward_transform(grad_f, tables)
    conv_out = inverse_transform(
        filt_re * mix_re - filt_im * mix_im, filt_re * mix_im + filt_im * mix_re, tables
    )
    corr_out = inverse_transform(
        filt_re * grad_re + filt_im * grad_im, filt_re * grad_im - filt_im * grad_re, tables
    )
    y_out = (conv_out + skip_part[:, None] * mixed_f).astype(jnp.bfloat16)
    dmixed = (corr_out + skip_part[:, None] * grad_f).astype(jnp.bfloat16)
    return (y_out, dmixed)


DENSE_MAX = 1024
FINE = 32


def angle_parts(length):
    base = np.arange(length, dtype=np.int64) * 4 + 1
    fine = np.arange(FINE, dtype=np.int64)[:, None] * base[None, :] % (4 * length)
    coarse = np.arange(0, length, FINE, dtype=np.int64)[:, None] * base[None, :] % (4 * length)
    scale = 2.0 * np.pi / (4 * length)
    return [
        func(part * scale).astype(np.float32)
        for part in (coarse, fine)
        for func in (np.cos, np.sin)
    ]


def dense_filter(filt, mixed_in, grad_in, skip_part):
    length = mixed_in.shape[1]
    cc, cs, fc, fs = [jnp.asarray(p)[:, None] if i < 2 else jnp.asarray(p)[None] for i, p in enumerate(angle_parts(length))]
    cos_t = (cc * fc - cs * fs).reshape(length, length)
    sin_t = (cs * fc + cc * fs).reshape(length, length)
    table = jnp.concatenate([cos_t, sin_t], axis=1).astype(jnp.bfloat16)

    def fwd(x):
        return jnp.dot(x, table, preferred_element_type=jnp.float32)

    def inv(x):
        return lax.dot_general(x.astype(jnp.bfloat16), table, (((1,), (1,)), ((), ())), preferred_element_type=jnp.float32) * (1.0 / length)

    h, m, g = fwd(filt), fwd(mixed_in), fwd(grad_in)
    hc, hs = h[:, :length], h[:, length:]
    mc, ms = m[:, :length], m[:, length:]
    gc, gs = g[:, :length], g[:, length:]
    conv_out = inv(jnp.concatenate([hc * mc - hs * ms, hc * ms + hs * mc], axis=1))
    corr_out = inv(jnp.concatenate([hc * gc + hs * gs, hc * gs - hs * gc], axis=1))
    y_out = (conv_out + skip_part[:, None] * mixed_in.astype(jnp.float32)).astype(jnp.bfloat16)
    dmixed = (corr_out + skip_part[:, None] * grad_in.astype(jnp.float32)).astype(jnp.bfloat16)
    return (y_out, dmixed)


def to_channels(stacked):
    return lax.all_to_all(stacked, "seq", split_axis=1, concat_axis=2, tiled=True)


def to_sequence(stacked):
    return lax.all_to_all(stacked, "seq", split_axis=2, concat_axis=1, tiled=True)


def local_general(features, dout, filters, taps, skip, lengths):
    blocks = lax.axis_size("seq")
    seq_rank = lax.axis_index("seq")
    span_rows = features.shape[2]
    channels_here = features.shape[1]
    chan_part = channels_here // blocks
    count = taps.shape[1]
    margin = count - 1
    rim = shifted(features[:, :, span_rows - margin :], "seq", 1)
    extended = jnp.concatenate([rim, features], axis=2)
    first_pos = seq_rank * span_rows
    offsets = genome_offsets(lengths, first_pos + jnp.arange(span_rows, dtype=jnp.int32))
    filtered = short_forward(extended, taps, offsets).astype(jnp.bfloat16)
    query_side = filtered[0].astype(jnp.float32)
    key_side = filtered[1].astype(jnp.float32)
    value_side = filtered[2].astype(jnp.float32)
    dout_f = dout.astype(jnp.float32)
    mixed = (key_side * value_side).astype(jnp.bfloat16)
    grad_in = (dout_f * query_side).astype(jnp.bfloat16)
    moved = to_channels(jnp.stack([mixed, grad_in, filters]))
    skip_part = lax.dynamic_slice_in_dim(skip, seq_rank * chan_part, chan_part, 0)
    run = dense_filter if moved.shape[2] <= DENSE_MAX else long_filter
    y_out, dmixed = run(moved[2], moved[0], moved[1], skip_part)
    returned = to_sequence(jnp.stack([y_out, dmixed]))
    y_here = returned[0].astype(jnp.float32)
    dmixed_here = returned[1].astype(jnp.float32)
    out = (query_side * y_here).astype(jnp.bfloat16)
    grads = jnp.stack([dout_f * y_here, dmixed_here * value_side, dmixed_here * key_side])
    ahead = shifted(grads[:, :, :margin], "seq", -1)
    grads_ext = jnp.concatenate([grads, ahead], axis=2)
    offsets_ext = genome_offsets(
        lengths, first_pos + jnp.arange(span_rows + margin, dtype=jnp.int32)
    )
    dfeatures = short_backward(grads_ext, taps, offsets_ext).astype(jnp.bfloat16)
    return (out, dfeatures)


CH = 128
BACK = 3
NN = (((1,), (0,)), ((), ()))
NT = (((1,), (1,)), ((), ()))
TN = (((0,), (0,)), ((), ()))
MESH = pl.DeviceIdType.MESH


def mm(a, b, dims=NN):
    return lax.dot_general(a, b, dims, preferred_element_type=jnp.float32)


def block_tables(size):
    place = np.arange(size, dtype=np.int64)
    phase = place[:, None] * (4 * place[None, :] + 1) % (4 * size)
    angle = phase * (2.0 * np.pi / (4 * size))
    cos, sin = np.cos(angle), np.sin(angle)
    there = np.stack([np.concatenate([cos, s * sin], axis=1) for s in (1, -1)])
    back = np.stack([np.concatenate([cos.T, s * sin.T], axis=0) for s in (1, -1)]) / size
    return there.astype(jnp.bfloat16), back.astype(jnp.bfloat16)


def mixer_kernel(
    lengths_hbm, feat_hbm, dout_hbm, filt_hbm, taps_hbm, skip_hbm, there_hbm, back_hbm,
    out_ref, df_ref,
    lengths_ref, xf, xd, taps_v, skip_v, par, wh, wsig, winv, keep_f, keep_b,
    rim_src, rim, h_all, sig, q_s, k_s, v_s, yd, w_loc, c_src, c_in,
    hal_src, hal, mini_src, mini, mini_own, spec_s, spec_h, prod,
    ld, rim_ss, rim_rs, h_zs, h_ys, h_bs, h_rs, u_ss, u_rs, c_ss, c_rs, hal_ss, hal_rs, mini_ss, mini_rs,
):
    rank = lax.axis_index("seq")
    group = lax.axis_index("groups")
    channels, span = xd.shape
    count = channels // CH
    half = count // 2
    mir = rank // 2
    inn = lax.rem(rank + mir, 2)
    inner = inn == 1
    inward = rank + 1 - 2 * mir
    outward = rank - 1 + 2 * mir
    far = 3 - 3 * mir
    bf = jnp.bfloat16
    f32 = jnp.float32

    loads = [
        pltpu.make_async_copy(feat_hbm, xf, ld.at[0]),
        pltpu.make_async_copy(taps_hbm, taps_v, ld.at[1]),
        pltpu.make_async_copy(skip_hbm, skip_v, ld.at[2]),
        pltpu.make_async_copy(dout_hbm, xd, ld.at[3]),
        pltpu.make_async_copy(filt_hbm, h_all.at[rank], ld.at[4]),
        pltpu.make_async_copy(there_hbm.at[0], wh, ld.at[5]),
        pltpu.make_async_copy(there_hbm.at[mir], wsig, ld.at[6]),
        pltpu.make_async_copy(back_hbm.at[mir], winv, ld.at[7]),
        pltpu.make_async_copy(lengths_hbm, lengths_ref, ld.at[8]),
    ]
    for load in loads:
        load.start()

    def greet(**where):
        pl.semaphore_signal(barrier, inc=1, device_id=where, device_id_type=MESH)

    barrier = pltpu.get_barrier_semaphore()
    greet(seq=inward)

    @pl.when(inner)
    def _():
        greet(seq=outward)

    @pl.when(inn == 0)
    def _():
        greet(seq=2 - mir)

    @pl.when(rank > 0)
    def _():
        greet(groups=1 - group)

    def rows_of(i):
        c = lax.rem(half * group + i, count)
        return c, pl.ds(pl.multiple_of(c * CH, CH), CH)

    def remote(src, dst, ss, rs, where):
        return pltpu.make_async_remote_copy(
            src_ref=src, dst_ref=dst, send_sem=ss, recv_sem=rs, device_id=where, device_id_type=MESH
        )

    def h_own_copy(i):
        c, rows = rows_of(i)
        return remote(filt_hbm.at[rows], h_all.at[rank, rows], h_zs.at[0, i], h_rs.at[rank, c], {"seq": inward})

    def h_on_copy(i):
        c, rows = rows_of(i)
        return remote(h_all.at[outward, rows], h_all.at[outward, rows], h_zs.at[1, i], h_rs.at[outward, c], {"seq": inward})

    def h_back_copy(i):
        c, rows = rows_of(i)
        return remote(h_all.at[0, rows], h_all.at[0, rows], h_bs.at[i], h_rs.at[0, c], {"seq": 3})

    def h_over_copy(which, slot, i):
        c, rows = rows_of(i)
        return remote(
            h_all.at[slot, rows], h_all.at[slot, rows], h_ys.at[which, i], h_rs.at[slot, c], {"groups": 1 - group}
        )

    def h_arrival(slot, i):
        c, rows = rows_of(i)
        return remote(h_all.at[slot, rows], h_all.at[slot, rows], h_zs.at[0, 0], h_rs.at[slot, c], {"seq": inward})

    def u_copy(i):
        c, rows = rows_of(i)
        return remote(sig.at[0, rows], sig.at[2, rows], u_ss.at[i], u_rs.at[c], {"seq": inward})

    def c_copy(which, i):
        c, rows = rows_of(i)
        where = (inward, far, outward)[which]
        slot = which // 2
        return remote(
            c_src.at[which, rows], c_in.at[slot, rows], c_ss.at[which, i], c_rs.at[slot, c], {"seq": where}
        )

    def c_arrival(slot, i):
        c, rows = rows_of(i)
        return remote(c_in.at[slot, rows], c_in.at[slot, rows], c_ss.at[0, i], c_rs.at[slot, c], {"seq": inward})

    def mini_copy(i):
        c, _ = rows_of(i)
        return remote(mini_src.at[c], mini.at[c], mini_ss.at[i], mini_rs.at[c], {"seq": 2 - 2 * mir})

    def rim_copy():
        return remote(rim_src, rim, rim_ss, rim_rs, {"seq": rank + 1})

    def hal_copy(i):
        c, _ = rows_of(i)
        return remote(hal_src.at[c], hal.at[c], hal_ss.at[i], hal_rs.at[c], {"seq": rank - 1})

    @pl.when(rank == 0)
    def _():
        rim[...] = jnp.zeros_like(rim)

    @pl.when(rank == 3)
    def _():
        hal[...] = jnp.zeros_like(hal)

    @pl.when(lax.rem(rank, 2) == 1)
    def _():
        mini[...] = jnp.zeros_like(mini)

    @pl.when(inn == 0)
    def _():
        mini_own[...] = jnp.zeros_like(mini_own)

    pl.semaphore_wait(barrier, 1 + 3 * inn + rank // 3)

    h_own_copy(0).start()

    loads[0].wait()
    r_id = lax.broadcasted_iota(jnp.int32, (16, 128), 0)
    p_id = lax.broadcasted_iota(jnp.int32, (16, 128), 1)
    total = None
    for a in range(3):
        hit = ((r_id == 2 * a) & (p_id == 126)) | ((r_id == 2 * a + 1) & (p_id == 127))
        term = mm(jnp.where(hit, 1.0, 0.0).astype(bf), xf[a, :, span - 128 :], NT)
        total = term if total is None else total + term
    rim_src[...] = total.astype(bf)

    @pl.when(rank < 3)
    def _():
        rim_copy().start()

    for i in range(1, half):
        h_own_copy(i).start()

    loads[8].wait()

    def keeps(ahead, least):
        position = rank * span + ahead + lax.broadcasted_iota(jnp.int32, (8, span), 1)
        offset = position
        end = jnp.int32(0)
        for g in range(lengths_ref.shape[0]):
            one = lengths_ref[g]
            end = end + one
            offset = offset - jnp.where(end <= position, one, 0)
        return jnp.where(offset >= least, 1.0, 0.0)

    for j in (1, 2):
        keep_f[j - 1] = keeps(0, j)
        keep_b[j - 1] = keeps(j, j)

    loads[1].wait()
    loads[2].wait()
    flat = jnp.concatenate(
        [taps_v[0], taps_v[1], taps_v[2], skip_v[...], jnp.zeros((6, channels), f32)], axis=0
    )
    for c in range(count):
        par[c * CH : (c + 1) * CH, 0:16] = flat[:, c * CH : (c + 1) * CH].T
    for load in loads[3:8]:
        load.wait()

    @pl.when(rank > 0)
    def _():
        rim_copy().wait_recv()

    rr = lax.broadcasted_iota(jnp.int32, (16, 384), 0)
    cc = lax.broadcasted_iota(jnp.int32, (16, 384), 1)

    def spread(first):
        hit = None
        for a in range(3):
            one = ((rr == 2 * a) & (cc == 128 * a + first)) | ((rr == 2 * a + 1) & (cc == 128 * a + first + 1))
            hit = one if hit is None else hit | one
        return jnp.where(hit, 1.0, 0.0).astype(bf)

    def prepare(i):
        c, rows = rows_of(i)
        edge = mm(rim[:, rows], spread(126), TN)
        tap = par[rows, :]
        result = []
        for a in range(3):
            here = xf[a, rows, :].astype(f32)
            wide = jnp.concatenate([edge[:, 128 * a : 128 * a + 128], here], axis=1)
            acc = tap[:, 3 * a : 3 * a + 1] * here
            for j in (1, 2):
                moved = pltpu.roll(wide, j, 1)[:, 128:]
                acc = acc + tap[:, 3 * a + j : 3 * a + j + 1] * (moved * keep_f[j - 1, 0:1, :])
            result.append(acc.astype(bf))
        q, k, v = result
        q_s[rows, :] = q
        k_s[rows, :] = k
        v_s[rows, :] = v
        sig[mir, rows, :] = (k.astype(f32) * v.astype(f32)).astype(bf)
        sig[1 - mir, rows, :] = (xd[rows, :].astype(f32) * q.astype(f32)).astype(bf)

        @pl.when(inn == 0)
        def _():
            u_copy(i).start()

        @pl.when(inner & (i < half))
        def _():
            h_arrival(outward, i).wait_recv()
            h_on_copy(i).start()
            h_over_copy(0, outward, i).start()

    def pick(block, rows_at):
        hit = None
        for first, lane in rows_at:
            one = ((r_id == first) & (p_id == lane)) | ((r_id == first + 1) & (p_id == lane + 1))
            hit = one if hit is None else hit | one
        return mm(jnp.where(hit, 1.0, 0.0).astype(bf), block, NT)

    def keep_local(rows, value):
        skip = par[rows, 9:10]
        yd[0, rows, :] = (value[0:CH] + skip * sig[0, rows, :].astype(f32)).astype(bf)
        other = value[CH : 2 * CH] + skip * sig[1, rows, :].astype(f32)
        w_loc[rows, :] = other
        yd[1, rows, :] = other.astype(bf)

    def products(terms_of):
        def block(b, carry):
            first = pl.multiple_of(b * 16, 16)

            def pair(ref, k):
                at = pl.ds(k * CH + first, 16)
                return ref[at, 0:span], ref[at, span:]

            for k, terms in enumerate(terms_of(lambda n: pair(spec_h, n), lambda n: pair(spec_s, n))):
                re = im = None
                for (tc, ts), (xc, xs), sign in terms:
                    if sign > 0:
                        new_re, new_im = tc * xc - ts * xs, tc * xs + ts * xc
                    else:
                        new_re, new_im = tc * xc + ts * xs, tc * xs - ts * xc
                    re = new_re if re is None else re + new_re
                    im = new_im if im is None else im + new_im
                at = pl.ds(k * CH + first, 16)
                prod[at, 0:span] = re.astype(bf)
                prod[at, span:] = im.astype(bf)
            return carry

        lax.fori_loop(0, CH // 16, block, 0)

    def inner_terms(h, s):
        hs = [h(k) for k in range(4)]
        t = [hs[0]] + [(hs[k][0] + hs[k - 1][1], hs[k][1] - hs[k - 1][0]) for k in (1, 2, 3)]
        own, other, near = [s(k) for k in range(3)]
        return [
            [(t[0], own, 1), (t[1], near, 1)],
            [(t[0], other, -1)],
            [(t[1], own, 1), (t[2], near, 1)],
            [(t[2], own, 1), (t[3], near, 1)],
            [(t[1], other, -1)],
        ]

    def outer_terms(h, s):
        return [[(h(0), s(0), 1)], [(h(0), s(1), -1)]]

    def main_inner(i):
        c, rows = rows_of(i)

        @pl.when(i < half)
        def _():
            h_arrival(inward, i).wait_recv()
            h_over_copy(1, inward, i).start()
            h_arrival(far, i).wait_recv()
            h_over_copy(2, far, i).start()

            @pl.when(rank == 2)
            def _():
                h_back_copy(i).start()

        @pl.when(i >= half)
        def _():
            h_arrival(outward, i).wait_recv()
            h_arrival(inward, i).wait_recv()
            h_arrival(far, i).wait_recv()

        u_copy(i).wait_recv()
        spec_h[...] = mm(h_all[:, rows, :].reshape(4 * CH, span), wh[...])
        spec_s[...] = mm(sig[:, rows, :].reshape(3 * CH, span), wsig[...])
        products(inner_terms)
        value = mm(prod[...], winv[...])
        for which in range(3):
            c_src[which, rows, :] = value[(2 + which) * CH : (3 + which) * CH].astype(bf)
        mini_src[c] = pick(c_src[1 - mir, rows, 0:128], [(2 * mir, 0), (4 * mir, 0)]).astype(bf)
        mini_own[c] = pick(c_src[2 * mir, rows, 0:128], [(0, 0)]).astype(bf)
        mini_copy(i).start()
        c_copy(1, i).start()
        c_copy(0, i).start()
        c_copy(2, i).start()
        keep_local(rows, value)

    def main_outer(i):
        c, rows = rows_of(i)

        @pl.when(rank == 3)
        def _():
            h_arrival(0, i).wait_recv()

            @pl.when(i < half)
            def _():
                h_over_copy(0, 0, i).start()

        spec_h[0:CH] = mm(h_all[0, rows, :], wh[...])
        spec_s[0 : 2 * CH] = mm(sig[0:2, rows, :].reshape(2 * CH, span), wsig[...])
        products(outer_terms)
        keep_local(rows, mm(prod[0 : 2 * CH], winv[...]))

    def grads_of(rows, lanes):
        y = yd[mir, rows, lanes].astype(f32)
        dm = yd[1 - mir, rows, lanes].astype(f32)
        return [
            xd[rows, lanes].astype(f32) * y,
            dm * v_s[rows, lanes].astype(f32),
            dm * k_s[rows, lanes].astype(f32),
        ]

    def halo(i):
        c, rows = rows_of(i)
        first = slice(0, 128)
        d_edge = pick(xd[rows, first], [(0, 0)])
        m_edge = pick(yd[1 - mir, rows, first], [(2, 0), (4, 0)])
        y_edge = pick(yd[mir, rows, first], [(0, 0)])
        v_edge = pick(v_s[rows, first], [(2, 0)])
        k_edge = pick(k_s[rows, first], [(4, 0)])
        hal_src[c, 0] = (d_edge + m_edge).astype(bf)
        hal_src[c, 1] = (y_edge + v_edge + k_edge).astype(bf)
        hal_copy(i).start()

    def finish(i):
        c, rows = rows_of(i)
        c_arrival(0, i).wait_recv()

        @pl.when(inner)
        def _():
            yd[1, rows, :] = (w_loc[rows, :] + c_in[0, rows, :].astype(f32)).astype(bf)

        @pl.when(inn == 0)
        def _():
            c_arrival(1, i).wait_recv()
            cross = c_in[0, rows, :].astype(f32) + c_in[1, rows, :].astype(f32)
            yd[1, rows, :] = (w_loc[rows, :] + cross).astype(bf)

        @pl.when(rank < 3)
        def _():
            hal_copy(i).wait_recv()

        @pl.when(lax.rem(rank, 2) == 0)
        def _():
            mini_copy(i).wait_recv()

        late = mini[c].astype(f32) + mini_own[c].astype(f32)
        left = hal[c, 0].astype(f32) + jnp.where(r_id >= 2, late, 0.0)
        right = hal[c, 1].astype(f32) + jnp.where(r_id < 2, late, 0.0)
        tap = par[rows, :]
        edge = mm((left * right).astype(bf), spread(0), TN)
        y = yd[mir, rows, :].astype(f32)
        out_ref[rows, :] = (q_s[rows, :].astype(f32) * y).astype(bf)
        for a, grad in enumerate(grads_of(rows, slice(None))):
            wide = jnp.concatenate([grad, edge[:, 128 * a : 128 * a + 128]], axis=1)
            acc = tap[:, 3 * a : 3 * a + 1] * grad
            for j in (1, 2):
                moved = pltpu.roll(wide, span + 128 - j, 1)[:, :span]
                acc = acc + tap[:, 3 * a + j : 3 * a + j + 1] * (moved * keep_b[j - 1, 0:1, :])
            df_ref[a, rows, :] = acc.astype(bf)

    def first_steps(s, carry):
        prepare(s)
        return carry

    lax.fori_loop(0, count, first_steps, 0)

    def step(s, carry):
        main = s < count

        @pl.when(inner & main)
        def _():
            main_inner(s)

        @pl.when((inn == 0) & main)
        def _():
            main_outer(s)

        @pl.when((rank > 0) & main)
        def _():
            halo(s)

        @pl.when(s >= BACK)
        def _():
            finish(s - BACK)

        return carry

    lax.fori_loop(0, count + BACK, step, 0)

    @pl.when(rank < 3)
    def _():
        rim_copy().wait_send()

    def drain(i, carry):
        @pl.when(inn == 0)
        def _():
            u_copy(i).wait_send()

        @pl.when(rank > 0)
        def _():
            hal_copy(i).wait_send()

        @pl.when(inner)
        def _():
            mini_copy(i).wait_send()
            for which in range(3):
                c_copy(which, i).wait_send()

        @pl.when(i < half)
        def _():
            h_own_copy(i).wait_send()

            @pl.when(inner)
            def _():
                h_on_copy(i).wait_send()
                h_over_copy(0, outward, i).wait_send()
                h_over_copy(1, inward, i).wait_send()
                h_over_copy(2, far, i).wait_send()

            @pl.when(rank == 2)
            def _():
                h_back_copy(i).wait_send()

            @pl.when(rank == 3)
            def _():
                h_over_copy(0, 0, i).wait_send()

        return carry

    lax.fori_loop(0, count, drain, 0)


def local_kernel(features, dout, filters, taps, skip, lengths):
    channels, span = dout.shape
    count = channels // CH
    bf = jnp.bfloat16
    f32 = jnp.float32
    there, back = block_tables(span)
    operands = [lengths, features, dout, filters, taps, skip[None], jnp.asarray(there), jnp.asarray(back)]
    vmem = pl.BlockSpec(memory_space=pltpu.VMEM)
    hbm = pl.BlockSpec(memory_space=pltpu.HBM)
    dma = pltpu.SemaphoreType.DMA
    return pl.pallas_call(
        mixer_kernel,
        out_shape=(pltpu.VMEM(dout.shape, bf), pltpu.VMEM(features.shape, bf)),
        in_specs=[hbm] * 8,
        out_specs=(vmem, vmem),
        scratch_shapes=[
            pltpu.SMEM(lengths.shape, jnp.int32),
            pltpu.VMEM((3, channels, span), bf),
            pltpu.VMEM((channels, span), bf),
            pltpu.VMEM((3, 3, channels), f32),
            pltpu.VMEM((1, channels), f32),
            pltpu.VMEM((channels, 128), f32),
            pltpu.VMEM((span, 2 * span), bf),
            pltpu.VMEM((span, 2 * span), bf),
            pltpu.VMEM((2 * span, span), bf),
            pltpu.VMEM((2, 8, span), f32),
            pltpu.VMEM((2, 8, span), f32),
            pltpu.VMEM((16, channels), bf),
            pltpu.VMEM((16, channels), bf),
            pltpu.VMEM((4, channels, span), bf),
            pltpu.VMEM((3, channels, span), bf),
            pltpu.VMEM((channels, span), bf),
            pltpu.VMEM((channels, span), bf),
            pltpu.VMEM((channels, span), bf),
            pltpu.VMEM((2, channels, span), bf),
            pltpu.VMEM((channels, span), f32),
            pltpu.VMEM((3, channels, span), bf),
            pltpu.VMEM((2, channels, span), bf),
            pltpu.VMEM((count, 2, 16, CH), bf),
            pltpu.VMEM((count, 2, 16, CH), bf),
            pltpu.VMEM((count, 16, CH), bf),
            pltpu.VMEM((count, 16, CH), bf),
            pltpu.VMEM((count, 16, CH), bf),
            pltpu.VMEM((3 * CH, 2 * span), f32),
            pltpu.VMEM((4 * CH, 2 * span), f32),
            pltpu.VMEM((5 * CH, 2 * span), bf),
            dma((9,)), dma, dma,
            dma((2, count)), dma((3, count)), dma((count,)), dma((4, count)),
            dma((count,)), dma((count,)), dma((3, count)), dma((2, count)),
            dma((count,)), dma((count,)), dma((count,)), dma((count,)),
        ],
        compiler_params=pltpu.CompilerParams(
            collective_id=0, has_side_effects=True, vmem_limit_bytes=32 * 1024 * 1024
        ),
    )(*[pltpu.with_memory_space_constraint(x, pltpu.HBM) for x in operands])


def local(features, dout, filters, taps, skip, lengths):
    channels, span = dout.shape
    fits = lax.axis_size("seq") == 4 and lax.axis_size("groups") == 2 and taps.shape[:2] == (3, 3)
    if fits and span == 256 and channels % (2 * CH) == 0:
        return local_kernel(features, dout, filters, taps, skip, lengths)
    return local_general(features, dout, filters, taps, skip, lengths)


def solution(mesh):
    in_specs = (
        P(None, ("chan", "sub"), ("groups", "seq")),
        P(("chan", "sub"), ("groups", "seq")),
        P(("chan", "sub"), "seq"),
        P(None, None, ("chan", "sub")),
        P(("chan", "sub")),
        P("groups"),
    )
    out_specs = (P(("chan", "sub"), ("groups", "seq")), P(None, ("chan", "sub"), ("groups", "seq")))
    return jax.shard_map(local, mesh=mesh, in_specs=in_specs, out_specs=out_specs, check_vma=False)
```

```python
import functools

import jax
import numpy as np
import jax.numpy as jnp
from jax import lax
from jax.experimental import pallas as pl
from jax.experimental.pallas import tpu as pltpu
from jax.sharding import PartitionSpec as P

HIGHEST = lax.Precision.HIGHEST
TWO_PI = 6.283185307179586


def shifted(value, axis, steps):
    count = lax.axis_size(axis)
    leading, last = (max(0, -steps), min(count, count - steps))
    return lax.ppermute(value, axis, [(source, source + steps) for source in range(leading, last)])


def genome_offsets(lengths, positions):
    order = jnp.arange(lengths.shape[0], dtype=jnp.int32)
    so_far = (order[None, :] <= order[:, None]).astype(jnp.int32)
    ends_at = jnp.sum(so_far * lengths[None, :], axis=1, dtype=jnp.int32)
    before = (ends_at[None, :] <= positions[:, None]).astype(jnp.int32)
    return positions - jnp.sum(before * lengths[None, :], axis=1, dtype=jnp.int32)


def short_forward(extended, taps_local, offsets):
    span_rows = offsets.shape[0]
    count = taps_local.shape[1]
    result = jnp.zeros(extended.shape[:2] + (span_rows,), jnp.float32)
    for tap_index in range(count):
        begin = count - 1 - tap_index
        window = extended[:, :, begin : begin + span_rows].astype(jnp.float32)
        keep_mask = (offsets >= tap_index).astype(jnp.float32)
        result = result + taps_local[:, tap_index, :, None] * window * keep_mask[None, None, :]
    return result


def short_backward(grads_ext, taps_local, offsets_ext):
    count = taps_local.shape[1]
    span_rows = offsets_ext.shape[0] - (count - 1)
    result = jnp.zeros(grads_ext.shape[:2] + (span_rows,), jnp.float32)
    for tap_index in range(count):
        window = grads_ext[:, :, tap_index : tap_index + span_rows]
        keep_mask = (offsets_ext[tap_index : tap_index + span_rows] >= tap_index).astype(
            jnp.float32
        )
        result = result + taps_local[:, tap_index, :, None] * window * keep_mask[None, None, :]
    return result


def dft_table(rows_n, cols_n, period):
    row_ids = jnp.arange(rows_n, dtype=jnp.int32)
    col_ids = jnp.arange(cols_n, dtype=jnp.int32)
    phase = row_ids[:, None] * col_ids[None, :] % period
    angles = phase.astype(jnp.float32) * (-TWO_PI / period)
    return (jnp.cos(angles), jnp.sin(angles))


def forward_transform(signal, tables):
    (row_re, row_im), (twid_re, twid_im), (col_re, col_im) = tables
    half_rows = signal.shape[1] // 128
    blocks_in = signal.reshape(signal.shape[0], half_rows, 128)
    part_re = jnp.einsum("kn,cnm->ckm", row_re[:, :half_rows], blocks_in, precision=HIGHEST)
    part_im = jnp.einsum("kn,cnm->ckm", row_im[:, :half_rows], blocks_in, precision=HIGHEST)
    turned_re = part_re * twid_re - part_im * twid_im
    turned_im = part_re * twid_im + part_im * twid_re
    spec_re = jnp.einsum("ckn,nm->ckm", turned_re, col_re, precision=HIGHEST) - jnp.einsum(
        "ckn,nm->ckm", turned_im, col_im, precision=HIGHEST
    )
    spec_im = jnp.einsum("ckn,nm->ckm", turned_re, col_im, precision=HIGHEST) + jnp.einsum(
        "ckn,nm->ckm", turned_im, col_re, precision=HIGHEST
    )
    return (spec_re, spec_im)


def inverse_transform(spec_re, spec_im, tables):
    (row_re, row_im), (twid_re, twid_im), (col_re, col_im) = tables
    rows_n = spec_re.shape[1]
    half_rows = rows_n // 2
    mid_re = jnp.einsum("ckn,nm->ckm", spec_re, col_re, precision=HIGHEST) + jnp.einsum(
        "ckn,nm->ckm", spec_im, col_im, precision=HIGHEST
    )
    mid_im = jnp.einsum("ckn,nm->ckm", spec_im, col_re, precision=HIGHEST) - jnp.einsum(
        "ckn,nm->ckm", spec_re, col_im, precision=HIGHEST
    )
    back_re = mid_re * twid_re + mid_im * twid_im
    back_im = mid_im * twid_re - mid_re * twid_im
    signal = jnp.einsum("nk,ckm->cnm", row_re[:half_rows], back_re, precision=HIGHEST) + jnp.einsum(
        "nk,ckm->cnm", row_im[:half_rows], back_im, precision=HIGHEST
    )
    return signal.reshape(signal.shape[0], half_rows * 128) * (1.0 / (rows_n * 128))


def long_filter(filt, mixed_in, grad_in, skip_part):
    rows_n = 2 * mixed_in.shape[1] // 128
    tables = (
        dft_table(rows_n, rows_n, rows_n),
        dft_table(rows_n, 128, rows_n * 128),
        dft_table(128, 128, 128),
    )
    mixed_f = mixed_in.astype(jnp.float32)
    grad_f = grad_in.astype(jnp.float32)
    filt_re, filt_im = forward_transform(filt.astype(jnp.float32), tables)
    mix_re, mix_im = forward_transform(mixed_f, tables)
    grad_re, grad_im = forward_transform(grad_f, tables)
    conv_out = inverse_transform(
        filt_re * mix_re - filt_im * mix_im, filt_re * mix_im + filt_im * mix_re, tables
    )
    corr_out = inverse_transform(
        filt_re * grad_re + filt_im * grad_im, filt_re * grad_im - filt_im * grad_re, tables
    )
    y_out = (conv_out + skip_part[:, None] * mixed_f).astype(jnp.bfloat16)
    dmixed = (corr_out + skip_part[:, None] * grad_f).astype(jnp.bfloat16)
    return (y_out, dmixed)


DENSE_MAX = 1024
FINE = 32


def angle_parts(length):
    base = np.arange(length, dtype=np.int64) * 4 + 1
    fine = np.arange(FINE, dtype=np.int64)[:, None] * base[None, :] % (4 * length)
    coarse = np.arange(0, length, FINE, dtype=np.int64)[:, None] * base[None, :] % (4 * length)
    scale = 2.0 * np.pi / (4 * length)
    return [
        func(part * scale).astype(np.float32)
        for part in (coarse, fine)
        for func in (np.cos, np.sin)
    ]


def dense_filter(filt, mixed_in, grad_in, skip_part):
    length = mixed_in.shape[1]
    cc, cs, fc, fs = [jnp.asarray(p)[:, None] if i < 2 else jnp.asarray(p)[None] for i, p in enumerate(angle_parts(length))]
    cos_t = (cc * fc - cs * fs).reshape(length, length)
    sin_t = (cs * fc + cc * fs).reshape(length, length)
    table = jnp.concatenate([cos_t, sin_t], axis=1).astype(jnp.bfloat16)

    def fwd(x):
        return jnp.dot(x, table, preferred_element_type=jnp.float32)

    def inv(x):
        return lax.dot_general(x.astype(jnp.bfloat16), table, (((1,), (1,)), ((), ())), preferred_element_type=jnp.float32) * (1.0 / length)

    h, m, g = fwd(filt), fwd(mixed_in), fwd(grad_in)
    hc, hs = h[:, :length], h[:, length:]
    mc, ms = m[:, :length], m[:, length:]
    gc, gs = g[:, :length], g[:, length:]
    conv_out = inv(jnp.concatenate([hc * mc - hs * ms, hc * ms + hs * mc], axis=1))
    corr_out = inv(jnp.concatenate([hc * gc + hs * gs, hc * gs - hs * gc], axis=1))
    y_out = (conv_out + skip_part[:, None] * mixed_in.astype(jnp.float32)).astype(jnp.bfloat16)
    dmixed = (corr_out + skip_part[:, None] * grad_in.astype(jnp.float32)).astype(jnp.bfloat16)
    return (y_out, dmixed)


def to_channels(stacked):
    return lax.all_to_all(stacked, "seq", split_axis=1, concat_axis=2, tiled=True)


def to_sequence(stacked):
    return lax.all_to_all(stacked, "seq", split_axis=2, concat_axis=1, tiled=True)


def local_general(features, dout, filters, taps, skip, lengths):
    blocks = lax.axis_size("seq")
    seq_rank = lax.axis_index("seq")
    span_rows = features.shape[2]
    channels_here = features.shape[1]
    chan_part = channels_here // blocks
    count = taps.shape[1]
    margin = count - 1
    rim = shifted(features[:, :, span_rows - margin :], "seq", 1)
    extended = jnp.concatenate([rim, features], axis=2)
    first_pos = seq_rank * span_rows
    offsets = genome_offsets(lengths, first_pos + jnp.arange(span_rows, dtype=jnp.int32))
    filtered = short_forward(extended, taps, offsets).astype(jnp.bfloat16)
    query_side = filtered[0].astype(jnp.float32)
    key_side = filtered[1].astype(jnp.float32)
    value_side = filtered[2].astype(jnp.float32)
    dout_f = dout.astype(jnp.float32)
    mixed = (key_side * value_side).astype(jnp.bfloat16)
    grad_in = (dout_f * query_side).astype(jnp.bfloat16)
    moved = to_channels(jnp.stack([mixed, grad_in, filters]))
    skip_part = lax.dynamic_slice_in_dim(skip, seq_rank * chan_part, chan_part, 0)
    run = dense_filter if moved.shape[2] <= DENSE_MAX else long_filter
    y_out, dmixed = run(moved[2], moved[0], moved[1], skip_part)
    returned = to_sequence(jnp.stack([y_out, dmixed]))
    y_here = returned[0].astype(jnp.float32)
    dmixed_here = returned[1].astype(jnp.float32)
    out = (query_side * y_here).astype(jnp.bfloat16)
    grads = jnp.stack([dout_f * y_here, dmixed_here * value_side, dmixed_here * key_side])
    ahead = shifted(grads[:, :, :margin], "seq", -1)
    grads_ext = jnp.concatenate([grads, ahead], axis=2)
    offsets_ext = genome_offsets(
        lengths, first_pos + jnp.arange(span_rows + margin, dtype=jnp.int32)
    )
    dfeatures = short_backward(grads_ext, taps, offsets_ext).astype(jnp.bfloat16)
    return (out, dfeatures)


CH = 128
BACK = 7
RELAY = 4
HOLD = 3
NN = (((1,), (0,)), ((), ()))
NT = (((1,), (1,)), ((), ()))
TN = (((0,), (0,)), ((), ()))
MESH = pl.DeviceIdType.MESH


def mm(a, b, dims=NN):
    return lax.dot_general(a, b, dims, preferred_element_type=jnp.float32)


def block_tables(size):
    place = np.arange(size, dtype=np.int64)
    phase = place[:, None] * (4 * place[None, :] + 1) % (4 * size)
    angle = phase * (2.0 * np.pi / (4 * size))
    cos, sin = np.cos(angle), np.sin(angle)
    there = np.stack([np.concatenate([cos, s * sin], axis=1) for s in (1, -1)])
    back = np.stack([np.concatenate([cos.T, s * sin.T], axis=0) for s in (1, -1)]) / size
    return there.astype(jnp.bfloat16), back.astype(jnp.bfloat16)


def mixer_kernel(
    lengths_hbm, feat_hbm, dout_hbm, filt_hbm, taps_hbm, skip_hbm, there_hbm, back_hbm,
    out_ref, df_ref,
    lengths_ref, xf, xd, taps_v, skip_v, par, wh, wsig, winv, keep_f, keep_b,
    rim_src, rim, h_all, sig, q_s, k_s, v_s, yd, w_loc, c_src, c_in,
    hal_src, hal, mini_src, mini, mini_own, spec_s, spec_h, prod,
    ld, rim_ss, rim_rs, h_zs, h_ys, h_bs, h_rs, u_ss, u_rs, c_ss, c_rs, hal_ss, hal_rs, mini_ss, mini_rs,
):
    rank = lax.axis_index("seq")
    group = lax.axis_index("groups")
    channels, span = xd.shape
    count = channels // CH
    half = count // 2
    mir = rank // 2
    inn = lax.rem(rank + mir, 2)
    inner = inn == 1
    inward = rank + 1 - 2 * mir
    outward = rank - 1 + 2 * mir
    far = 3 - 3 * mir
    bf = jnp.bfloat16
    f32 = jnp.float32

    loads = [
        pltpu.make_async_copy(feat_hbm, xf, ld.at[0]),
        pltpu.make_async_copy(taps_hbm, taps_v, ld.at[1]),
        pltpu.make_async_copy(skip_hbm, skip_v, ld.at[2]),
        pltpu.make_async_copy(dout_hbm, xd, ld.at[3]),
        pltpu.make_async_copy(filt_hbm, h_all.at[rank], ld.at[4]),
        pltpu.make_async_copy(there_hbm.at[0], wh, ld.at[5]),
        pltpu.make_async_copy(there_hbm.at[mir], wsig, ld.at[6]),
        pltpu.make_async_copy(back_hbm.at[mir], winv, ld.at[7]),
        pltpu.make_async_copy(lengths_hbm, lengths_ref, ld.at[8]),
    ]
    for load in loads:
        load.start()

    def greet(**where):
        pl.semaphore_signal(barrier, inc=1, device_id=where, device_id_type=MESH)

    barrier = pltpu.get_barrier_semaphore()
    greet(seq=inward)

    @pl.when(inner)
    def _():
        greet(seq=outward)

    @pl.when(inn == 0)
    def _():
        greet(seq=2 - mir)

    @pl.when(rank > 0)
    def _():
        greet(groups=1 - group)

    def rows_of(i):
        c = lax.rem(half * group + i, count)
        return c, pl.ds(pl.multiple_of(c * CH, CH), CH)

    def remote(src, dst, ss, rs, where):
        return pltpu.make_async_remote_copy(
            src_ref=src, dst_ref=dst, send_sem=ss, recv_sem=rs, device_id=where, device_id_type=MESH
        )

    def h_own_copy(i):
        c, rows = rows_of(i)
        return remote(filt_hbm.at[rows], h_all.at[rank, rows], h_zs.at[0, i], h_rs.at[rank, c], {"seq": inward})

    def h_on_copy(i):
        c, rows = rows_of(i)
        return remote(h_all.at[outward, rows], h_all.at[outward, rows], h_zs.at[1, i], h_rs.at[outward, c], {"seq": inward})

    def h_back_copy(i):
        c, rows = rows_of(i)
        return remote(h_all.at[0, rows], h_all.at[0, rows], h_bs.at[i], h_rs.at[0, c], {"seq": 3})

    def h_over_copy(which, slot, i):
        c, rows = rows_of(i)
        return remote(
            h_all.at[slot, rows], h_all.at[slot, rows], h_ys.at[which, i], h_rs.at[slot, c], {"groups": 1 - group}
        )

    def h_arrival(slot, i):
        c, rows = rows_of(i)
        return remote(h_all.at[slot, rows], h_all.at[slot, rows], h_zs.at[0, 0], h_rs.at[slot, c], {"seq": inward})

    def u_copy(i):
        c, rows = rows_of(i)
        return remote(sig.at[0, rows], sig.at[2, rows], u_ss.at[i], u_rs.at[c], {"seq": inward})

    def c_copy(which, i):
        c, rows = rows_of(i)
        direct = (i >= RELAY).astype(jnp.int32)
        slot = (0, 1 - direct, 1)[which]
        where = (inward, inward + (far - inward) * direct, outward)[which]
        return remote(
            c_src.at[which, rows], c_in.at[slot, rows], c_ss.at[which, i], c_rs.at[slot, c], {"seq": where}
        )

    def c_arrival(slot, i):
        c, rows = rows_of(i)
        return remote(c_in.at[slot, rows], c_in.at[slot, rows], c_ss.at[0, i], c_rs.at[slot, c], {"seq": inward})

    def mini_copy(i):
        c, _ = rows_of(i)
        where = (2 - 2 * mir) * (i >= RELAY).astype(jnp.int32)
        return remote(mini_src.at[c], mini.at[c], mini_ss.at[i], mini_rs.at[c], {"seq": where})

    def rim_copy():
        return remote(rim_src, rim, rim_ss, rim_rs, {"seq": rank + 1})

    def hal_copy(i):
        c, _ = rows_of(i)
        return remote(hal_src.at[c], hal.at[c], hal_ss.at[i], hal_rs.at[c], {"seq": rank - 1})

    @pl.when(rank == 0)
    def _():
        rim[...] = jnp.zeros_like(rim)

    @pl.when(rank == 3)
    def _():
        hal[...] = jnp.zeros_like(hal)

    @pl.when(lax.rem(rank, 2) == 1)
    def _():
        mini[...] = jnp.zeros_like(mini)

    @pl.when(rank == 2)
    def _():
        for i in range(min(RELAY, count)):
            mini[rows_of(i)[0]] = jnp.zeros((16, CH), bf)

    @pl.when(inn == 0)
    def _():
        mini_own[...] = jnp.zeros_like(mini_own)

    pl.semaphore_wait(barrier, 1 + 3 * inn + rank // 3)

    h_own_copy(0).start()

    loads[0].wait()
    r_id = lax.broadcasted_iota(jnp.int32, (16, 128), 0)
    p_id = lax.broadcasted_iota(jnp.int32, (16, 128), 1)
    total = None
    for part in range(2):
        for a in range(3):
            first = 8 * part + 2 * a
            hit = ((r_id == first) & (p_id == 126)) | ((r_id == first + 1) & (p_id == 127))
            edge = xf[a, part * half * CH : (part + 1) * half * CH, span - 128 :]
            term = mm(jnp.where(hit, 1.0, 0.0).astype(bf), edge, NT)
            total = term if total is None else total + term
    rim_src[...] = total.astype(bf)

    @pl.when(rank < 3)
    def _():
        rim_copy().start()

    for i in range(1, half):
        h_own_copy(i).start()

    loads[8].wait()

    def keeps(ahead, least):
        position = rank * span + ahead + lax.broadcasted_iota(jnp.int32, (8, span), 1)
        offset = position
        end = jnp.int32(0)
        for g in range(lengths_ref.shape[0]):
            one = lengths_ref[g]
            end = end + one
            offset = offset - jnp.where(end <= position, one, 0)
        return jnp.where(offset >= least, 1.0, 0.0)

    for j in (1, 2):
        keep_f[j - 1] = keeps(0, j)
        keep_b[j - 1] = keeps(j, j)

    loads[1].wait()
    loads[2].wait()
    flat = jnp.concatenate(
        [taps_v[0], taps_v[1], taps_v[2], skip_v[...], jnp.zeros((6, channels), f32)], axis=0
    )
    for c in range(count):
        par[c * CH : (c + 1) * CH, 0:16] = flat[:, c * CH : (c + 1) * CH].T
    for load in loads[3:8]:
        load.wait()

    def pass_on(i):
        h_arrival(outward, i).wait_recv()
        h_on_copy(i).start()
        h_over_copy(0, outward, i).start()

    @pl.when(inner)
    def _():
        for i in range(min(2, half)):
            pass_on(i)

    @pl.when(rank > 0)
    def _():
        rim_copy().wait_recv()

    rr = lax.broadcasted_iota(jnp.int32, (16, 384), 0)
    cc = lax.broadcasted_iota(jnp.int32, (16, 384), 1)

    def spread(first, above=0):
        hit = None
        for a in range(3):
            row = 2 * a + above
            one = ((rr == row) & (cc == 128 * a + first)) | ((rr == row + 1) & (cc == 128 * a + first + 1))
            hit = one if hit is None else hit | one
        return jnp.where(hit, 1.0, 0.0).astype(bf)

    def prepare(i):
        c, rows = rows_of(i)
        upper = c // half
        cols = pl.ds(pl.multiple_of((c - half * upper) * CH, CH), CH)
        edge = mm(rim[:, cols], spread(126, 8 * upper), TN)
        tap = par[rows, :]
        result = []
        for a in range(3):
            here = xf[a, rows, :].astype(f32)
            wide = jnp.concatenate([edge[:, 128 * a : 128 * a + 128], here], axis=1)
            acc = tap[:, 3 * a : 3 * a + 1] * here
            for j in (1, 2):
                moved = pltpu.roll(wide, j, 1)[:, 128:]
                acc = acc + tap[:, 3 * a + j : 3 * a + j + 1] * (moved * keep_f[j - 1, 0:1, :])
            result.append(acc.astype(bf))
        q, k, v = result
        q_s[rows, :] = q
        k_s[rows, :] = k
        v_s[rows, :] = v
        sig[mir, rows, :] = (k.astype(f32) * v.astype(f32)).astype(bf)
        sig[1 - mir, rows, :] = (xd[rows, :].astype(f32) * q.astype(f32)).astype(bf)

        @pl.when(inn == 0)
        def _():
            u_copy(i).start()

        @pl.when(inner & (i + 2 < half))
        def _():
            pass_on(i + 2)

    def pick(block, rows_at):
        hit = None
        for first, lane in rows_at:
            one = ((r_id == first) & (p_id == lane)) | ((r_id == first + 1) & (p_id == lane + 1))
            hit = one if hit is None else hit | one
        return mm(jnp.where(hit, 1.0, 0.0).astype(bf), block, NT)

    def keep_local(rows, value):
        skip = par[rows, 9:10]
        yd[0, rows, :] = (value[0:CH] + skip * sig[0, rows, :].astype(f32)).astype(bf)
        other = value[CH : 2 * CH] + skip * sig[1, rows, :].astype(f32)
        w_loc[rows, :] = other
        yd[1, rows, :] = other.astype(bf)

    def products(terms_of):
        def block(b, carry):
            first = pl.multiple_of(b * 16, 16)

            def pair(ref, k):
                at = pl.ds(k * CH + first, 16)
                return ref[at, 0:span], ref[at, span:]

            for k, terms in enumerate(terms_of(lambda n: pair(spec_h, n), lambda n: pair(spec_s, n))):
                re = im = None
                for (tc, ts), (xc, xs), sign in terms:
                    if sign > 0:
                        new_re, new_im = tc * xc - ts * xs, tc * xs + ts * xc
                    else:
                        new_re, new_im = tc * xc + ts * xs, tc * xs - ts * xc
                    re = new_re if re is None else re + new_re
                    im = new_im if im is None else im + new_im
                at = pl.ds(k * CH + first, 16)
                prod[at, 0:span] = re.astype(bf)
                prod[at, span:] = im.astype(bf)
            return carry

        lax.fori_loop(0, CH // 16, block, 0)

    def inner_terms(h, s):
        hs = [h(k) for k in range(4)]
        t = [hs[0]] + [(hs[k][0] + hs[k - 1][1], hs[k][1] - hs[k - 1][0]) for k in (1, 2, 3)]
        own, other, near = [s(k) for k in range(3)]
        return [
            [(t[0], own, 1), (t[1], near, 1)],
            [(t[0], other, -1)],
            [(t[1], own, 1), (t[2], near, 1)],
            [(t[2], own, 1), (t[3], near, 1)],
            [(t[1], other, -1)],
        ]

    def outer_terms(h, s):
        return [[(h(0), s(0), 1)], [(h(0), s(1), -1)]]

    def main_inner(i):
        c, rows = rows_of(i)

        @pl.when(i < half)
        def _():
            h_arrival(inward, i).wait_recv()
            h_over_copy(1, inward, i).start()
            h_arrival(far, i).wait_recv()
            h_over_copy(2, far, i).start()

            @pl.when(rank == 2)
            def _():
                h_back_copy(i).start()

        @pl.when(i >= half)
        def _():
            h_arrival(outward, i).wait_recv()
            h_arrival(inward, i).wait_recv()
            h_arrival(far, i).wait_recv()

        u_copy(i).wait_recv()
        spec_h[...] = mm(h_all[:, rows, :].reshape(4 * CH, span), wh[...])
        spec_s[...] = mm(sig[:, rows, :].reshape(3 * CH, span), wsig[...])
        products(inner_terms)
        value = mm(prod[...], winv[...])
        for which in range(3):
            c_src[which, rows, :] = value[(2 + which) * CH : (3 + which) * CH].astype(bf)

        @pl.when(i >= RELAY)
        def _():
            mini_src[c] = pick(c_src[1 - mir, rows, 0:128], [(8 - 6 * mir, 0), (8 - 4 * mir, 0)]).astype(bf)
            mini_copy(i).start()

        c_copy(1, i).start()

        c_copy(0, i).start()

        @pl.when(i >= RELAY)
        def _():
            c_copy(2, i).start()

        @pl.when((rank == 1) | (i >= RELAY))
        def _():
            mini_own[c] = pick(c_src[2 * mir, rows, 0:128], [(8, 0)]).astype(bf)

        keep_local(rows, value)

    def relay(i):
        c, rows = rows_of(i)
        c_arrival(1, i).wait_recv()
        c_src[2, rows, :] = (c_src[2, rows, :].astype(f32) + c_in[1, rows, :].astype(f32)).astype(bf)
        c_copy(2, i).start()
        c_arrival(0, i).wait_recv()

        @pl.when(rank == 1)
        def _():
            mini_src[c] = pick(c_in[0, rows, 0:128], [(2, 0), (4, 0)]).astype(bf)
            mini_copy(i).start()

        @pl.when(rank == 2)
        def _():
            mini_own[c] = pick(c_src[2, rows, 0:128], [(8, 0)]).astype(bf)

    def main_outer(i):
        c, rows = rows_of(i)

        @pl.when(rank == 3)
        def _():
            h_arrival(0, i).wait_recv()

            @pl.when(i < half)
            def _():
                h_over_copy(0, 0, i).start()

        spec_h[0:CH] = mm(h_all[0, rows, :], wh[...])
        spec_s[0 : 2 * CH] = mm(sig[0:2, rows, :].reshape(2 * CH, span), wsig[...])
        products(outer_terms)
        keep_local(rows, mm(prod[0 : 2 * CH], winv[...]))

    def grads_of(rows, lanes):
        y = yd[mir, rows, lanes].astype(f32)
        dm = yd[1 - mir, rows, lanes].astype(f32)
        return [
            xd[rows, lanes].astype(f32) * y,
            dm * v_s[rows, lanes].astype(f32),
            dm * k_s[rows, lanes].astype(f32),
        ]

    def halo(i):
        c, rows = rows_of(i)
        first = slice(0, 128)
        edge = pick(xd[rows, first], [(0, 0)]) + pick(yd[1 - mir, rows, first], [(2, 0), (4, 0)])
        edge = edge + pick(yd[mir, rows, first], [(8, 0)])
        edge = edge + pick(v_s[rows, first], [(10, 0)]) + pick(k_s[rows, first], [(12, 0)])
        hal_src[c] = edge.astype(bf)
        hal_copy(i).start()

    def finish(i):
        c, rows = rows_of(i)

        @pl.when(i >= RELAY)
        def _():
            c_arrival(0, i).wait_recv()

        @pl.when(inner)
        def _():
            yd[1, rows, :] = (w_loc[rows, :] + c_in[0, rows, :].astype(f32)).astype(bf)

        @pl.when((inn == 0) & (i >= RELAY))
        def _():
            c_arrival(1, i).wait_recv()
            cross = c_in[0, rows, :].astype(f32) + c_in[1, rows, :].astype(f32)
            yd[1, rows, :] = (w_loc[rows, :] + cross).astype(bf)

        @pl.when((inn == 0) & (i < RELAY))
        def _():
            c_arrival(1, i).wait_recv()
            yd[1, rows, :] = (w_loc[rows, :] + c_in[1, rows, :].astype(f32)).astype(bf)

        @pl.when(rank < 3)
        def _():
            hal_copy(i).wait_recv()

        @pl.when((rank == 0) | ((rank == 2) & (i >= RELAY)))
        def _():
            mini_copy(i).wait_recv()

        both = hal[c].astype(f32) + mini[c].astype(f32) + mini_own[c].astype(f32)
        first_grads = jnp.concatenate([both[0:8] * both[8:16], jnp.zeros((8, CH), f32)], axis=0)
        tap = par[rows, :]
        edge = mm(first_grads.astype(bf), spread(0), TN)
        y = yd[mir, rows, :].astype(f32)
        out_ref[rows, :] = (q_s[rows, :].astype(f32) * y).astype(bf)
        for a, grad in enumerate(grads_of(rows, slice(None))):
            wide = jnp.concatenate([grad, edge[:, 128 * a : 128 * a + 128]], axis=1)
            acc = tap[:, 3 * a : 3 * a + 1] * grad
            for j in (1, 2):
                moved = pltpu.roll(wide, span + 128 - j, 1)[:, :span]
                acc = acc + tap[:, 3 * a + j : 3 * a + j + 1] * (moved * keep_b[j - 1, 0:1, :])
            df_ref[a, rows, :] = acc.astype(bf)

    def first_steps(s, carry):
        prepare(s)
        return carry

    lax.fori_loop(0, count, first_steps, 0)

    def step(s, carry):
        main = s < count

        @pl.when(inner & main)
        def _():
            main_inner(s)

        @pl.when((inn == 0) & main)
        def _():
            main_outer(s)

        @pl.when((rank > 0) & main)
        def _():
            halo(s)

        @pl.when(inner & (s >= HOLD) & (s < RELAY + HOLD) & (s < count + HOLD))
        def _():
            relay(s - HOLD)

        @pl.when(s >= BACK)
        def _():
            finish(s - BACK)

        return carry

    lax.fori_loop(0, count + BACK, step, 0)

    @pl.when(rank < 3)
    def _():
        rim_copy().wait_send()

    def drain(i, carry):
        @pl.when(inn == 0)
        def _():
            u_copy(i).wait_send()

        @pl.when(rank > 0)
        def _():
            hal_copy(i).wait_send()

        @pl.when(inner)
        def _():
            for which in range(3):
                c_copy(which, i).wait_send()

        @pl.when((rank == 1) | ((rank == 2) & (i >= RELAY)))
        def _():
            mini_copy(i).wait_send()

        @pl.when(i < half)
        def _():
            h_own_copy(i).wait_send()

            @pl.when(inner)
            def _():
                h_on_copy(i).wait_send()
                h_over_copy(0, outward, i).wait_send()
                h_over_copy(1, inward, i).wait_send()
                h_over_copy(2, far, i).wait_send()

            @pl.when(rank == 2)
            def _():
                h_back_copy(i).wait_send()

            @pl.when(rank == 3)
            def _():
                h_over_copy(0, 0, i).wait_send()

        return carry

    lax.fori_loop(0, count, drain, 0)


def local_kernel(features, dout, filters, taps, skip, lengths):
    channels, span = dout.shape
    count = channels // CH
    bf = jnp.bfloat16
    f32 = jnp.float32
    there, back = block_tables(span)
    operands = [lengths, features, dout, filters, taps, skip[None], jnp.asarray(there), jnp.asarray(back)]
    vmem = pl.BlockSpec(memory_space=pltpu.VMEM)
    hbm = pl.BlockSpec(memory_space=pltpu.HBM)
    dma = pltpu.SemaphoreType.DMA
    return pl.pallas_call(
        mixer_kernel,
        out_shape=(pltpu.VMEM(dout.shape, bf), pltpu.VMEM(features.shape, bf)),
        in_specs=[hbm] * 8,
        out_specs=(vmem, vmem),
        scratch_shapes=[
            pltpu.SMEM(lengths.shape, jnp.int32),
            pltpu.VMEM((3, channels, span), bf),
            pltpu.VMEM((channels, span), bf),
            pltpu.VMEM((3, 3, channels), f32),
            pltpu.VMEM((1, channels), f32),
            pltpu.VMEM((channels, 128), f32),
            pltpu.VMEM((span, 2 * span), bf),
            pltpu.VMEM((span, 2 * span), bf),
            pltpu.VMEM((2 * span, span), bf),
            pltpu.VMEM((2, 8, span), f32),
            pltpu.VMEM((2, 8, span), f32),
            pltpu.VMEM((16, channels // 2), bf),
            pltpu.VMEM((16, channels // 2), bf),
            pltpu.VMEM((4, channels, span), bf),
            pltpu.VMEM((3, channels, span), bf),
            pltpu.VMEM((channels, span), bf),
            pltpu.VMEM((channels, span), bf),
            pltpu.VMEM((channels, span), bf),
            pltpu.VMEM((2, channels, span), bf),
            pltpu.VMEM((channels, span), f32),
            pltpu.VMEM((3, channels, span), bf),
            pltpu.VMEM((2, channels, span), bf),
            pltpu.VMEM((count, 16, CH), bf),
            pltpu.VMEM((count, 16, CH), bf),
            pltpu.VMEM((count, 16, CH), bf),
            pltpu.VMEM((count, 16, CH), bf),
            pltpu.VMEM((count, 16, CH), bf),
            pltpu.VMEM((3 * CH, 2 * span), f32),
            pltpu.VMEM((4 * CH, 2 * span), f32),
            pltpu.VMEM((5 * CH, 2 * span), bf),
            dma((9,)), dma, dma,
            dma((2, count)), dma((3, count)), dma((count,)), dma((4, count)),
            dma((count,)), dma((count,)), dma((3, count)), dma((2, count)),
            dma((count,)), dma((count,)), dma((count,)), dma((count,)),
        ],
        compiler_params=pltpu.CompilerParams(
            collective_id=0, has_side_effects=True, vmem_limit_bytes=32 * 1024 * 1024
        ),
    )(*[pltpu.with_memory_space_constraint(x, pltpu.HBM) for x in operands])


def local(features, dout, filters, taps, skip, lengths):
    channels, span = dout.shape
    fits = lax.axis_size("seq") == 4 and lax.axis_size("groups") == 2 and taps.shape[:2] == (3, 3)
    if fits and span == 256 and channels % (2 * CH) == 0:
        return local_kernel(features, dout, filters, taps, skip, lengths)
    return local_general(features, dout, filters, taps, skip, lengths)


def solution(mesh):
    in_specs = (
        P(None, ("chan", "sub"), ("groups", "seq")),
        P(("chan", "sub"), ("groups", "seq")),
        P(("chan", "sub"), "seq"),
        P(None, None, ("chan", "sub")),
        P(("chan", "sub")),
        P("groups"),
    )
    out_specs = (P(("chan", "sub"), ("groups", "seq")), P(None, ("chan", "sub"), ("groups", "seq")))
    return jax.shard_map(local, mesh=mesh, in_specs=in_specs, out_specs=out_specs, check_vma=False)
```

```python
import functools

import jax
import numpy as np
import jax.numpy as jnp
from jax import lax
from jax.experimental import pallas as pl
from jax.experimental.pallas import tpu as pltpu
from jax.sharding import PartitionSpec as P

HIGHEST = lax.Precision.HIGHEST
TWO_PI = 6.283185307179586


def shifted(value, axis, steps):
    count = lax.axis_size(axis)
    leading, last = (max(0, -steps), min(count, count - steps))
    return lax.ppermute(value, axis, [(source, source + steps) for source in range(leading, last)])


def genome_offsets(lengths, positions):
    order = jnp.arange(lengths.shape[0], dtype=jnp.int32)
    so_far = (order[None, :] <= order[:, None]).astype(jnp.int32)
    ends_at = jnp.sum(so_far * lengths[None, :], axis=1, dtype=jnp.int32)
    before = (ends_at[None, :] <= positions[:, None]).astype(jnp.int32)
    return positions - jnp.sum(before * lengths[None, :], axis=1, dtype=jnp.int32)


def short_forward(extended, taps_local, offsets):
    span_rows = offsets.shape[0]
    count = taps_local.shape[1]
    result = jnp.zeros(extended.shape[:2] + (span_rows,), jnp.float32)
    for tap_index in range(count):
        begin = count - 1 - tap_index
        window = extended[:, :, begin : begin + span_rows].astype(jnp.float32)
        keep_mask = (offsets >= tap_index).astype(jnp.float32)
        result = result + taps_local[:, tap_index, :, None] * window * keep_mask[None, None, :]
    return result


def short_backward(grads_ext, taps_local, offsets_ext):
    count = taps_local.shape[1]
    span_rows = offsets_ext.shape[0] - (count - 1)
    result = jnp.zeros(grads_ext.shape[:2] + (span_rows,), jnp.float32)
    for tap_index in range(count):
        window = grads_ext[:, :, tap_index : tap_index + span_rows]
        keep_mask = (offsets_ext[tap_index : tap_index + span_rows] >= tap_index).astype(
            jnp.float32
        )
        result = result + taps_local[:, tap_index, :, None] * window * keep_mask[None, None, :]
    return result


def dft_table(rows_n, cols_n, period):
    row_ids = jnp.arange(rows_n, dtype=jnp.int32)
    col_ids = jnp.arange(cols_n, dtype=jnp.int32)
    phase = row_ids[:, None] * col_ids[None, :] % period
    angles = phase.astype(jnp.float32) * (-TWO_PI / period)
    return (jnp.cos(angles), jnp.sin(angles))


def forward_transform(signal, tables):
    (row_re, row_im), (twid_re, twid_im), (col_re, col_im) = tables
    half_rows = signal.shape[1] // 128
    blocks_in = signal.reshape(signal.shape[0], half_rows, 128)
    part_re = jnp.einsum("kn,cnm->ckm", row_re[:, :half_rows], blocks_in, precision=HIGHEST)
    part_im = jnp.einsum("kn,cnm->ckm", row_im[:, :half_rows], blocks_in, precision=HIGHEST)
    turned_re = part_re * twid_re - part_im * twid_im
    turned_im = part_re * twid_im + part_im * twid_re
    spec_re = jnp.einsum("ckn,nm->ckm", turned_re, col_re, precision=HIGHEST) - jnp.einsum(
        "ckn,nm->ckm", turned_im, col_im, precision=HIGHEST
    )
    spec_im = jnp.einsum("ckn,nm->ckm", turned_re, col_im, precision=HIGHEST) + jnp.einsum(
        "ckn,nm->ckm", turned_im, col_re, precision=HIGHEST
    )
    return (spec_re, spec_im)


def inverse_transform(spec_re, spec_im, tables):
    (row_re, row_im), (twid_re, twid_im), (col_re, col_im) = tables
    rows_n = spec_re.shape[1]
    half_rows = rows_n // 2
    mid_re = jnp.einsum("ckn,nm->ckm", spec_re, col_re, precision=HIGHEST) + jnp.einsum(
        "ckn,nm->ckm", spec_im, col_im, precision=HIGHEST
    )
    mid_im = jnp.einsum("ckn,nm->ckm", spec_im, col_re, precision=HIGHEST) - jnp.einsum(
        "ckn,nm->ckm", spec_re, col_im, precision=HIGHEST
    )
    back_re = mid_re * twid_re + mid_im * twid_im
    back_im = mid_im * twid_re - mid_re * twid_im
    signal = jnp.einsum("nk,ckm->cnm", row_re[:half_rows], back_re, precision=HIGHEST) + jnp.einsum(
        "nk,ckm->cnm", row_im[:half_rows], back_im, precision=HIGHEST
    )
    return signal.reshape(signal.shape[0], half_rows * 128) * (1.0 / (rows_n * 128))


def long_filter(filt, mixed_in, grad_in, skip_part):
    rows_n = 2 * mixed_in.shape[1] // 128
    tables = (
        dft_table(rows_n, rows_n, rows_n),
        dft_table(rows_n, 128, rows_n * 128),
        dft_table(128, 128, 128),
    )
    mixed_f = mixed_in.astype(jnp.float32)
    grad_f = grad_in.astype(jnp.float32)
    filt_re, filt_im = forward_transform(filt.astype(jnp.float32), tables)
    mix_re, mix_im = forward_transform(mixed_f, tables)
    grad_re, grad_im = forward_transform(grad_f, tables)
    conv_out = inverse_transform(
        filt_re * mix_re - filt_im * mix_im, filt_re * mix_im + filt_im * mix_re, tables
    )
    corr_out = inverse_transform(
        filt_re * grad_re + filt_im * grad_im, filt_re * grad_im - filt_im * grad_re, tables
    )
    y_out = (conv_out + skip_part[:, None] * mixed_f).astype(jnp.bfloat16)
    dmixed = (corr_out + skip_part[:, None] * grad_f).astype(jnp.bfloat16)
    return (y_out, dmixed)


DENSE_MAX = 1024
FINE = 32


def angle_parts(length):
    base = np.arange(length, dtype=np.int64) * 4 + 1
    fine = np.arange(FINE, dtype=np.int64)[:, None] * base[None, :] % (4 * length)
    coarse = np.arange(0, length, FINE, dtype=np.int64)[:, None] * base[None, :] % (4 * length)
    scale = 2.0 * np.pi / (4 * length)
    return [
        func(part * scale).astype(np.float32)
        for part in (coarse, fine)
        for func in (np.cos, np.sin)
    ]


def dense_filter(filt, mixed_in, grad_in, skip_part):
    length = mixed_in.shape[1]
    cc, cs, fc, fs = [jnp.asarray(p)[:, None] if i < 2 else jnp.asarray(p)[None] for i, p in enumerate(angle_parts(length))]
    cos_t = (cc * fc - cs * fs).reshape(length, length)
    sin_t = (cs * fc + cc * fs).reshape(length, length)
    table = jnp.concatenate([cos_t, sin_t], axis=1).astype(jnp.bfloat16)

    def fwd(x):
        return jnp.dot(x, table, preferred_element_type=jnp.float32)

    def inv(x):
        return lax.dot_general(x.astype(jnp.bfloat16), table, (((1,), (1,)), ((), ())), preferred_element_type=jnp.float32) * (1.0 / length)

    h, m, g = fwd(filt), fwd(mixed_in), fwd(grad_in)
    hc, hs = h[:, :length], h[:, length:]
    mc, ms = m[:, :length], m[:, length:]
    gc, gs = g[:, :length], g[:, length:]
    conv_out = inv(jnp.concatenate([hc * mc - hs * ms, hc * ms + hs * mc], axis=1))
    corr_out = inv(jnp.concatenate([hc * gc + hs * gs, hc * gs - hs * gc], axis=1))
    y_out = (conv_out + skip_part[:, None] * mixed_in.astype(jnp.float32)).astype(jnp.bfloat16)
    dmixed = (corr_out + skip_part[:, None] * grad_in.astype(jnp.float32)).astype(jnp.bfloat16)
    return (y_out, dmixed)


def to_channels(stacked):
    return lax.all_to_all(stacked, "seq", split_axis=1, concat_axis=2, tiled=True)


def to_sequence(stacked):
    return lax.all_to_all(stacked, "seq", split_axis=2, concat_axis=1, tiled=True)


def local_general(features, dout, filters, taps, skip, lengths):
    blocks = lax.axis_size("seq")
    seq_rank = lax.axis_index("seq")
    span_rows = features.shape[2]
    channels_here = features.shape[1]
    chan_part = channels_here // blocks
    count = taps.shape[1]
    margin = count - 1
    rim = shifted(features[:, :, span_rows - margin :], "seq", 1)
    extended = jnp.concatenate([rim, features], axis=2)
    first_pos = seq_rank * span_rows
    offsets = genome_offsets(lengths, first_pos + jnp.arange(span_rows, dtype=jnp.int32))
    filtered = short_forward(extended, taps, offsets).astype(jnp.bfloat16)
    query_side = filtered[0].astype(jnp.float32)
    key_side = filtered[1].astype(jnp.float32)
    value_side = filtered[2].astype(jnp.float32)
    dout_f = dout.astype(jnp.float32)
    mixed = (key_side * value_side).astype(jnp.bfloat16)
    grad_in = (dout_f * query_side).astype(jnp.bfloat16)
    moved = to_channels(jnp.stack([mixed, grad_in, filters]))
    skip_part = lax.dynamic_slice_in_dim(skip, seq_rank * chan_part, chan_part, 0)
    run = dense_filter if moved.shape[2] <= DENSE_MAX else long_filter
    y_out, dmixed = run(moved[2], moved[0], moved[1], skip_part)
    returned = to_sequence(jnp.stack([y_out, dmixed]))
    y_here = returned[0].astype(jnp.float32)
    dmixed_here = returned[1].astype(jnp.float32)
    out = (query_side * y_here).astype(jnp.bfloat16)
    grads = jnp.stack([dout_f * y_here, dmixed_here * value_side, dmixed_here * key_side])
    ahead = shifted(grads[:, :, :margin], "seq", -1)
    grads_ext = jnp.concatenate([grads, ahead], axis=2)
    offsets_ext = genome_offsets(
        lengths, first_pos + jnp.arange(span_rows + margin, dtype=jnp.int32)
    )
    dfeatures = short_backward(grads_ext, taps, offsets_ext).astype(jnp.bfloat16)
    return (out, dfeatures)


CH = 128
BACK = 7
RELAY = 4
HOLD = 3
NN = (((1,), (0,)), ((), ()))
NT = (((1,), (1,)), ((), ()))
TN = (((0,), (0,)), ((), ()))
MESH = pl.DeviceIdType.MESH


def mm(a, b, dims=NN):
    return lax.dot_general(a, b, dims, preferred_element_type=jnp.float32)


def block_tables(size):
    place = np.arange(size, dtype=np.int64)
    phase = place[:, None] * (4 * place[None, :] + 1) % (4 * size)
    angle = phase * (2.0 * np.pi / (4 * size))
    cos, sin = np.cos(angle), np.sin(angle)
    there = np.stack([np.concatenate([cos, s * sin], axis=1) for s in (1, -1)])
    back = np.stack([np.concatenate([cos.T, s * sin.T], axis=0) for s in (1, -1)]) / size
    return there.astype(jnp.bfloat16), back.astype(jnp.bfloat16)


def mixer_kernel(
    lengths_hbm, feat_hbm, dout_hbm, filt_hbm, taps_hbm, skip_hbm, there_hbm, back_hbm,
    out_ref, df_ref,
    lengths_ref, xf, xd, taps_v, skip_v, par, wh, wsig, winv, keep_f, keep_b,
    rim_src, rim, h_all, sig, q_s, k_s, v_s, yd, w_loc, c_src, c_in,
    hal_src, hal, mini_src, mini, mini_own, spec_s, spec_h, prod,
    ld, rim_ss, rim_rs, h_zs, h_ys, h_bs, h_rs, u_ss, u_rs, c_ss, c_rs, hal_ss, hal_rs, mini_ss, mini_rs,
):
    rank = lax.axis_index("seq")
    group = lax.axis_index("groups")
    channels, span = xd.shape
    count = channels // CH
    half = count // 2
    mir = rank // 2
    inn = lax.rem(rank + mir, 2)
    inner = inn == 1
    inward = rank + 1 - 2 * mir
    outward = rank - 1 + 2 * mir
    far = 3 - 3 * mir
    bf = jnp.bfloat16
    f32 = jnp.float32

    loads = [
        pltpu.make_async_copy(feat_hbm, xf, ld.at[0]),
        pltpu.make_async_copy(taps_hbm, taps_v, ld.at[1]),
        pltpu.make_async_copy(skip_hbm, skip_v, ld.at[2]),
        pltpu.make_async_copy(dout_hbm, xd, ld.at[3]),
        pltpu.make_async_copy(filt_hbm, h_all.at[rank], ld.at[4]),
        pltpu.make_async_copy(there_hbm.at[0], wh, ld.at[5]),
        pltpu.make_async_copy(there_hbm.at[mir], wsig, ld.at[6]),
        pltpu.make_async_copy(back_hbm.at[mir], winv, ld.at[7]),
        pltpu.make_async_copy(lengths_hbm, lengths_ref, ld.at[8]),
    ]
    for load in loads:
        load.start()

    def greet(**where):
        pl.semaphore_signal(barrier, inc=1, device_id=where, device_id_type=MESH)

    barrier = pltpu.get_barrier_semaphore()
    greet(seq=inward)

    @pl.when(inner)
    def _():
        greet(seq=outward)

    @pl.when(inn == 0)
    def _():
        greet(seq=2 - mir)

    @pl.when(rank > 0)
    def _():
        greet(groups=1 - group)

    def rows_of(i):
        c = lax.rem(half * group + i, count)
        return c, pl.ds(pl.multiple_of(c * CH, CH), CH)

    def remote(src, dst, ss, rs, where):
        return pltpu.make_async_remote_copy(
            src_ref=src, dst_ref=dst, send_sem=ss, recv_sem=rs, device_id=where, device_id_type=MESH
        )

    def h_own_copy(i):
        c, rows = rows_of(i)
        return remote(filt_hbm.at[rows], h_all.at[rank, rows], h_zs.at[0, i], h_rs.at[rank, c], {"seq": inward})

    def h_on_copy(i):
        c, rows = rows_of(i)
        return remote(h_all.at[outward, rows], h_all.at[outward, rows], h_zs.at[1, i], h_rs.at[outward, c], {"seq": inward})

    def h_back_copy(i):
        c, rows = rows_of(i)
        return remote(h_all.at[0, rows], h_all.at[0, rows], h_bs.at[i], h_rs.at[0, c], {"seq": 3})

    def h_over_copy(which, slot, i):
        c, rows = rows_of(i)
        return remote(
            h_all.at[slot, rows], h_all.at[slot, rows], h_ys.at[which, i], h_rs.at[slot, c], {"groups": 1 - group}
        )

    def h_arrival(slot, i):
        c, rows = rows_of(i)
        return remote(h_all.at[slot, rows], h_all.at[slot, rows], h_zs.at[0, 0], h_rs.at[slot, c], {"seq": inward})

    def u_copy(i):
        c, rows = rows_of(i)
        return remote(sig.at[0, rows], sig.at[2, rows], u_ss.at[i], u_rs.at[c], {"seq": inward})

    def c_copy(which, i):
        c, rows = rows_of(i)
        direct = (i >= RELAY).astype(jnp.int32)
        slot = (0, 1 - direct, 1)[which]
        where = (inward, inward + (far - inward) * direct, outward)[which]
        return remote(
            c_src.at[which, rows], c_in.at[slot, rows], c_ss.at[which, i], c_rs.at[slot, c], {"seq": where}
        )

    def c_arrival(slot, i):
        c, rows = rows_of(i)
        return remote(c_in.at[slot, rows], c_in.at[slot, rows], c_ss.at[0, i], c_rs.at[slot, c], {"seq": inward})

    def mini_copy(i):
        c, _ = rows_of(i)
        where = (2 - 2 * mir) * (i >= RELAY).astype(jnp.int32)
        return remote(mini_src.at[c], mini.at[c], mini_ss.at[i], mini_rs.at[c], {"seq": where})

    def rim_copy():
        return remote(rim_src, rim, rim_ss, rim_rs, {"seq": rank + 1})

    def hal_copy(i):
        c, _ = rows_of(i)
        return remote(hal_src.at[c], hal.at[c], hal_ss.at[i], hal_rs.at[c], {"seq": rank - 1})

    @pl.when(rank == 0)
    def _():
        rim[...] = jnp.zeros_like(rim)

    @pl.when(rank == 3)
    def _():
        hal[...] = jnp.zeros_like(hal)

    @pl.when(lax.rem(rank, 2) == 1)
    def _():
        mini[...] = jnp.zeros_like(mini)

    @pl.when(rank == 2)
    def _():
        for i in range(min(RELAY, count)):
            mini[rows_of(i)[0]] = jnp.zeros((16, CH), bf)

    @pl.when(inn == 0)
    def _():
        mini_own[...] = jnp.zeros_like(mini_own)

    pl.semaphore_wait(barrier, 1 + 3 * inn + rank // 3)

    h_own_copy(0).start()

    loads[0].wait()
    r_id = lax.broadcasted_iota(jnp.int32, (16, 128), 0)
    p_id = lax.broadcasted_iota(jnp.int32, (16, 128), 1)
    total = None
    for part in range(2):
        for a in range(3):
            first = 8 * part + 2 * a
            hit = ((r_id == first) & (p_id == 126)) | ((r_id == first + 1) & (p_id == 127))
            edge = xf[a, part * half * CH : (part + 1) * half * CH, span - 128 :]
            term = mm(jnp.where(hit, 1.0, 0.0).astype(bf), edge, NT)
            total = term if total is None else total + term
    rim_src[...] = total.astype(bf)

    @pl.when(rank < 3)
    def _():
        rim_copy().start()

    for i in range(1, max(half - 1, 1)):
        h_own_copy(i).start()

    @pl.when(inn == 0)
    def _():
        for i in range(max(half - 1, 1), half):
            h_own_copy(i).start()

    loads[8].wait()

    def keeps(ahead, least):
        position = rank * span + ahead + lax.broadcasted_iota(jnp.int32, (8, span), 1)
        offset = position
        end = jnp.int32(0)
        for g in range(lengths_ref.shape[0]):
            one = lengths_ref[g]
            end = end + one
            offset = offset - jnp.where(end <= position, one, 0)
        return jnp.where(offset >= least, 1.0, 0.0)

    for j in (1, 2):
        keep_f[j - 1] = keeps(0, j)
        keep_b[j - 1] = keeps(j, j)

    loads[1].wait()
    loads[2].wait()
    flat = jnp.concatenate(
        [taps_v[0], taps_v[1], taps_v[2], skip_v[...], jnp.zeros((6, channels), f32)], axis=0
    )
    for c in range(count):
        par[c * CH : (c + 1) * CH, 0:16] = flat[:, c * CH : (c + 1) * CH].T
    for load in loads[3:8]:
        load.wait()

    def pass_on(i):
        h_arrival(outward, i).wait_recv()
        h_on_copy(i).start()
        h_over_copy(0, outward, i).start()

    @pl.when(inner)
    def _():
        for i in range(min(2, half)):
            pass_on(i)
            if i == 0:
                for k in range(max(half - 1, 1), half):
                    h_own_copy(k).start()

    @pl.when(rank > 0)
    def _():
        rim_copy().wait_recv()

    rr = lax.broadcasted_iota(jnp.int32, (16, 384), 0)
    cc = lax.broadcasted_iota(jnp.int32, (16, 384), 1)

    def spread(first, above=0):
        hit = None
        for a in range(3):
            row = 2 * a + above
            one = ((rr == row) & (cc == 128 * a + first)) | ((rr == row + 1) & (cc == 128 * a + first + 1))
            hit = one if hit is None else hit | one
        return jnp.where(hit, 1.0, 0.0).astype(bf)

    def prepare(i):
        c, rows = rows_of(i)
        upper = c // half
        cols = pl.ds(pl.multiple_of((c - half * upper) * CH, CH), CH)
        edge = mm(rim[:, cols], spread(126, 8 * upper), TN)
        tap = par[rows, :]
        result = []
        for a in range(3):
            here = xf[a, rows, :].astype(f32)
            wide = jnp.concatenate([edge[:, 128 * a : 128 * a + 128], here], axis=1)
            acc = tap[:, 3 * a : 3 * a + 1] * here
            for j in (1, 2):
                moved = pltpu.roll(wide, j, 1)[:, 128:]
                acc = acc + tap[:, 3 * a + j : 3 * a + j + 1] * (moved * keep_f[j - 1, 0:1, :])
            result.append(acc.astype(bf))
        q, k, v = result
        q_s[rows, :] = q
        k_s[rows, :] = k
        v_s[rows, :] = v
        sig[mir, rows, :] = (k.astype(f32) * v.astype(f32)).astype(bf)
        sig[1 - mir, rows, :] = (xd[rows, :].astype(f32) * q.astype(f32)).astype(bf)

        @pl.when(inn == 0)
        def _():
            u_copy(i).start()

        @pl.when(inner & (i + 2 < half))
        def _():
            pass_on(i + 2)

    def pick(block, rows_at):
        hit = None
        for first, lane in rows_at:
            one = ((r_id == first) & (p_id == lane)) | ((r_id == first + 1) & (p_id == lane + 1))
            hit = one if hit is None else hit | one
        return mm(jnp.where(hit, 1.0, 0.0).astype(bf), block, NT)

    def keep_local(rows, value):
        skip = par[rows, 9:10]
        yd[0, rows, :] = (value[0:CH] + skip * sig[0, rows, :].astype(f32)).astype(bf)
        other = value[CH : 2 * CH] + skip * sig[1, rows, :].astype(f32)
        w_loc[rows, :] = other
        yd[1, rows, :] = other.astype(bf)

    def products(terms_of):
        def block(b, carry):
            first = pl.multiple_of(b * 16, 16)

            def pair(ref, k):
                at = pl.ds(k * CH + first, 16)
                return ref[at, 0:span], ref[at, span:]

            for k, terms in enumerate(terms_of(lambda n: pair(spec_h, n), lambda n: pair(spec_s, n))):
                re = im = None
                for (tc, ts), (xc, xs), sign in terms:
                    if sign > 0:
                        new_re, new_im = tc * xc - ts * xs, tc * xs + ts * xc
                    else:
                        new_re, new_im = tc * xc + ts * xs, tc * xs - ts * xc
                    re = new_re if re is None else re + new_re
                    im = new_im if im is None else im + new_im
                at = pl.ds(k * CH + first, 16)
                prod[at, 0:span] = re.astype(bf)
                prod[at, span:] = im.astype(bf)
            return carry

        lax.fori_loop(0, CH // 16, block, 0, unroll=8)

    def inner_terms(h, s):
        hs = [h(k) for k in range(4)]
        t = [hs[0]] + [(hs[k][0] + hs[k - 1][1], hs[k][1] - hs[k - 1][0]) for k in (1, 2, 3)]
        own, other, near = [s(k) for k in range(3)]
        return [
            [(t[0], own, 1), (t[1], near, 1)],
            [(t[0], other, -1)],
            [(t[1], own, 1), (t[2], near, 1)],
            [(t[2], own, 1), (t[3], near, 1)],
            [(t[1], other, -1)],
        ]

    def outer_terms(h, s):
        return [[(h(0), s(0), 1)], [(h(0), s(1), -1)]]

    def main_inner(i):
        c, rows = rows_of(i)

        @pl.when(i < half)
        def _():
            h_arrival(inward, i).wait_recv()
            h_over_copy(1, inward, i).start()
            h_arrival(far, i).wait_recv()
            h_over_copy(2, far, i).start()

            @pl.when(rank == 2)
            def _():
                h_back_copy(i).start()

        @pl.when(i >= half)
        def _():
            h_arrival(outward, i).wait_recv()
            h_arrival(inward, i).wait_recv()
            h_arrival(far, i).wait_recv()

        u_copy(i).wait_recv()
        spec_h[...] = mm(h_all[:, rows, :].reshape(4 * CH, span), wh[...])
        spec_s[...] = mm(sig[:, rows, :].reshape(3 * CH, span), wsig[...])
        products(inner_terms)
        value = mm(prod[...], winv[...])
        for which in range(3):
            c_src[which, rows, :] = value[(2 + which) * CH : (3 + which) * CH].astype(bf)

        @pl.when(i >= RELAY)
        def _():
            mini_src[c] = pick(c_src[1 - mir, rows, 0:128], [(8 - 6 * mir, 0), (8 - 4 * mir, 0)]).astype(bf)
            mini_copy(i).start()

        c_copy(1, i).start()

        c_copy(0, i).start()

        @pl.when(i >= RELAY)
        def _():
            c_copy(2, i).start()

        @pl.when((rank == 1) | (i >= RELAY))
        def _():
            mini_own[c] = pick(c_src[2 * mir, rows, 0:128], [(8, 0)]).astype(bf)

        keep_local(rows, value)

    def relay(i):
        c, rows = rows_of(i)
        c_arrival(1, i).wait_recv()
        c_src[2, rows, :] = (c_src[2, rows, :].astype(f32) + c_in[1, rows, :].astype(f32)).astype(bf)
        c_copy(2, i).start()
        c_arrival(0, i).wait_recv()

        @pl.when(rank == 1)
        def _():
            mini_src[c] = pick(c_in[0, rows, 0:128], [(2, 0), (4, 0)]).astype(bf)
            mini_copy(i).start()

        @pl.when(rank == 2)
        def _():
            mini_own[c] = pick(c_src[2, rows, 0:128], [(8, 0)]).astype(bf)

    def main_outer(i):
        c, rows = rows_of(i)

        @pl.when(rank == 3)
        def _():
            h_arrival(0, i).wait_recv()

            @pl.when(i < half)
            def _():
                h_over_copy(0, 0, i).start()

        spec_h[0:CH] = mm(h_all[0, rows, :], wh[...])
        spec_s[0 : 2 * CH] = mm(sig[0:2, rows, :].reshape(2 * CH, span), wsig[...])
        products(outer_terms)
        keep_local(rows, mm(prod[0 : 2 * CH], winv[...]))

    def grads_of(rows, lanes):
        y = yd[mir, rows, lanes].astype(f32)
        dm = yd[1 - mir, rows, lanes].astype(f32)
        return [
            xd[rows, lanes].astype(f32) * y,
            dm * v_s[rows, lanes].astype(f32),
            dm * k_s[rows, lanes].astype(f32),
        ]

    def halo(i):
        c, rows = rows_of(i)
        first = slice(0, 128)
        edge = pick(xd[rows, first], [(0, 0)]) + pick(yd[1 - mir, rows, first], [(2, 0), (4, 0)])
        edge = edge + pick(yd[mir, rows, first], [(8, 0)])
        edge = edge + pick(v_s[rows, first], [(10, 0)]) + pick(k_s[rows, first], [(12, 0)])
        hal_src[c] = edge.astype(bf)
        hal_copy(i).start()

    def finish(i):
        c, rows = rows_of(i)

        @pl.when(i >= RELAY)
        def _():
            c_arrival(0, i).wait_recv()

        @pl.when(inner)
        def _():
            yd[1, rows, :] = (w_loc[rows, :] + c_in[0, rows, :].astype(f32)).astype(bf)

        @pl.when((inn == 0) & (i >= RELAY))
        def _():
            c_arrival(1, i).wait_recv()
            cross = c_in[0, rows, :].astype(f32) + c_in[1, rows, :].astype(f32)
            yd[1, rows, :] = (w_loc[rows, :] + cross).astype(bf)

        @pl.when((inn == 0) & (i < RELAY))
        def _():
            c_arrival(1, i).wait_recv()
            yd[1, rows, :] = (w_loc[rows, :] + c_in[1, rows, :].astype(f32)).astype(bf)

        @pl.when(rank < 3)
        def _():
            hal_copy(i).wait_recv()

        @pl.when((rank == 0) | ((rank == 2) & (i >= RELAY)))
        def _():
            mini_copy(i).wait_recv()

        both = hal[c].astype(f32) + mini[c].astype(f32) + mini_own[c].astype(f32)
        first_grads = jnp.concatenate([both[0:8] * both[8:16], jnp.zeros((8, CH), f32)], axis=0)
        tap = par[rows, :]
        edge = mm(first_grads.astype(bf), spread(0), TN)
        y = yd[mir, rows, :].astype(f32)
        out_ref[rows, :] = (q_s[rows, :].astype(f32) * y).astype(bf)
        for a, grad in enumerate(grads_of(rows, slice(None))):
            wide = jnp.concatenate([grad, edge[:, 128 * a : 128 * a + 128]], axis=1)
            acc = tap[:, 3 * a : 3 * a + 1] * grad
            for j in (1, 2):
                moved = pltpu.roll(wide, span + 128 - j, 1)[:, :span]
                acc = acc + tap[:, 3 * a + j : 3 * a + j + 1] * (moved * keep_b[j - 1, 0:1, :])
            df_ref[a, rows, :] = acc.astype(bf)

    def first_steps(s, carry):
        prepare(s)
        return carry

    lax.fori_loop(0, count, first_steps, 0)

    def step(s, carry):
        main = s < count

        @pl.when(inner & main)
        def _():
            main_inner(s)

        @pl.when((inn == 0) & main)
        def _():
            main_outer(s)

        @pl.when((rank > 0) & main)
        def _():
            halo(s)

        @pl.when(inner & (s >= HOLD) & (s < RELAY + HOLD) & (s < count + HOLD))
        def _():
            relay(s - HOLD)

        @pl.when(s >= BACK)
        def _():
            finish(s - BACK)

        return carry

    lax.fori_loop(0, count + BACK, step, 0)

    @pl.when(rank < 3)
    def _():
        rim_copy().wait_send()

    def drain(i, carry):
        @pl.when(inn == 0)
        def _():
            u_copy(i).wait_send()

        @pl.when(rank > 0)
        def _():
            hal_copy(i).wait_send()

        @pl.when(inner)
        def _():
            for which in range(3):
                c_copy(which, i).wait_send()

        @pl.when((rank == 1) | ((rank == 2) & (i >= RELAY)))
        def _():
            mini_copy(i).wait_send()

        @pl.when(i < half)
        def _():
            h_own_copy(i).wait_send()

            @pl.when(inner)
            def _():
                h_on_copy(i).wait_send()
                h_over_copy(0, outward, i).wait_send()
                h_over_copy(1, inward, i).wait_send()
                h_over_copy(2, far, i).wait_send()

            @pl.when(rank == 2)
            def _():
                h_back_copy(i).wait_send()

            @pl.when(rank == 3)
            def _():
                h_over_copy(0, 0, i).wait_send()

        return carry

    lax.fori_loop(0, count, drain, 0)


def local_kernel(features, dout, filters, taps, skip, lengths):
    channels, span = dout.shape
    count = channels // CH
    bf = jnp.bfloat16
    f32 = jnp.float32
    there, back = block_tables(span)
    operands = [lengths, features, dout, filters, taps, skip[None], jnp.asarray(there), jnp.asarray(back)]
    vmem = pl.BlockSpec(memory_space=pltpu.VMEM)
    hbm = pl.BlockSpec(memory_space=pltpu.HBM)
    dma = pltpu.SemaphoreType.DMA
    return pl.pallas_call(
        mixer_kernel,
        out_shape=(pltpu.VMEM(dout.shape, bf), pltpu.VMEM(features.shape, bf)),
        in_specs=[hbm] * 8,
        out_specs=(vmem, vmem),
        scratch_shapes=[
            pltpu.SMEM(lengths.shape, jnp.int32),
            pltpu.VMEM((3, channels, span), bf),
            pltpu.VMEM((channels, span), bf),
            pltpu.VMEM((3, 3, channels), f32),
            pltpu.VMEM((1, channels), f32),
            pltpu.VMEM((channels, 128), f32),
            pltpu.VMEM((span, 2 * span), bf),
            pltpu.VMEM((span, 2 * span), bf),
            pltpu.VMEM((2 * span, span), bf),
            pltpu.VMEM((2, 8, span), f32),
            pltpu.VMEM((2, 8, span), f32),
            pltpu.VMEM((16, channels // 2), bf),
            pltpu.VMEM((16, channels // 2), bf),
            pltpu.VMEM((4, channels, span), bf),
            pltpu.VMEM((3, channels, span), bf),
            pltpu.VMEM((channels, span), bf),
            pltpu.VMEM((channels, span), bf),
            pltpu.VMEM((channels, span), bf),
            pltpu.VMEM((2, channels, span), bf),
            pltpu.VMEM((channels, span), f32),
            pltpu.VMEM((3, channels, span), bf),
            pltpu.VMEM((2, channels, span), bf),
            pltpu.VMEM((count, 16, CH), bf),
            pltpu.VMEM((count, 16, CH), bf),
            pltpu.VMEM((count, 16, CH), bf),
            pltpu.VMEM((count, 16, CH), bf),
            pltpu.VMEM((count, 16, CH), bf),
            pltpu.VMEM((3 * CH, 2 * span), f32),
            pltpu.VMEM((4 * CH, 2 * span), f32),
            pltpu.VMEM((5 * CH, 2 * span), bf),
            dma((9,)), dma, dma,
            dma((2, count)), dma((3, count)), dma((count,)), dma((4, count)),
            dma((count,)), dma((count,)), dma((3, count)), dma((2, count)),
            dma((count,)), dma((count,)), dma((count,)), dma((count,)),
        ],
        compiler_params=pltpu.CompilerParams(
            collective_id=0, has_side_effects=True, vmem_limit_bytes=32 * 1024 * 1024
        ),
    )(*[pltpu.with_memory_space_constraint(x, pltpu.HBM) for x in operands])


def local(features, dout, filters, taps, skip, lengths):
    channels, span = dout.shape
    fits = lax.axis_size("seq") == 4 and lax.axis_size("groups") == 2 and taps.shape[:2] == (3, 3)
    if fits and span == 256 and channels % (2 * CH) == 0:
        return local_kernel(features, dout, filters, taps, skip, lengths)
    return local_general(features, dout, filters, taps, skip, lengths)


def solution(mesh):
    in_specs = (
        P(None, ("chan", "sub"), ("groups", "seq")),
        P(("chan", "sub"), ("groups", "seq")),
        P(("chan", "sub"), "seq"),
        P(None, None, ("chan", "sub")),
        P(("chan", "sub")),
        P("groups"),
    )
    out_specs = (P(("chan", "sub"), ("groups", "seq")), P(None, ("chan", "sub"), ("groups", "seq")))
    return jax.shard_map(local, mesh=mesh, in_specs=in_specs, out_specs=out_specs, check_vma=False)
```

```python
import functools

import jax
import numpy as np
import jax.numpy as jnp
from jax import lax
from jax.experimental import pallas as pl
from jax.experimental.pallas import tpu as pltpu
from jax.sharding import PartitionSpec as P

HIGHEST = lax.Precision.HIGHEST
TWO_PI = 6.283185307179586


def shifted(value, axis, steps):
    count = lax.axis_size(axis)
    leading, last = (max(0, -steps), min(count, count - steps))
    return lax.ppermute(value, axis, [(source, source + steps) for source in range(leading, last)])


def genome_offsets(lengths, positions):
    order = jnp.arange(lengths.shape[0], dtype=jnp.int32)
    so_far = (order[None, :] <= order[:, None]).astype(jnp.int32)
    ends_at = jnp.sum(so_far * lengths[None, :], axis=1, dtype=jnp.int32)
    before = (ends_at[None, :] <= positions[:, None]).astype(jnp.int32)
    return positions - jnp.sum(before * lengths[None, :], axis=1, dtype=jnp.int32)


def short_forward(extended, taps_local, offsets):
    span_rows = offsets.shape[0]
    count = taps_local.shape[1]
    result = jnp.zeros(extended.shape[:2] + (span_rows,), jnp.float32)
    for tap_index in range(count):
        begin = count - 1 - tap_index
        window = extended[:, :, begin : begin + span_rows].astype(jnp.float32)
        keep_mask = (offsets >= tap_index).astype(jnp.float32)
        result = result + taps_local[:, tap_index, :, None] * window * keep_mask[None, None, :]
    return result


def short_backward(grads_ext, taps_local, offsets_ext):
    count = taps_local.shape[1]
    span_rows = offsets_ext.shape[0] - (count - 1)
    result = jnp.zeros(grads_ext.shape[:2] + (span_rows,), jnp.float32)
    for tap_index in range(count):
        window = grads_ext[:, :, tap_index : tap_index + span_rows]
        keep_mask = (offsets_ext[tap_index : tap_index + span_rows] >= tap_index).astype(
            jnp.float32
        )
        result = result + taps_local[:, tap_index, :, None] * window * keep_mask[None, None, :]
    return result


def dft_table(rows_n, cols_n, period):
    row_ids = jnp.arange(rows_n, dtype=jnp.int32)
    col_ids = jnp.arange(cols_n, dtype=jnp.int32)
    phase = row_ids[:, None] * col_ids[None, :] % period
    angles = phase.astype(jnp.float32) * (-TWO_PI / period)
    return (jnp.cos(angles), jnp.sin(angles))


def forward_transform(signal, tables):
    (row_re, row_im), (twid_re, twid_im), (col_re, col_im) = tables
    half_rows = signal.shape[1] // 128
    blocks_in = signal.reshape(signal.shape[0], half_rows, 128)
    part_re = jnp.einsum("kn,cnm->ckm", row_re[:, :half_rows], blocks_in, precision=HIGHEST)
    part_im = jnp.einsum("kn,cnm->ckm", row_im[:, :half_rows], blocks_in, precision=HIGHEST)
    turned_re = part_re * twid_re - part_im * twid_im
    turned_im = part_re * twid_im + part_im * twid_re
    spec_re = jnp.einsum("ckn,nm->ckm", turned_re, col_re, precision=HIGHEST) - jnp.einsum(
        "ckn,nm->ckm", turned_im, col_im, precision=HIGHEST
    )
    spec_im = jnp.einsum("ckn,nm->ckm", turned_re, col_im, precision=HIGHEST) + jnp.einsum(
        "ckn,nm->ckm", turned_im, col_re, precision=HIGHEST
    )
    return (spec_re, spec_im)


def inverse_transform(spec_re, spec_im, tables):
    (row_re, row_im), (twid_re, twid_im), (col_re, col_im) = tables
    rows_n = spec_re.shape[1]
    half_rows = rows_n // 2
    mid_re = jnp.einsum("ckn,nm->ckm", spec_re, col_re, precision=HIGHEST) + jnp.einsum(
        "ckn,nm->ckm", spec_im, col_im, precision=HIGHEST
    )
    mid_im = jnp.einsum("ckn,nm->ckm", spec_im, col_re, precision=HIGHEST) - jnp.einsum(
        "ckn,nm->ckm", spec_re, col_im, precision=HIGHEST
    )
    back_re = mid_re * twid_re + mid_im * twid_im
    back_im = mid_im * twid_re - mid_re * twid_im
    signal = jnp.einsum("nk,ckm->cnm", row_re[:half_rows], back_re, precision=HIGHEST) + jnp.einsum(
        "nk,ckm->cnm", row_im[:half_rows], back_im, precision=HIGHEST
    )
    return signal.reshape(signal.shape[0], half_rows * 128) * (1.0 / (rows_n * 128))


def long_filter(filt, mixed_in, grad_in, skip_part):
    rows_n = 2 * mixed_in.shape[1] // 128
    tables = (
        dft_table(rows_n, rows_n, rows_n),
        dft_table(rows_n, 128, rows_n * 128),
        dft_table(128, 128, 128),
    )
    mixed_f = mixed_in.astype(jnp.float32)
    grad_f = grad_in.astype(jnp.float32)
    filt_re, filt_im = forward_transform(filt.astype(jnp.float32), tables)
    mix_re, mix_im = forward_transform(mixed_f, tables)
    grad_re, grad_im = forward_transform(grad_f, tables)
    conv_out = inverse_transform(
        filt_re * mix_re - filt_im * mix_im, filt_re * mix_im + filt_im * mix_re, tables
    )
    corr_out = inverse_transform(
        filt_re * grad_re + filt_im * grad_im, filt_re * grad_im - filt_im * grad_re, tables
    )
    y_out = (conv_out + skip_part[:, None] * mixed_f).astype(jnp.bfloat16)
    dmixed = (corr_out + skip_part[:, None] * grad_f).astype(jnp.bfloat16)
    return (y_out, dmixed)


DENSE_MAX = 1024
FINE = 32


def angle_parts(length):
    base = np.arange(length, dtype=np.int64) * 4 + 1
    fine = np.arange(FINE, dtype=np.int64)[:, None] * base[None, :] % (4 * length)
    coarse = np.arange(0, length, FINE, dtype=np.int64)[:, None] * base[None, :] % (4 * length)
    scale = 2.0 * np.pi / (4 * length)
    return [
        func(part * scale).astype(np.float32)
        for part in (coarse, fine)
        for func in (np.cos, np.sin)
    ]


def dense_filter(filt, mixed_in, grad_in, skip_part):
    length = mixed_in.shape[1]
    cc, cs, fc, fs = [jnp.asarray(p)[:, None] if i < 2 else jnp.asarray(p)[None] for i, p in enumerate(angle_parts(length))]
    cos_t = (cc * fc - cs * fs).reshape(length, length)
    sin_t = (cs * fc + cc * fs).reshape(length, length)
    table = jnp.concatenate([cos_t, sin_t], axis=1).astype(jnp.bfloat16)

    def fwd(x):
        return jnp.dot(x, table, preferred_element_type=jnp.float32)

    def inv(x):
        return lax.dot_general(x.astype(jnp.bfloat16), table, (((1,), (1,)), ((), ())), preferred_element_type=jnp.float32) * (1.0 / length)

    h, m, g = fwd(filt), fwd(mixed_in), fwd(grad_in)
    hc, hs = h[:, :length], h[:, length:]
    mc, ms = m[:, :length], m[:, length:]
    gc, gs = g[:, :length], g[:, length:]
    conv_out = inv(jnp.concatenate([hc * mc - hs * ms, hc * ms + hs * mc], axis=1))
    corr_out = inv(jnp.concatenate([hc * gc + hs * gs, hc * gs - hs * gc], axis=1))
    y_out = (conv_out + skip_part[:, None] * mixed_in.astype(jnp.float32)).astype(jnp.bfloat16)
    dmixed = (corr_out + skip_part[:, None] * grad_in.astype(jnp.float32)).astype(jnp.bfloat16)
    return (y_out, dmixed)


def to_channels(stacked):
    return lax.all_to_all(stacked, "seq", split_axis=1, concat_axis=2, tiled=True)


def to_sequence(stacked):
    return lax.all_to_all(stacked, "seq", split_axis=2, concat_axis=1, tiled=True)


def local_general(features, dout, filters, taps, skip, lengths):
    blocks = lax.axis_size("seq")
    seq_rank = lax.axis_index("seq")
    span_rows = features.shape[2]
    channels_here = features.shape[1]
    chan_part = channels_here // blocks
    count = taps.shape[1]
    margin = count - 1
    rim = shifted(features[:, :, span_rows - margin :], "seq", 1)
    extended = jnp.concatenate([rim, features], axis=2)
    first_pos = seq_rank * span_rows
    offsets = genome_offsets(lengths, first_pos + jnp.arange(span_rows, dtype=jnp.int32))
    filtered = short_forward(extended, taps, offsets).astype(jnp.bfloat16)
    query_side = filtered[0].astype(jnp.float32)
    key_side = filtered[1].astype(jnp.float32)
    value_side = filtered[2].astype(jnp.float32)
    dout_f = dout.astype(jnp.float32)
    mixed = (key_side * value_side).astype(jnp.bfloat16)
    grad_in = (dout_f * query_side).astype(jnp.bfloat16)
    moved = to_channels(jnp.stack([mixed, grad_in, filters]))
    skip_part = lax.dynamic_slice_in_dim(skip, seq_rank * chan_part, chan_part, 0)
    run = dense_filter if moved.shape[2] <= DENSE_MAX else long_filter
    y_out, dmixed = run(moved[2], moved[0], moved[1], skip_part)
    returned = to_sequence(jnp.stack([y_out, dmixed]))
    y_here = returned[0].astype(jnp.float32)
    dmixed_here = returned[1].astype(jnp.float32)
    out = (query_side * y_here).astype(jnp.bfloat16)
    grads = jnp.stack([dout_f * y_here, dmixed_here * value_side, dmixed_here * key_side])
    ahead = shifted(grads[:, :, :margin], "seq", -1)
    grads_ext = jnp.concatenate([grads, ahead], axis=2)
    offsets_ext = genome_offsets(
        lengths, first_pos + jnp.arange(span_rows + margin, dtype=jnp.int32)
    )
    dfeatures = short_backward(grads_ext, taps, offsets_ext).astype(jnp.bfloat16)
    return (out, dfeatures)


CH = 128
BACK = 1
RELAY = 5
HOLD = 4
NN = (((1,), (0,)), ((), ()))
NT = (((1,), (1,)), ((), ()))
TN = (((0,), (0,)), ((), ()))
MESH = pl.DeviceIdType.MESH


def mm(a, b, dims=NN):
    return lax.dot_general(a, b, dims, preferred_element_type=jnp.float32)


def block_tables(size):
    place = np.arange(size, dtype=np.int64)
    phase = place[:, None] * (4 * place[None, :] + 1) % (4 * size)
    angle = phase * (2.0 * np.pi / (4 * size))
    cos, sin = np.cos(angle), np.sin(angle)
    there = np.stack([np.concatenate([cos, s * sin], axis=1) for s in (1, -1)])
    back = np.stack([np.concatenate([cos.T, s * sin.T], axis=0) for s in (1, -1)]) / size
    return there.astype(jnp.bfloat16), back.astype(jnp.bfloat16)


def mixer_kernel(
    lengths_hbm, feat_hbm, dout_hbm, filt_hbm, taps_hbm, skip_hbm, there_hbm, back_hbm,
    out_ref, df_ref,
    lengths_ref, xf, xd, taps_v, skip_v, par, wh, wsig, winv, keep_f, keep_b,
    rim_src, rim, h_all, sig, q_s, k_s, v_s, yd, w_loc, c_src, c_in,
    hal_src, hal, mini_src, mini, mini_own, spec_s, spec_h, prod,
    ld, rim_ss, rim_rs, h_zs, h_ys, h_bs, h_rs, u_ss, u_rs, c_ss, c_rs, hal_ss, hal_rs, mini_ss, mini_rs,
):
    rank = lax.axis_index("seq")
    group = lax.axis_index("groups")
    channels, span = xd.shape
    count = channels // CH
    half = count // 2
    mir = rank // 2
    inn = lax.rem(rank + mir, 2)
    inner = inn == 1
    inward = rank + 1 - 2 * mir
    outward = rank - 1 + 2 * mir
    far = 3 - 3 * mir
    bf = jnp.bfloat16
    f32 = jnp.float32

    loads = [
        pltpu.make_async_copy(feat_hbm, xf, ld.at[0]),
        pltpu.make_async_copy(taps_hbm, taps_v, ld.at[1]),
        pltpu.make_async_copy(skip_hbm, skip_v, ld.at[2]),
        pltpu.make_async_copy(dout_hbm, xd, ld.at[3]),
        pltpu.make_async_copy(filt_hbm, h_all.at[rank], ld.at[4]),
        pltpu.make_async_copy(there_hbm.at[0], wh, ld.at[5]),
        pltpu.make_async_copy(there_hbm.at[mir], wsig, ld.at[6]),
        pltpu.make_async_copy(back_hbm.at[mir], winv, ld.at[7]),
        pltpu.make_async_copy(lengths_hbm, lengths_ref, ld.at[8]),
    ]
    for load in loads:
        load.start()

    def greet(**where):
        pl.semaphore_signal(barrier, inc=1, device_id=where, device_id_type=MESH)

    barrier = pltpu.get_barrier_semaphore()
    greet(seq=inward)

    @pl.when(inner)
    def _():
        greet(seq=outward)

    @pl.when(inn == 0)
    def _():
        greet(seq=2 - mir)

    @pl.when(rank > 0)
    def _():
        greet(groups=1 - group)

    def rows_of(i):
        c = lax.rem(half * group + i, count)
        return c, pl.ds(pl.multiple_of(c * CH, CH), CH)

    def remote(src, dst, ss, rs, where):
        return pltpu.make_async_remote_copy(
            src_ref=src, dst_ref=dst, send_sem=ss, recv_sem=rs, device_id=where, device_id_type=MESH
        )

    def h_own_copy(i):
        c, rows = rows_of(i)
        return remote(filt_hbm.at[rows], h_all.at[rank, rows], h_zs.at[0, i], h_rs.at[rank, c], {"seq": inward})

    def h_on_copy(i):
        c, rows = rows_of(i)
        return remote(h_all.at[outward, rows], h_all.at[outward, rows], h_zs.at[1, i], h_rs.at[outward, c], {"seq": inward})

    def h_back_copy(i):
        c, rows = rows_of(i)
        return remote(h_all.at[0, rows], h_all.at[0, rows], h_bs.at[i], h_rs.at[0, c], {"seq": 3})

    def h_over_copy(which, slot, i):
        c, rows = rows_of(i)
        return remote(
            h_all.at[slot, rows], h_all.at[slot, rows], h_ys.at[which, i], h_rs.at[slot, c], {"groups": 1 - group}
        )

    def h_arrival(slot, i):
        c, rows = rows_of(i)
        return remote(h_all.at[slot, rows], h_all.at[slot, rows], h_zs.at[0, 0], h_rs.at[slot, c], {"seq": inward})

    def u_copy(i):
        c, rows = rows_of(i)
        return remote(sig.at[0, rows], sig.at[2, rows], u_ss.at[i], u_rs.at[c], {"seq": inward})

    def c_copy(which, i):
        c, rows = rows_of(i)
        direct = (i >= RELAY).astype(jnp.int32)
        slot = (0, 1 - direct, 1)[which]
        where = (inward, inward + (far - inward) * direct, outward)[which]
        return remote(
            c_src.at[which, rows], c_in.at[slot, rows], c_ss.at[which, i], c_rs.at[slot, c], {"seq": where}
        )

    def c_arrival(slot, i):
        c, rows = rows_of(i)
        return remote(c_in.at[slot, rows], c_in.at[slot, rows], c_ss.at[0, i], c_rs.at[slot, c], {"seq": inward})

    def mini_copy(i):
        c, _ = rows_of(i)
        where = (2 - 2 * mir) * (i >= RELAY).astype(jnp.int32)
        return remote(mini_src.at[c], mini.at[c], mini_ss.at[i], mini_rs.at[c], {"seq": where})

    def rim_copy():
        return remote(rim_src, rim, rim_ss, rim_rs, {"seq": rank + 1})

    def hal_copy(i):
        c, _ = rows_of(i)
        return remote(hal_src.at[c], hal.at[c], hal_ss.at[i], hal_rs.at[c], {"seq": rank - 1})

    @pl.when(rank == 0)
    def _():
        rim[...] = jnp.zeros_like(rim)

    @pl.when(rank == 3)
    def _():
        hal[...] = jnp.zeros_like(hal)

    @pl.when(lax.rem(rank, 2) == 1)
    def _():
        mini[...] = jnp.zeros_like(mini)

    @pl.when(rank == 2)
    def _():
        for i in range(min(RELAY, count)):
            mini[rows_of(i)[0]] = jnp.zeros((16, CH), bf)

    @pl.when(inn == 0)
    def _():
        mini_own[...] = jnp.zeros_like(mini_own)

    pl.semaphore_wait(barrier, 1 + 3 * inn + rank // 3)

    h_own_copy(0).start()

    loads[0].wait()
    r_id = lax.broadcasted_iota(jnp.int32, (16, 128), 0)
    p_id = lax.broadcasted_iota(jnp.int32, (16, 128), 1)
    total = None
    for part in range(2):
        for a in range(3):
            first = 8 * part + 2 * a
            hit = ((r_id == first) & (p_id == 126)) | ((r_id == first + 1) & (p_id == 127))
            edge = xf[a, part * half * CH : (part + 1) * half * CH, span - 128 :]
            term = mm(jnp.where(hit, 1.0, 0.0).astype(bf), edge, NT)
            total = term if total is None else total + term
    rim_src[...] = total.astype(bf)

    @pl.when(rank < 3)
    def _():
        rim_copy().start()

    for i in range(1, max(half - 1, 1)):
        h_own_copy(i).start()

    @pl.when(inn == 0)
    def _():
        for i in range(max(half - 1, 1), half):
            h_own_copy(i).start()

    loads[8].wait()

    def keeps(ahead, least):
        position = rank * span + ahead + lax.broadcasted_iota(jnp.int32, (8, span), 1)
        offset = position
        end = jnp.int32(0)
        for g in range(lengths_ref.shape[0]):
            one = lengths_ref[g]
            end = end + one
            offset = offset - jnp.where(end <= position, one, 0)
        return jnp.where(offset >= least, 1.0, 0.0)

    for j in (1, 2):
        keep_f[j - 1] = keeps(0, j)
        keep_b[j - 1] = keeps(j, j)

    loads[1].wait()
    loads[2].wait()
    flat = jnp.concatenate(
        [taps_v[0], taps_v[1], taps_v[2], skip_v[...], jnp.zeros((6, channels), f32)], axis=0
    )
    for c in range(count):
        par[c * CH : (c + 1) * CH, 0:16] = flat[:, c * CH : (c + 1) * CH].T
    for load in loads[3:8]:
        load.wait()

    def pass_on(i):
        h_arrival(outward, i).wait_recv()
        h_on_copy(i).start()
        h_over_copy(0, outward, i).start()

    @pl.when(inner)
    def _():
        for i in range(min(2, half)):
            pass_on(i)
            if i == 0:
                for k in range(max(half - 1, 1), half):
                    h_own_copy(k).start()

    @pl.when(rank > 0)
    def _():
        rim_copy().wait_recv()

    rr = lax.broadcasted_iota(jnp.int32, (16, 384), 0)
    cc = lax.broadcasted_iota(jnp.int32, (16, 384), 1)

    def spread(first, above=0):
        hit = None
        for a in range(3):
            row = 2 * a + above
            one = ((rr == row) & (cc == 128 * a + first)) | ((rr == row + 1) & (cc == 128 * a + first + 1))
            hit = one if hit is None else hit | one
        return jnp.where(hit, 1.0, 0.0).astype(bf)

    def prepare(i):
        c, rows = rows_of(i)
        upper = c // half
        cols = pl.ds(pl.multiple_of((c - half * upper) * CH, CH), CH)
        edge = mm(rim[:, cols], spread(126, 8 * upper), TN)
        tap = par[rows, :]
        result = []
        for a in range(3):
            here = xf[a, rows, :].astype(f32)
            wide = jnp.concatenate([edge[:, 128 * a : 128 * a + 128], here], axis=1)
            acc = tap[:, 3 * a : 3 * a + 1] * here
            for j in (1, 2):
                moved = pltpu.roll(wide, j, 1)[:, 128:]
                acc = acc + tap[:, 3 * a + j : 3 * a + j + 1] * (moved * keep_f[j - 1, 0:1, :])
            result.append(acc.astype(bf))
        q, k, v = result
        q_s[rows, :] = q
        k_s[rows, :] = k
        v_s[rows, :] = v
        sig[mir, rows, :] = (k.astype(f32) * v.astype(f32)).astype(bf)
        sig[1 - mir, rows, :] = (xd[rows, :].astype(f32) * q.astype(f32)).astype(bf)

        @pl.when(inn == 0)
        def _():
            u_copy(i).start()

        @pl.when(inner & (i + 2 < half))
        def _():
            pass_on(i + 2)

    def pick(block, rows_at):
        hit = None
        for first, lane in rows_at:
            one = ((r_id == first) & (p_id == lane)) | ((r_id == first + 1) & (p_id == lane + 1))
            hit = one if hit is None else hit | one
        return mm(jnp.where(hit, 1.0, 0.0).astype(bf), block, NT)

    def keep_local(rows, value):
        skip = par[rows, 9:10]
        yd[0, rows, :] = (value[0:CH] + skip * sig[0, rows, :].astype(f32)).astype(bf)
        other = value[CH : 2 * CH] + skip * sig[1, rows, :].astype(f32)
        w_loc[rows, :] = other
        yd[1, rows, :] = other.astype(bf)

    def products(terms_of):
        def block(b, carry):
            first = pl.multiple_of(b * 16, 16)

            def pair(ref, k):
                at = pl.ds(k * CH + first, 16)
                return ref[at, 0:span], ref[at, span:]

            for k, terms in enumerate(terms_of(lambda n: pair(spec_h, n), lambda n: pair(spec_s, n))):
                re = im = None
                for (tc, ts), (xc, xs), sign in terms:
                    if sign > 0:
                        new_re, new_im = tc * xc - ts * xs, tc * xs + ts * xc
                    else:
                        new_re, new_im = tc * xc + ts * xs, tc * xs - ts * xc
                    re = new_re if re is None else re + new_re
                    im = new_im if im is None else im + new_im
                at = pl.ds(k * CH + first, 16)
                prod[at, 0:span] = re.astype(bf)
                prod[at, span:] = im.astype(bf)
            return carry

        lax.fori_loop(0, CH // 16, block, 0, unroll=8)

    def inner_terms(h, s):
        hs = [h(k) for k in range(4)]
        t = [hs[0]] + [(hs[k][0] + hs[k - 1][1], hs[k][1] - hs[k - 1][0]) for k in (1, 2, 3)]
        own, other, near = [s(k) for k in range(3)]
        return [
            [(t[0], own, 1), (t[1], near, 1)],
            [(t[0], other, -1)],
            [(t[1], own, 1), (t[2], near, 1)],
            [(t[2], own, 1), (t[3], near, 1)],
            [(t[1], other, -1)],
        ]

    def outer_terms(h, s):
        return [[(h(0), s(0), 1)], [(h(0), s(1), -1)]]

    def main_inner(i):
        c, rows = rows_of(i)

        @pl.when(i < half)
        def _():
            h_arrival(inward, i).wait_recv()
            h_over_copy(1, inward, i).start()
            h_arrival(far, i).wait_recv()
            h_over_copy(2, far, i).start()

            @pl.when(rank == 2)
            def _():
                h_back_copy(i).start()

        @pl.when(i >= half)
        def _():
            h_arrival(outward, i).wait_recv()
            h_arrival(inward, i).wait_recv()
            h_arrival(far, i).wait_recv()

        u_copy(i).wait_recv()
        spec_h[...] = mm(h_all[:, rows, :].reshape(4 * CH, span), wh[...])
        spec_s[...] = mm(sig[:, rows, :].reshape(3 * CH, span), wsig[...])
        products(inner_terms)
        value = mm(prod[...], winv[...])
        for which in range(3):
            c_src[which, rows, :] = value[(2 + which) * CH : (3 + which) * CH].astype(bf)

        @pl.when(i >= RELAY)
        def _():
            mini_src[c] = pick(c_src[1 - mir, rows, 0:128], [(8 - 6 * mir, 0), (8 - 4 * mir, 0)]).astype(bf)
            mini_copy(i).start()

        c_copy(1, i).start()
        keep_local(rows, value)
        halo(i)
        c_copy(0, i).start()

        @pl.when(i >= RELAY)
        def _():
            c_copy(2, i).start()

        @pl.when((rank == 1) | (i >= RELAY))
        def _():
            mini_own[c] = pick(c_src[2 * mir, rows, 0:128], [(8, 0)]).astype(bf)

    def relay(i):
        c, rows = rows_of(i)
        c_arrival(1, i).wait_recv()
        c_src[2, rows, :] = (c_src[2, rows, :].astype(f32) + c_in[1, rows, :].astype(f32)).astype(bf)
        c_copy(2, i).start()
        c_arrival(0, i).wait_recv()

        @pl.when(rank == 1)
        def _():
            mini_src[c] = pick(c_in[0, rows, 0:128], [(2, 0), (4, 0)]).astype(bf)
            mini_copy(i).start()

        @pl.when(rank == 2)
        def _():
            mini_own[c] = pick(c_src[2, rows, 0:128], [(8, 0)]).astype(bf)

    def main_outer(i):
        c, rows = rows_of(i)

        @pl.when(rank == 3)
        def _():
            h_arrival(0, i).wait_recv()

            @pl.when(i < half)
            def _():
                h_over_copy(0, 0, i).start()

        spec_h[0:CH] = mm(h_all[0, rows, :], wh[...])
        spec_s[0 : 2 * CH] = mm(sig[0:2, rows, :].reshape(2 * CH, span), wsig[...])
        products(outer_terms)
        keep_local(rows, mm(prod[0 : 2 * CH], winv[...]))

    def grad_of(a, rows):
        if a == 0:
            return xd[rows, :].astype(f32) * yd[mir, rows, :].astype(f32)
        other = v_s if a == 1 else k_s
        return yd[1 - mir, rows, :].astype(f32) * other[rows, :].astype(f32)

    def halo(i):
        c, rows = rows_of(i)
        first = slice(0, 128)
        edge = pick(xd[rows, first], [(0, 0)]) + pick(yd[1 - mir, rows, first], [(2, 0), (4, 0)])
        edge = edge + pick(yd[mir, rows, first], [(8, 0)])
        edge = edge + pick(v_s[rows, first], [(10, 0)]) + pick(k_s[rows, first], [(12, 0)])
        hal_src[c] = edge.astype(bf)
        hal_copy(i).start()

    def gates(rows, edges, arrays):
        tap = par[rows, :]
        first_grads = jnp.concatenate([edges[0:8] * edges[8:16], jnp.zeros((8, CH), f32)], axis=0)
        edge = mm(first_grads.astype(bf), spread(0), TN)
        if 0 in arrays:
            out_ref[rows, :] = (q_s[rows, :].astype(f32) * yd[mir, rows, :].astype(f32)).astype(bf)
        for a in arrays:
            grad = grad_of(a, rows)
            wide = jnp.concatenate([grad, edge[:, 128 * a : 128 * a + 128]], axis=1)
            acc = tap[:, 3 * a : 3 * a + 1] * grad
            for j in (1, 2):
                moved = pltpu.roll(wide, span + 128 - j, 1)[:, :span]
                acc = acc + tap[:, 3 * a + j : 3 * a + j + 1] * (moved * keep_b[j - 1, 0:1, :])
            df_ref[a, rows, :] = acc.astype(bf)

    def early(i):
        c, rows = rows_of(i)

        @pl.when(rank < 3)
        def _():
            hal_copy(i).wait_recv()

        edges = hal[c].astype(f32) + mini_own[c].astype(f32)

        @pl.when(mir == 0)
        def _():
            gates(rows, edges, (0,))

        @pl.when(mir == 1)
        def _():
            gates(rows, edges, (1, 2))

    def late(i):
        c, rows = rows_of(i)

        @pl.when(i >= RELAY)
        def _():
            c_arrival(0, i).wait_recv()

        @pl.when(inner)
        def _():
            yd[1, rows, :] = (w_loc[rows, :] + c_in[0, rows, :].astype(f32)).astype(bf)

        @pl.when((inn == 0) & (i >= RELAY))
        def _():
            c_arrival(1, i).wait_recv()
            cross = c_in[0, rows, :].astype(f32) + c_in[1, rows, :].astype(f32)
            yd[1, rows, :] = (w_loc[rows, :] + cross).astype(bf)

        @pl.when((inn == 0) & (i < RELAY))
        def _():
            c_arrival(1, i).wait_recv()
            yd[1, rows, :] = (w_loc[rows, :] + c_in[1, rows, :].astype(f32)).astype(bf)

        @pl.when((rank == 0) | ((rank == 2) & (i >= RELAY)))
        def _():
            mini_copy(i).wait_recv()

        edges = hal[c].astype(f32) + mini[c].astype(f32) + mini_own[c].astype(f32)

        @pl.when(mir == 0)
        def _():
            gates(rows, edges, (1, 2))

        @pl.when(mir == 1)
        def _():
            gates(rows, edges, (0,))

    def first_steps(s, carry):
        prepare(s)
        return carry

    lax.fori_loop(0, count, first_steps, 0)

    def step(s, carry):
        main = s < count

        @pl.when(inner & main)
        def _():
            main_inner(s)

        @pl.when((inn == 0) & main)
        def _():
            main_outer(s)

        @pl.when((rank == 3) & main)
        def _():
            halo(s)

        @pl.when(inner & (s >= HOLD) & (s < RELAY + HOLD) & (s < count + HOLD))
        def _():
            relay(s - HOLD)

        return carry

    lax.fori_loop(0, max(count, min(RELAY, count) + HOLD), step, 0)

    def last_steps(s, carry):
        @pl.when(s < count)
        def _():
            early(s)

        @pl.when(s >= BACK)
        def _():
            late(s - BACK)

        return carry

    lax.fori_loop(0, count + BACK, last_steps, 0)

    @pl.when(rank < 3)
    def _():
        rim_copy().wait_send()

    def drain(i, carry):
        @pl.when(inn == 0)
        def _():
            u_copy(i).wait_send()

        @pl.when(rank > 0)
        def _():
            hal_copy(i).wait_send()

        @pl.when(inner)
        def _():
            for which in range(3):
                c_copy(which, i).wait_send()

        @pl.when((rank == 1) | ((rank == 2) & (i >= RELAY)))
        def _():
            mini_copy(i).wait_send()

        @pl.when(i < half)
        def _():
            h_own_copy(i).wait_send()

            @pl.when(inner)
            def _():
                h_on_copy(i).wait_send()
                h_over_copy(0, outward, i).wait_send()
                h_over_copy(1, inward, i).wait_send()
                h_over_copy(2, far, i).wait_send()

            @pl.when(rank == 2)
            def _():
                h_back_copy(i).wait_send()

            @pl.when(rank == 3)
            def _():
                h_over_copy(0, 0, i).wait_send()

        return carry

    lax.fori_loop(0, count, drain, 0)


def local_kernel(features, dout, filters, taps, skip, lengths):
    channels, span = dout.shape
    count = channels // CH
    bf = jnp.bfloat16
    f32 = jnp.float32
    there, back = block_tables(span)
    operands = [lengths, features, dout, filters, taps, skip[None], jnp.asarray(there), jnp.asarray(back)]
    vmem = pl.BlockSpec(memory_space=pltpu.VMEM)
    hbm = pl.BlockSpec(memory_space=pltpu.HBM)
    dma = pltpu.SemaphoreType.DMA
    return pl.pallas_call(
        mixer_kernel,
        out_shape=(pltpu.VMEM(dout.shape, bf), pltpu.VMEM(features.shape, bf)),
        in_specs=[hbm] * 8,
        out_specs=(vmem, vmem),
        scratch_shapes=[
            pltpu.SMEM(lengths.shape, jnp.int32),
            pltpu.VMEM((3, channels, span), bf),
            pltpu.VMEM((channels, span), bf),
            pltpu.VMEM((3, 3, channels), f32),
            pltpu.VMEM((1, channels), f32),
            pltpu.VMEM((channels, 128), f32),
            pltpu.VMEM((span, 2 * span), bf),
            pltpu.VMEM((span, 2 * span), bf),
            pltpu.VMEM((2 * span, span), bf),
            pltpu.VMEM((2, 8, span), f32),
            pltpu.VMEM((2, 8, span), f32),
            pltpu.VMEM((16, channels // 2), bf),
            pltpu.VMEM((16, channels // 2), bf),
            pltpu.VMEM((4, channels, span), bf),
            pltpu.VMEM((3, channels, span), bf),
            pltpu.VMEM((channels, span), bf),
            pltpu.VMEM((channels, span), bf),
            pltpu.VMEM((channels, span), bf),
            pltpu.VMEM((2, channels, span), bf),
            pltpu.VMEM((channels, span), f32),
            pltpu.VMEM((3, channels, span), bf),
            pltpu.VMEM((2, channels, span), bf),
            pltpu.VMEM((count, 16, CH), bf),
            pltpu.VMEM((count, 16, CH), bf),
            pltpu.VMEM((count, 16, CH), bf),
            pltpu.VMEM((count, 16, CH), bf),
            pltpu.VMEM((count, 16, CH), bf),
            pltpu.VMEM((3 * CH, 2 * span), f32),
            pltpu.VMEM((4 * CH, 2 * span), f32),
            pltpu.VMEM((5 * CH, 2 * span), bf),
            dma((9,)), dma, dma,
            dma((2, count)), dma((3, count)), dma((count,)), dma((4, count)),
            dma((count,)), dma((count,)), dma((3, count)), dma((2, count)),
            dma((count,)), dma((count,)), dma((count,)), dma((count,)),
        ],
        compiler_params=pltpu.CompilerParams(
            collective_id=0, has_side_effects=True, vmem_limit_bytes=32 * 1024 * 1024
        ),
    )(*[pltpu.with_memory_space_constraint(x, pltpu.HBM) for x in operands])


def local(features, dout, filters, taps, skip, lengths):
    channels, span = dout.shape
    fits = lax.axis_size("seq") == 4 and lax.axis_size("groups") == 2 and taps.shape[:2] == (3, 3)
    if fits and span == 256 and channels % (2 * CH) == 0:
        return local_kernel(features, dout, filters, taps, skip, lengths)
    return local_general(features, dout, filters, taps, skip, lengths)


def solution(mesh):
    in_specs = (
        P(None, ("chan", "sub"), ("groups", "seq")),
        P(("chan", "sub"), ("groups", "seq")),
        P(("chan", "sub"), "seq"),
        P(None, None, ("chan", "sub")),
        P(("chan", "sub")),
        P("groups"),
    )
    out_specs = (P(("chan", "sub"), ("groups", "seq")), P(None, ("chan", "sub"), ("groups", "seq")))
    return jax.shard_map(local, mesh=mesh, in_specs=in_specs, out_specs=out_specs, check_vma=False)
```

```python
import functools

import jax
import numpy as np
import jax.numpy as jnp
from jax import lax
from jax.experimental import pallas as pl
from jax.experimental.pallas import tpu as pltpu
from jax.sharding import PartitionSpec as P

HIGHEST = lax.Precision.HIGHEST
TWO_PI = 6.283185307179586


def shifted(value, axis, steps):
    count = lax.axis_size(axis)
    leading, last = (max(0, -steps), min(count, count - steps))
    return lax.ppermute(value, axis, [(source, source + steps) for source in range(leading, last)])


def genome_offsets(lengths, positions):
    order = jnp.arange(lengths.shape[0], dtype=jnp.int32)
    so_far = (order[None, :] <= order[:, None]).astype(jnp.int32)
    ends_at = jnp.sum(so_far * lengths[None, :], axis=1, dtype=jnp.int32)
    before = (ends_at[None, :] <= positions[:, None]).astype(jnp.int32)
    return positions - jnp.sum(before * lengths[None, :], axis=1, dtype=jnp.int32)


def short_forward(extended, taps_local, offsets):
    span_rows = offsets.shape[0]
    count = taps_local.shape[1]
    result = jnp.zeros(extended.shape[:2] + (span_rows,), jnp.float32)
    for tap_index in range(count):
        begin = count - 1 - tap_index
        window = extended[:, :, begin : begin + span_rows].astype(jnp.float32)
        keep_mask = (offsets >= tap_index).astype(jnp.float32)
        result = result + taps_local[:, tap_index, :, None] * window * keep_mask[None, None, :]
    return result


def short_backward(grads_ext, taps_local, offsets_ext):
    count = taps_local.shape[1]
    span_rows = offsets_ext.shape[0] - (count - 1)
    result = jnp.zeros(grads_ext.shape[:2] + (span_rows,), jnp.float32)
    for tap_index in range(count):
        window = grads_ext[:, :, tap_index : tap_index + span_rows]
        keep_mask = (offsets_ext[tap_index : tap_index + span_rows] >= tap_index).astype(
            jnp.float32
        )
        result = result + taps_local[:, tap_index, :, None] * window * keep_mask[None, None, :]
    return result


def dft_table(rows_n, cols_n, period):
    row_ids = jnp.arange(rows_n, dtype=jnp.int32)
    col_ids = jnp.arange(cols_n, dtype=jnp.int32)
    phase = row_ids[:, None] * col_ids[None, :] % period
    angles = phase.astype(jnp.float32) * (-TWO_PI / period)
    return (jnp.cos(angles), jnp.sin(angles))


def forward_transform(signal, tables):
    (row_re, row_im), (twid_re, twid_im), (col_re, col_im) = tables
    half_rows = signal.shape[1] // 128
    blocks_in = signal.reshape(signal.shape[0], half_rows, 128)
    part_re = jnp.einsum("kn,cnm->ckm", row_re[:, :half_rows], blocks_in, precision=HIGHEST)
    part_im = jnp.einsum("kn,cnm->ckm", row_im[:, :half_rows], blocks_in, precision=HIGHEST)
    turned_re = part_re * twid_re - part_im * twid_im
    turned_im = part_re * twid_im + part_im * twid_re
    spec_re = jnp.einsum("ckn,nm->ckm", turned_re, col_re, precision=HIGHEST) - jnp.einsum(
        "ckn,nm->ckm", turned_im, col_im, precision=HIGHEST
    )
    spec_im = jnp.einsum("ckn,nm->ckm", turned_re, col_im, precision=HIGHEST) + jnp.einsum(
        "ckn,nm->ckm", turned_im, col_re, precision=HIGHEST
    )
    return (spec_re, spec_im)


def inverse_transform(spec_re, spec_im, tables):
    (row_re, row_im), (twid_re, twid_im), (col_re, col_im) = tables
    rows_n = spec_re.shape[1]
    half_rows = rows_n // 2
    mid_re = jnp.einsum("ckn,nm->ckm", spec_re, col_re, precision=HIGHEST) + jnp.einsum(
        "ckn,nm->ckm", spec_im, col_im, precision=HIGHEST
    )
    mid_im = jnp.einsum("ckn,nm->ckm", spec_im, col_re, precision=HIGHEST) - jnp.einsum(
        "ckn,nm->ckm", spec_re, col_im, precision=HIGHEST
    )
    back_re = mid_re * twid_re + mid_im * twid_im
    back_im = mid_im * twid_re - mid_re * twid_im
    signal = jnp.einsum("nk,ckm->cnm", row_re[:half_rows], back_re, precision=HIGHEST) + jnp.einsum(
        "nk,ckm->cnm", row_im[:half_rows], back_im, precision=HIGHEST
    )
    return signal.reshape(signal.shape[0], half_rows * 128) * (1.0 / (rows_n * 128))


def long_filter(filt, mixed_in, grad_in, skip_part):
    rows_n = 2 * mixed_in.shape[1] // 128
    tables = (
        dft_table(rows_n, rows_n, rows_n),
        dft_table(rows_n, 128, rows_n * 128),
        dft_table(128, 128, 128),
    )
    mixed_f = mixed_in.astype(jnp.float32)
    grad_f = grad_in.astype(jnp.float32)
    filt_re, filt_im = forward_transform(filt.astype(jnp.float32), tables)
    mix_re, mix_im = forward_transform(mixed_f, tables)
    grad_re, grad_im = forward_transform(grad_f, tables)
    conv_out = inverse_transform(
        filt_re * mix_re - filt_im * mix_im, filt_re * mix_im + filt_im * mix_re, tables
    )
    corr_out = inverse_transform(
        filt_re * grad_re + filt_im * grad_im, filt_re * grad_im - filt_im * grad_re, tables
    )
    y_out = (conv_out + skip_part[:, None] * mixed_f).astype(jnp.bfloat16)
    dmixed = (corr_out + skip_part[:, None] * grad_f).astype(jnp.bfloat16)
    return (y_out, dmixed)


DENSE_MAX = 1024
FINE = 32


def angle_parts(length):
    base = np.arange(length, dtype=np.int64) * 4 + 1
    fine = np.arange(FINE, dtype=np.int64)[:, None] * base[None, :] % (4 * length)
    coarse = np.arange(0, length, FINE, dtype=np.int64)[:, None] * base[None, :] % (4 * length)
    scale = 2.0 * np.pi / (4 * length)
    return [
        func(part * scale).astype(np.float32)
        for part in (coarse, fine)
        for func in (np.cos, np.sin)
    ]


def dense_filter(filt, mixed_in, grad_in, skip_part):
    length = mixed_in.shape[1]
    cc, cs, fc, fs = [jnp.asarray(p)[:, None] if i < 2 else jnp.asarray(p)[None] for i, p in enumerate(angle_parts(length))]
    cos_t = (cc * fc - cs * fs).reshape(length, length)
    sin_t = (cs * fc + cc * fs).reshape(length, length)
    table = jnp.concatenate([cos_t, sin_t], axis=1).astype(jnp.bfloat16)

    def fwd(x):
        return jnp.dot(x, table, preferred_element_type=jnp.float32)

    def inv(x):
        return lax.dot_general(x.astype(jnp.bfloat16), table, (((1,), (1,)), ((), ())), preferred_element_type=jnp.float32) * (1.0 / length)

    h, m, g = fwd(filt), fwd(mixed_in), fwd(grad_in)
    hc, hs = h[:, :length], h[:, length:]
    mc, ms = m[:, :length], m[:, length:]
    gc, gs = g[:, :length], g[:, length:]
    conv_out = inv(jnp.concatenate([hc * mc - hs * ms, hc * ms + hs * mc], axis=1))
    corr_out = inv(jnp.concatenate([hc * gc + hs * gs, hc * gs - hs * gc], axis=1))
    y_out = (conv_out + skip_part[:, None] * mixed_in.astype(jnp.float32)).astype(jnp.bfloat16)
    dmixed = (corr_out + skip_part[:, None] * grad_in.astype(jnp.float32)).astype(jnp.bfloat16)
    return (y_out, dmixed)


def to_channels(stacked):
    return lax.all_to_all(stacked, "seq", split_axis=1, concat_axis=2, tiled=True)


def to_sequence(stacked):
    return lax.all_to_all(stacked, "seq", split_axis=2, concat_axis=1, tiled=True)


def local_general(features, dout, filters, taps, skip, lengths):
    blocks = lax.axis_size("seq")
    seq_rank = lax.axis_index("seq")
    span_rows = features.shape[2]
    channels_here = features.shape[1]
    chan_part = channels_here // blocks
    count = taps.shape[1]
    margin = count - 1
    rim = shifted(features[:, :, span_rows - margin :], "seq", 1)
    extended = jnp.concatenate([rim, features], axis=2)
    first_pos = seq_rank * span_rows
    offsets = genome_offsets(lengths, first_pos + jnp.arange(span_rows, dtype=jnp.int32))
    filtered = short_forward(extended, taps, offsets).astype(jnp.bfloat16)
    query_side = filtered[0].astype(jnp.float32)
    key_side = filtered[1].astype(jnp.float32)
    value_side = filtered[2].astype(jnp.float32)
    dout_f = dout.astype(jnp.float32)
    mixed = (key_side * value_side).astype(jnp.bfloat16)
    grad_in = (dout_f * query_side).astype(jnp.bfloat16)
    moved = to_channels(jnp.stack([mixed, grad_in, filters]))
    skip_part = lax.dynamic_slice_in_dim(skip, seq_rank * chan_part, chan_part, 0)
    run = dense_filter if moved.shape[2] <= DENSE_MAX else long_filter
    y_out, dmixed = run(moved[2], moved[0], moved[1], skip_part)
    returned = to_sequence(jnp.stack([y_out, dmixed]))
    y_here = returned[0].astype(jnp.float32)
    dmixed_here = returned[1].astype(jnp.float32)
    out = (query_side * y_here).astype(jnp.bfloat16)
    grads = jnp.stack([dout_f * y_here, dmixed_here * value_side, dmixed_here * key_side])
    ahead = shifted(grads[:, :, :margin], "seq", -1)
    grads_ext = jnp.concatenate([grads, ahead], axis=2)
    offsets_ext = genome_offsets(
        lengths, first_pos + jnp.arange(span_rows + margin, dtype=jnp.int32)
    )
    dfeatures = short_backward(grads_ext, taps, offsets_ext).astype(jnp.bfloat16)
    return (out, dfeatures)


CH = 128
BACK = 1
RELAY = 5
HOLD = 4
NN = (((1,), (0,)), ((), ()))
NT = (((1,), (1,)), ((), ()))
TN = (((0,), (0,)), ((), ()))
MESH = pl.DeviceIdType.MESH


def mm(a, b, dims=NN):
    return lax.dot_general(a, b, dims, preferred_element_type=jnp.float32)


def block_tables(size):
    place = np.arange(size, dtype=np.int64)
    phase = place[:, None] * (4 * place[None, :] + 1) % (4 * size)
    angle = phase * (2.0 * np.pi / (4 * size))
    cos, sin = np.cos(angle), np.sin(angle)
    there = np.stack([np.concatenate([cos, s * sin], axis=1) for s in (1, -1)])
    back = np.stack([np.concatenate([cos.T, s * sin.T], axis=0) for s in (1, -1)]) / size
    return there.astype(jnp.bfloat16), back.astype(jnp.bfloat16)


def mixer_kernel(
    lengths_hbm, feat_hbm, dout_hbm, filt_hbm, taps_hbm, skip_hbm, there_hbm, back_hbm,
    out_ref, df_ref,
    lengths_ref, xf, xd, taps_v, skip_v, par, wh, wsig, winv, keep_f, keep_b,
    rim_src, rim, h_all, sig, q_s, k_s, v_s, yd, w_loc, c_src, c_in,
    hal_src, hal, mini_src, mini, mini_own, spec_s, spec_h, prod,
    ld, rim_ss, rim_rs, h_zs, h_ys, h_bs, h_rs, u_ss, u_rs, c_ss, c_rs, hal_ss, hal_rs, mini_ss, mini_rs,
):
    rank = lax.axis_index("seq")
    group = lax.axis_index("groups")
    channels, span = xd.shape
    count = channels // CH
    half = count // 2
    mir = rank // 2
    inn = lax.rem(rank + mir, 2)
    inner = inn == 1
    inward = rank + 1 - 2 * mir
    outward = rank - 1 + 2 * mir
    far = 3 - 3 * mir
    bf = jnp.bfloat16
    f32 = jnp.float32

    def greet(**where):
        pl.semaphore_signal(barrier, inc=1, device_id=where, device_id_type=MESH)

    barrier = pltpu.get_barrier_semaphore()
    greet(seq=inward)

    @pl.when(inner)
    def _():
        greet(seq=outward)

    @pl.when(inn == 0)
    def _():
        greet(seq=2 - mir)

    @pl.when(rank > 0)
    def _():
        greet(groups=1 - group)

    loads = [
        pltpu.make_async_copy(feat_hbm, xf, ld.at[0]),
        pltpu.make_async_copy(taps_hbm, taps_v, ld.at[1]),
        pltpu.make_async_copy(skip_hbm, skip_v, ld.at[2]),
        pltpu.make_async_copy(dout_hbm, xd, ld.at[3]),
        pltpu.make_async_copy(filt_hbm, h_all.at[rank], ld.at[4]),
        pltpu.make_async_copy(there_hbm.at[0], wh, ld.at[5]),
        pltpu.make_async_copy(there_hbm.at[mir], wsig, ld.at[6]),
        pltpu.make_async_copy(back_hbm.at[mir], winv, ld.at[7]),
        pltpu.make_async_copy(lengths_hbm, lengths_ref, ld.at[8]),
    ]
    for load in loads:
        load.start()

    def rows_of(i):
        c = lax.rem(half * group + i, count)
        return c, pl.ds(pl.multiple_of(c * CH, CH), CH)

    def remote(src, dst, ss, rs, where):
        return pltpu.make_async_remote_copy(
            src_ref=src, dst_ref=dst, send_sem=ss, recv_sem=rs, device_id=where, device_id_type=MESH
        )

    def h_own_copy(i):
        c, rows = rows_of(i)
        return remote(filt_hbm.at[rows], h_all.at[rank, rows], h_zs.at[0, i], h_rs.at[rank, c], {"seq": inward})

    def h_on_copy(i):
        c, rows = rows_of(i)
        return remote(h_all.at[outward, rows], h_all.at[outward, rows], h_zs.at[1, i], h_rs.at[outward, c], {"seq": inward})

    def h_back_copy(i):
        c, rows = rows_of(i)
        return remote(h_all.at[0, rows], h_all.at[0, rows], h_bs.at[i], h_rs.at[0, c], {"seq": 3})

    def h_over_copy(which, slot, i):
        c, rows = rows_of(i)
        return remote(
            h_all.at[slot, rows], h_all.at[slot, rows], h_ys.at[which, i], h_rs.at[slot, c], {"groups": 1 - group}
        )

    def h_arrival(slot, i):
        c, rows = rows_of(i)
        return remote(h_all.at[slot, rows], h_all.at[slot, rows], h_zs.at[0, 0], h_rs.at[slot, c], {"seq": inward})

    def u_copy(i):
        c, rows = rows_of(i)
        return remote(sig.at[0, rows], sig.at[2, rows], u_ss.at[i], u_rs.at[c], {"seq": inward})

    def c_copy(which, i):
        c, rows = rows_of(i)
        direct = (i >= RELAY).astype(jnp.int32)
        slot = (0, 1 - direct, 1)[which]
        where = (inward, inward + (far - inward) * direct, outward)[which]
        return remote(
            c_src.at[which, rows], c_in.at[slot, rows], c_ss.at[which, i], c_rs.at[slot, c], {"seq": where}
        )

    def c_arrival(slot, i):
        c, rows = rows_of(i)
        return remote(c_in.at[slot, rows], c_in.at[slot, rows], c_ss.at[0, i], c_rs.at[slot, c], {"seq": inward})

    def mini_copy(i):
        c, _ = rows_of(i)
        where = (2 - 2 * mir) * (i >= RELAY).astype(jnp.int32)
        return remote(mini_src.at[c], mini.at[c], mini_ss.at[i], mini_rs.at[c], {"seq": where})

    def rim_copy():
        return remote(rim_src, rim, rim_ss, rim_rs, {"seq": jnp.minimum(rank + 1, 3)})

    def hal_copy(i):
        c, _ = rows_of(i)
        return remote(hal_src.at[c], hal.at[c], hal_ss.at[i], hal_rs.at[c], {"seq": jnp.maximum(rank - 1, 0)})

    @pl.when(rank == 0)
    def _():
        rim[...] = jnp.zeros_like(rim)

    @pl.when(rank == 3)
    def _():
        hal[...] = jnp.zeros_like(hal)

    @pl.when(lax.rem(rank, 2) == 1)
    def _():
        mini[...] = jnp.zeros_like(mini)

    @pl.when(rank == 2)
    def _():
        for i in range(min(RELAY, count)):
            mini[rows_of(i)[0]] = jnp.zeros((16, CH), bf)

    @pl.when(inn == 0)
    def _():
        mini_own[...] = jnp.zeros_like(mini_own)

    pl.semaphore_wait(barrier, 1 + 3 * inn + rank // 3)

    h_own_copy(0).start()

    loads[0].wait()
    r_id = lax.broadcasted_iota(jnp.int32, (16, 128), 0)
    p_id = lax.broadcasted_iota(jnp.int32, (16, 128), 1)
    total = None
    for part in range(2):
        for a in range(3):
            first = 8 * part + 2 * a
            hit = ((r_id == first) & (p_id == 126)) | ((r_id == first + 1) & (p_id == 127))
            edge = xf[a, part * half * CH : (part + 1) * half * CH, span - 128 :]
            term = mm(jnp.where(hit, 1.0, 0.0).astype(bf), edge, NT)
            total = term if total is None else total + term
    rim_src[...] = total.astype(bf)

    @pl.when(rank < 3)
    def _():
        rim_copy().start()

    for i in range(1, max(half - 1, 1)):
        h_own_copy(i).start()

    @pl.when(inn == 0)
    def _():
        for i in range(max(half - 1, 1), half):
            h_own_copy(i).start()

    loads[8].wait()

    def keeps(ahead, least):
        position = rank * span + ahead + lax.broadcasted_iota(jnp.int32, (8, span), 1)
        offset = position
        end = jnp.int32(0)
        for g in range(lengths_ref.shape[0]):
            one = lengths_ref[g]
            end = end + one
            offset = offset - jnp.where(end <= position, one, 0)
        return jnp.where(offset >= least, 1.0, 0.0)

    for j in (1, 2):
        keep_f[j - 1] = keeps(0, j)
        keep_b[j - 1] = keeps(j, j)

    loads[1].wait()
    loads[2].wait()
    flat = jnp.concatenate(
        [taps_v[0], taps_v[1], taps_v[2], skip_v[...], jnp.zeros((6, channels), f32)], axis=0
    )
    for c in range(count):
        par[c * CH : (c + 1) * CH, 0:16] = flat[:, c * CH : (c + 1) * CH].T
    for load in loads[3:8]:
        load.wait()

    def pass_on(i):
        h_arrival(outward, i).wait_recv()
        h_on_copy(i).start()
        h_over_copy(0, outward, i).start()

    @pl.when(inner)
    def _():
        for i in range(min(2, half)):
            pass_on(i)
            if i == 0:
                for k in range(max(half - 1, 1), half):
                    h_own_copy(k).start()

    @pl.when(rank > 0)
    def _():
        rim_copy().wait_recv()

    rr = lax.broadcasted_iota(jnp.int32, (16, 384), 0)
    cc = lax.broadcasted_iota(jnp.int32, (16, 384), 1)

    def spread(first, above=0):
        hit = None
        for a in range(3):
            row = 2 * a + above
            one = ((rr == row) & (cc == 128 * a + first)) | ((rr == row + 1) & (cc == 128 * a + first + 1))
            hit = one if hit is None else hit | one
        return jnp.where(hit, 1.0, 0.0).astype(bf)

    def prepare(i):
        c, rows = rows_of(i)
        upper = c // half
        cols = pl.ds(pl.multiple_of((c - half * upper) * CH, CH), CH)
        edge = mm(rim[:, cols], spread(126, 8 * upper), TN)
        tap = par[rows, :]
        result = []
        for a in range(3):
            here = xf[a, rows, :].astype(f32)
            wide = jnp.concatenate([edge[:, 128 * a : 128 * a + 128], here], axis=1)
            acc = tap[:, 3 * a : 3 * a + 1] * here
            for j in (1, 2):
                moved = pltpu.roll(wide, j, 1)[:, 128:]
                acc = acc + tap[:, 3 * a + j : 3 * a + j + 1] * (moved * keep_f[j - 1, 0:1, :])
            result.append(acc.astype(bf))
        q, k, v = result
        q_s[rows, :] = q
        k_s[rows, :] = k
        v_s[rows, :] = v
        sig[mir, rows, :] = (k.astype(f32) * v.astype(f32)).astype(bf)
        sig[1 - mir, rows, :] = (xd[rows, :].astype(f32) * q.astype(f32)).astype(bf)

        @pl.when(inn == 0)
        def _():
            u_copy(i).start()

        @pl.when(inner & (i + 2 < half))
        def _():
            pass_on(i + 2)

    def pick(block, rows_at):
        hit = None
        for first, lane in rows_at:
            one = ((r_id == first) & (p_id == lane)) | ((r_id == first + 1) & (p_id == lane + 1))
            hit = one if hit is None else hit | one
        return mm(jnp.where(hit, 1.0, 0.0).astype(bf), block, NT)

    def keep_local(rows, value):
        skip = par[rows, 9:10]
        yd[0, rows, :] = (value[0:CH] + skip * sig[0, rows, :].astype(f32)).astype(bf)
        other = value[CH : 2 * CH] + skip * sig[1, rows, :].astype(f32)
        w_loc[rows, :] = other
        yd[1, rows, :] = other.astype(bf)

    def products(terms_of):
        def block(b, carry):
            first = pl.multiple_of(b * 16, 16)

            def pair(ref, k):
                at = pl.ds(k * CH + first, 16)
                return ref[at, 0:span], ref[at, span:]

            for k, terms in enumerate(terms_of(lambda n: pair(spec_h, n), lambda n: pair(spec_s, n))):
                re = im = None
                for (tc, ts), (xc, xs), sign in terms:
                    if sign > 0:
                        new_re, new_im = tc * xc - ts * xs, tc * xs + ts * xc
                    else:
                        new_re, new_im = tc * xc + ts * xs, tc * xs - ts * xc
                    re = new_re if re is None else re + new_re
                    im = new_im if im is None else im + new_im
                at = pl.ds(k * CH + first, 16)
                prod[at, 0:span] = re.astype(bf)
                prod[at, span:] = im.astype(bf)
            return carry

        lax.fori_loop(0, CH // 16, block, 0, unroll=8)

    def inner_terms(h, s):
        hs = [h(k) for k in range(4)]
        t = [hs[0]] + [(hs[k][0] + hs[k - 1][1], hs[k][1] - hs[k - 1][0]) for k in (1, 2, 3)]
        own, other, near = [s(k) for k in range(3)]
        return [
            [(t[0], own, 1), (t[1], near, 1)],
            [(t[0], other, -1)],
            [(t[1], own, 1), (t[2], near, 1)],
            [(t[2], own, 1), (t[3], near, 1)],
            [(t[1], other, -1)],
        ]

    def outer_terms(h, s):
        return [[(h(0), s(0), 1)], [(h(0), s(1), -1)]]

    def main_inner(i):
        c, rows = rows_of(i)

        @pl.when(i < half)
        def _():
            h_arrival(inward, i).wait_recv()
            h_over_copy(1, inward, i).start()
            h_arrival(far, i).wait_recv()
            h_over_copy(2, far, i).start()

            @pl.when(rank == 2)
            def _():
                h_back_copy(i).start()

        @pl.when(i >= half)
        def _():
            h_arrival(outward, i).wait_recv()
            h_arrival(inward, i).wait_recv()
            h_arrival(far, i).wait_recv()

        u_copy(i).wait_recv()
        spec_h[...] = mm(h_all[:, rows, :].reshape(4 * CH, span), wh[...])
        spec_s[...] = mm(sig[:, rows, :].reshape(3 * CH, span), wsig[...])
        products(inner_terms)
        value = mm(prod[...], winv[...])
        for which in range(3):
            c_src[which, rows, :] = value[(2 + which) * CH : (3 + which) * CH].astype(bf)

        @pl.when(i >= RELAY)
        def _():
            mini_src[c] = pick(c_src[1 - mir, rows, 0:128], [(8 - 6 * mir, 0), (8 - 4 * mir, 0)]).astype(bf)
            mini_copy(i).start()

        c_copy(1, i).start()
        keep_local(rows, value)
        halo(i)
        c_copy(0, i).start()

        @pl.when(i >= RELAY)
        def _():
            c_copy(2, i).start()

        @pl.when((rank == 1) | (i >= RELAY))
        def _():
            mini_own[c] = pick(c_src[2 * mir, rows, 0:128], [(8, 0)]).astype(bf)

    def relay(i):
        c, rows = rows_of(i)
        c_arrival(1, i).wait_recv()
        c_src[2, rows, :] = (c_src[2, rows, :].astype(f32) + c_in[1, rows, :].astype(f32)).astype(bf)
        c_copy(2, i).start()
        c_arrival(0, i).wait_recv()

        @pl.when(rank == 1)
        def _():
            mini_src[c] = pick(c_in[0, rows, 0:128], [(2, 0), (4, 0)]).astype(bf)
            mini_copy(i).start()

        @pl.when(rank == 2)
        def _():
            mini_own[c] = pick(c_src[2, rows, 0:128], [(8, 0)]).astype(bf)

    def main_outer(i):
        c, rows = rows_of(i)

        @pl.when(rank == 3)
        def _():
            h_arrival(0, i).wait_recv()

            @pl.when(i < half)
            def _():
                h_over_copy(0, 0, i).start()

        spec_h[0:CH] = mm(h_all[0, rows, :], wh[...])
        spec_s[0 : 2 * CH] = mm(sig[0:2, rows, :].reshape(2 * CH, span), wsig[...])
        products(outer_terms)
        keep_local(rows, mm(prod[0 : 2 * CH], winv[...]))

    def grad_of(a, rows):
        if a == 0:
            return xd[rows, :].astype(f32) * yd[mir, rows, :].astype(f32)
        other = v_s if a == 1 else k_s
        return yd[1 - mir, rows, :].astype(f32) * other[rows, :].astype(f32)

    def halo(i):
        c, rows = rows_of(i)
        first = slice(0, 128)
        edge = pick(xd[rows, first], [(0, 0)]) + pick(yd[1 - mir, rows, first], [(2, 0), (4, 0)])
        edge = edge + pick(yd[mir, rows, first], [(8, 0)])
        edge = edge + pick(v_s[rows, first], [(10, 0)]) + pick(k_s[rows, first], [(12, 0)])
        hal_src[c] = edge.astype(bf)
        hal_copy(i).start()

    def gates(rows, edges, arrays):
        tap = par[rows, :]
        first_grads = jnp.concatenate([edges[0:8] * edges[8:16], jnp.zeros((8, CH), f32)], axis=0)
        edge = mm(first_grads.astype(bf), spread(0), TN)
        if 0 in arrays:
            out_ref[rows, :] = (q_s[rows, :].astype(f32) * yd[mir, rows, :].astype(f32)).astype(bf)
        for a in arrays:
            grad = grad_of(a, rows)
            wide = jnp.concatenate([grad, edge[:, 128 * a : 128 * a + 128]], axis=1)
            acc = tap[:, 3 * a : 3 * a + 1] * grad
            for j in (1, 2):
                moved = pltpu.roll(wide, span + 128 - j, 1)[:, :span]
                acc = acc + tap[:, 3 * a + j : 3 * a + j + 1] * (moved * keep_b[j - 1, 0:1, :])
            df_ref[a, rows, :] = acc.astype(bf)

    def early(i):
        c, rows = rows_of(i)

        @pl.when(rank < 3)
        def _():
            hal_copy(i).wait_recv()

        edges = hal[c].astype(f32) + mini_own[c].astype(f32)

        @pl.when(mir == 0)
        def _():
            gates(rows, edges, (0,))

        @pl.when(mir == 1)
        def _():
            gates(rows, edges, (1, 2))

    def late(i):
        c, rows = rows_of(i)

        @pl.when(i >= RELAY)
        def _():
            c_arrival(0, i).wait_recv()

        @pl.when(inner)
        def _():
            yd[1, rows, :] = (w_loc[rows, :] + c_in[0, rows, :].astype(f32)).astype(bf)

        @pl.when((inn == 0) & (i >= RELAY))
        def _():
            c_arrival(1, i).wait_recv()
            cross = c_in[0, rows, :].astype(f32) + c_in[1, rows, :].astype(f32)
            yd[1, rows, :] = (w_loc[rows, :] + cross).astype(bf)

        @pl.when((inn == 0) & (i < RELAY))
        def _():
            c_arrival(1, i).wait_recv()
            yd[1, rows, :] = (w_loc[rows, :] + c_in[1, rows, :].astype(f32)).astype(bf)

        @pl.when((rank == 0) | ((rank == 2) & (i >= RELAY)))
        def _():
            mini_copy(i).wait_recv()

        edges = hal[c].astype(f32) + mini[c].astype(f32) + mini_own[c].astype(f32)

        @pl.when(mir == 0)
        def _():
            gates(rows, edges, (1, 2))

        @pl.when(mir == 1)
        def _():
            gates(rows, edges, (0,))

    def first_steps(s, carry):
        prepare(s)
        return carry

    lax.fori_loop(0, count, first_steps, 0)

    def step(s, carry):
        main = s < count

        @pl.when(inner & main)
        def _():
            main_inner(s)

        @pl.when((inn == 0) & main)
        def _():
            main_outer(s)

        @pl.when((rank == 3) & main)
        def _():
            halo(s)

        @pl.when(inner & (s >= HOLD) & (s < RELAY + HOLD) & (s < count + HOLD))
        def _():
            relay(s - HOLD)

        return carry

    lax.fori_loop(0, max(count, min(RELAY, count) + HOLD), step, 0)

    def last_steps(s, carry):
        @pl.when(s < count)
        def _():
            early(s)

        @pl.when(s >= BACK)
        def _():
            late(s - BACK)

        return carry

    lax.fori_loop(0, count + BACK, last_steps, 0)

    @pl.when(rank < 3)
    def _():
        rim_copy().wait_send()

    def drain(i, carry):
        @pl.when(inn == 0)
        def _():
            u_copy(i).wait_send()

        @pl.when(rank > 0)
        def _():
            hal_copy(i).wait_send()

        @pl.when(inner)
        def _():
            for which in range(3):
                c_copy(which, i).wait_send()

        @pl.when((rank == 1) | ((rank == 2) & (i >= RELAY)))
        def _():
            mini_copy(i).wait_send()

        @pl.when(i < half)
        def _():
            h_own_copy(i).wait_send()

            @pl.when(inner)
            def _():
                h_on_copy(i).wait_send()
                h_over_copy(0, outward, i).wait_send()
                h_over_copy(1, inward, i).wait_send()
                h_over_copy(2, far, i).wait_send()

            @pl.when(rank == 2)
            def _():
                h_back_copy(i).wait_send()

            @pl.when(rank == 3)
            def _():
                h_over_copy(0, 0, i).wait_send()

        return carry

    lax.fori_loop(0, count, drain, 0)


def local_kernel(features, dout, filters, taps, skip, lengths):
    channels, span = dout.shape
    count = channels // CH
    bf = jnp.bfloat16
    f32 = jnp.float32
    there, back = block_tables(span)
    operands = [lengths, features, dout, filters, taps, skip[None], jnp.asarray(there), jnp.asarray(back)]
    vmem = pl.BlockSpec(memory_space=pltpu.VMEM)
    hbm = pl.BlockSpec(memory_space=pltpu.HBM)
    dma = pltpu.SemaphoreType.DMA
    return pl.pallas_call(
        mixer_kernel,
        out_shape=(pltpu.VMEM(dout.shape, bf), pltpu.VMEM(features.shape, bf)),
        in_specs=[hbm] * 8,
        out_specs=(vmem, vmem),
        scratch_shapes=[
            pltpu.SMEM(lengths.shape, jnp.int32),
            pltpu.VMEM((3, channels, span), bf),
            pltpu.VMEM((channels, span), bf),
            pltpu.VMEM((3, 3, channels), f32),
            pltpu.VMEM((1, channels), f32),
            pltpu.VMEM((channels, 128), f32),
            pltpu.VMEM((span, 2 * span), bf),
            pltpu.VMEM((span, 2 * span), bf),
            pltpu.VMEM((2 * span, span), bf),
            pltpu.VMEM((2, 8, span), f32),
            pltpu.VMEM((2, 8, span), f32),
            pltpu.VMEM((16, channels // 2), bf),
            pltpu.VMEM((16, channels // 2), bf),
            pltpu.VMEM((4, channels, span), bf),
            pltpu.VMEM((3, channels, span), bf),
            pltpu.VMEM((channels, span), bf),
            pltpu.VMEM((channels, span), bf),
            pltpu.VMEM((channels, span), bf),
            pltpu.VMEM((2, channels, span), bf),
            pltpu.VMEM((channels, span), f32),
            pltpu.VMEM((3, channels, span), bf),
            pltpu.VMEM((2, channels, span), bf),
            pltpu.VMEM((count, 16, CH), bf),
            pltpu.VMEM((count, 16, CH), bf),
            pltpu.VMEM((count, 16, CH), bf),
            pltpu.VMEM((count, 16, CH), bf),
            pltpu.VMEM((count, 16, CH), bf),
            pltpu.VMEM((3 * CH, 2 * span), f32),
            pltpu.VMEM((4 * CH, 2 * span), f32),
            pltpu.VMEM((5 * CH, 2 * span), bf),
            dma((9,)), dma, dma,
            dma((2, count)), dma((3, count)), dma((count,)), dma((4, count)),
            dma((count,)), dma((count,)), dma((3, count)), dma((2, count)),
            dma((count,)), dma((count,)), dma((count,)), dma((count,)),
        ],
        compiler_params=pltpu.CompilerParams(
            collective_id=0, has_side_effects=True, vmem_limit_bytes=32 * 1024 * 1024
        ),
    )(*[pltpu.with_memory_space_constraint(x, pltpu.HBM) for x in operands])


def local(features, dout, filters, taps, skip, lengths):
    channels, span = dout.shape
    fits = lax.axis_size("seq") == 4 and lax.axis_size("groups") == 2 and taps.shape[:2] == (3, 3)
    if fits and span == 256 and channels % (2 * CH) == 0:
        return local_kernel(features, dout, filters, taps, skip, lengths)
    return local_general(features, dout, filters, taps, skip, lengths)


def solution(mesh):
    in_specs = (
        P(None, ("chan", "sub"), ("groups", "seq")),
        P(("chan", "sub"), ("groups", "seq")),
        P(("chan", "sub"), "seq"),
        P(None, None, ("chan", "sub")),
        P(("chan", "sub")),
        P("groups"),
    )
    out_specs = (P(("chan", "sub"), ("groups", "seq")), P(None, ("chan", "sub"), ("groups", "seq")))
    return jax.shard_map(local, mesh=mesh, in_specs=in_specs, out_specs=out_specs, check_vma=False)
```

```python
import functools

import jax
import numpy as np
import jax.numpy as jnp
from jax import lax
from jax.experimental import pallas as pl
from jax.experimental.pallas import tpu as pltpu
from jax.sharding import PartitionSpec as P

HIGHEST = lax.Precision.HIGHEST
TWO_PI = 6.283185307179586


def shifted(value, axis, steps):
    count = lax.axis_size(axis)
    leading, last = (max(0, -steps), min(count, count - steps))
    return lax.ppermute(value, axis, [(source, source + steps) for source in range(leading, last)])


def genome_offsets(lengths, positions):
    order = jnp.arange(lengths.shape[0], dtype=jnp.int32)
    so_far = (order[None, :] <= order[:, None]).astype(jnp.int32)
    ends_at = jnp.sum(so_far * lengths[None, :], axis=1, dtype=jnp.int32)
    before = (ends_at[None, :] <= positions[:, None]).astype(jnp.int32)
    return positions - jnp.sum(before * lengths[None, :], axis=1, dtype=jnp.int32)


def short_forward(extended, taps_local, offsets):
    span_rows = offsets.shape[0]
    count = taps_local.shape[1]
    result = jnp.zeros(extended.shape[:2] + (span_rows,), jnp.float32)
    for tap_index in range(count):
        begin = count - 1 - tap_index
        window = extended[:, :, begin : begin + span_rows].astype(jnp.float32)
        keep_mask = (offsets >= tap_index).astype(jnp.float32)
        result = result + taps_local[:, tap_index, :, None] * window * keep_mask[None, None, :]
    return result


def short_backward(grads_ext, taps_local, offsets_ext):
    count = taps_local.shape[1]
    span_rows = offsets_ext.shape[0] - (count - 1)
    result = jnp.zeros(grads_ext.shape[:2] + (span_rows,), jnp.float32)
    for tap_index in range(count):
        window = grads_ext[:, :, tap_index : tap_index + span_rows]
        keep_mask = (offsets_ext[tap_index : tap_index + span_rows] >= tap_index).astype(
            jnp.float32
        )
        result = result + taps_local[:, tap_index, :, None] * window * keep_mask[None, None, :]
    return result


def dft_table(rows_n, cols_n, period):
    row_ids = jnp.arange(rows_n, dtype=jnp.int32)
    col_ids = jnp.arange(cols_n, dtype=jnp.int32)
    phase = row_ids[:, None] * col_ids[None, :] % period
    angles = phase.astype(jnp.float32) * (-TWO_PI / period)
    return (jnp.cos(angles), jnp.sin(angles))


def forward_transform(signal, tables):
    (row_re, row_im), (twid_re, twid_im), (col_re, col_im) = tables
    half_rows = signal.shape[1] // 128
    blocks_in = signal.reshape(signal.shape[0], half_rows, 128)
    part_re = jnp.einsum("kn,cnm->ckm", row_re[:, :half_rows], blocks_in, precision=HIGHEST)
    part_im = jnp.einsum("kn,cnm->ckm", row_im[:, :half_rows], blocks_in, precision=HIGHEST)
    turned_re = part_re * twid_re - part_im * twid_im
    turned_im = part_re * twid_im + part_im * twid_re
    spec_re = jnp.einsum("ckn,nm->ckm", turned_re, col_re, precision=HIGHEST) - jnp.einsum(
        "ckn,nm->ckm", turned_im, col_im, precision=HIGHEST
    )
    spec_im = jnp.einsum("ckn,nm->ckm", turned_re, col_im, precision=HIGHEST) + jnp.einsum(
        "ckn,nm->ckm", turned_im, col_re, precision=HIGHEST
    )
    return (spec_re, spec_im)


def inverse_transform(spec_re, spec_im, tables):
    (row_re, row_im), (twid_re, twid_im), (col_re, col_im) = tables
    rows_n = spec_re.shape[1]
    half_rows = rows_n // 2
    mid_re = jnp.einsum("ckn,nm->ckm", spec_re, col_re, precision=HIGHEST) + jnp.einsum(
        "ckn,nm->ckm", spec_im, col_im, precision=HIGHEST
    )
    mid_im = jnp.einsum("ckn,nm->ckm", spec_im, col_re, precision=HIGHEST) - jnp.einsum(
        "ckn,nm->ckm", spec_re, col_im, precision=HIGHEST
    )
    back_re = mid_re * twid_re + mid_im * twid_im
    back_im = mid_im * twid_re - mid_re * twid_im
    signal = jnp.einsum("nk,ckm->cnm", row_re[:half_rows], back_re, precision=HIGHEST) + jnp.einsum(
        "nk,ckm->cnm", row_im[:half_rows], back_im, precision=HIGHEST
    )
    return signal.reshape(signal.shape[0], half_rows * 128) * (1.0 / (rows_n * 128))


def long_filter(filt, mixed_in, grad_in, skip_part):
    rows_n = 2 * mixed_in.shape[1] // 128
    tables = (
        dft_table(rows_n, rows_n, rows_n),
        dft_table(rows_n, 128, rows_n * 128),
        dft_table(128, 128, 128),
    )
    mixed_f = mixed_in.astype(jnp.float32)
    grad_f = grad_in.astype(jnp.float32)
    filt_re, filt_im = forward_transform(filt.astype(jnp.float32), tables)
    mix_re, mix_im = forward_transform(mixed_f, tables)
    grad_re, grad_im = forward_transform(grad_f, tables)
    conv_out = inverse_transform(
        filt_re * mix_re - filt_im * mix_im, filt_re * mix_im + filt_im * mix_re, tables
    )
    corr_out = inverse_transform(
        filt_re * grad_re + filt_im * grad_im, filt_re * grad_im - filt_im * grad_re, tables
    )
    y_out = (conv_out + skip_part[:, None] * mixed_f).astype(jnp.bfloat16)
    dmixed = (corr_out + skip_part[:, None] * grad_f).astype(jnp.bfloat16)
    return (y_out, dmixed)


DENSE_MAX = 1024
FINE = 32


def angle_parts(length):
    base = np.arange(length, dtype=np.int64) * 4 + 1
    fine = np.arange(FINE, dtype=np.int64)[:, None] * base[None, :] % (4 * length)
    coarse = np.arange(0, length, FINE, dtype=np.int64)[:, None] * base[None, :] % (4 * length)
    scale = 2.0 * np.pi / (4 * length)
    return [
        func(part * scale).astype(np.float32)
        for part in (coarse, fine)
        for func in (np.cos, np.sin)
    ]


def dense_filter(filt, mixed_in, grad_in, skip_part):
    length = mixed_in.shape[1]
    cc, cs, fc, fs = [jnp.asarray(p)[:, None] if i < 2 else jnp.asarray(p)[None] for i, p in enumerate(angle_parts(length))]
    cos_t = (cc * fc - cs * fs).reshape(length, length)
    sin_t = (cs * fc + cc * fs).reshape(length, length)
    table = jnp.concatenate([cos_t, sin_t], axis=1).astype(jnp.bfloat16)

    def fwd(x):
        return jnp.dot(x, table, preferred_element_type=jnp.float32)

    def inv(x):
        return lax.dot_general(x.astype(jnp.bfloat16), table, (((1,), (1,)), ((), ())), preferred_element_type=jnp.float32) * (1.0 / length)

    h, m, g = fwd(filt), fwd(mixed_in), fwd(grad_in)
    hc, hs = h[:, :length], h[:, length:]
    mc, ms = m[:, :length], m[:, length:]
    gc, gs = g[:, :length], g[:, length:]
    conv_out = inv(jnp.concatenate([hc * mc - hs * ms, hc * ms + hs * mc], axis=1))
    corr_out = inv(jnp.concatenate([hc * gc + hs * gs, hc * gs - hs * gc], axis=1))
    y_out = (conv_out + skip_part[:, None] * mixed_in.astype(jnp.float32)).astype(jnp.bfloat16)
    dmixed = (corr_out + skip_part[:, None] * grad_in.astype(jnp.float32)).astype(jnp.bfloat16)
    return (y_out, dmixed)


def to_channels(stacked):
    return lax.all_to_all(stacked, "seq", split_axis=1, concat_axis=2, tiled=True)


def to_sequence(stacked):
    return lax.all_to_all(stacked, "seq", split_axis=2, concat_axis=1, tiled=True)


def local_general(features, dout, filters, taps, skip, lengths):
    blocks = lax.axis_size("seq")
    seq_rank = lax.axis_index("seq")
    span_rows = features.shape[2]
    channels_here = features.shape[1]
    chan_part = channels_here // blocks
    count = taps.shape[1]
    margin = count - 1
    rim = shifted(features[:, :, span_rows - margin :], "seq", 1)
    extended = jnp.concatenate([rim, features], axis=2)
    first_pos = seq_rank * span_rows
    offsets = genome_offsets(lengths, first_pos + jnp.arange(span_rows, dtype=jnp.int32))
    filtered = short_forward(extended, taps, offsets).astype(jnp.bfloat16)
    query_side = filtered[0].astype(jnp.float32)
    key_side = filtered[1].astype(jnp.float32)
    value_side = filtered[2].astype(jnp.float32)
    dout_f = dout.astype(jnp.float32)
    mixed = (key_side * value_side).astype(jnp.bfloat16)
    grad_in = (dout_f * query_side).astype(jnp.bfloat16)
    moved = to_channels(jnp.stack([mixed, grad_in, filters]))
    skip_part = lax.dynamic_slice_in_dim(skip, seq_rank * chan_part, chan_part, 0)
    run = dense_filter if moved.shape[2] <= DENSE_MAX else long_filter
    y_out, dmixed = run(moved[2], moved[0], moved[1], skip_part)
    returned = to_sequence(jnp.stack([y_out, dmixed]))
    y_here = returned[0].astype(jnp.float32)
    dmixed_here = returned[1].astype(jnp.float32)
    out = (query_side * y_here).astype(jnp.bfloat16)
    grads = jnp.stack([dout_f * y_here, dmixed_here * value_side, dmixed_here * key_side])
    ahead = shifted(grads[:, :, :margin], "seq", -1)
    grads_ext = jnp.concatenate([grads, ahead], axis=2)
    offsets_ext = genome_offsets(
        lengths, first_pos + jnp.arange(span_rows + margin, dtype=jnp.int32)
    )
    dfeatures = short_backward(grads_ext, taps, offsets_ext).astype(jnp.bfloat16)
    return (out, dfeatures)


CH = 128
BACK = 1
RELAY = 5
HOLD = 4
NN = (((1,), (0,)), ((), ()))
NT = (((1,), (1,)), ((), ()))
TN = (((0,), (0,)), ((), ()))
MESH = pl.DeviceIdType.MESH


def mm(a, b, dims=NN):
    return lax.dot_general(a, b, dims, preferred_element_type=jnp.float32)


def block_tables(size):
    place = np.arange(size, dtype=np.int64)
    phase = place[:, None] * (4 * place[None, :] + 1) % (4 * size)
    angle = phase * (2.0 * np.pi / (4 * size))
    cos, sin = np.cos(angle), np.sin(angle)
    there = np.stack([np.concatenate([cos, s * sin], axis=1) for s in (1, -1)])
    back = np.stack([np.concatenate([cos.T, s * sin.T], axis=0) for s in (1, -1)]) / size
    return there.astype(jnp.bfloat16), back.astype(jnp.bfloat16)


def mixer_kernel(
    lengths_hbm, feat_hbm, dout_hbm, filt_hbm, taps_hbm, skip_hbm, there_hbm, back_hbm,
    out_ref, df_ref,
    lengths_ref, xf, xd, taps_v, skip_v, par, wh, wsig, winv, keep_f, keep_b,
    rim_src, rim, h_all, sig, q_s, k_s, v_s, yd, w_loc, c_src, c_in,
    hal_src, hal, mini_src, mini, mini_own, spec_s, spec_h, prod,
    ld, rim_ss, rim_rs, h_zs, h_ys, h_bs, h_rs, u_ss, u_rs, c_ss, c_rs, hal_ss, hal_rs, mini_ss, mini_rs,
):
    rank = lax.axis_index("seq")
    group = lax.axis_index("groups")
    channels, span = xd.shape
    count = channels // CH
    half = count // 2
    mir = rank // 2
    inn = lax.rem(rank + mir, 2)
    inner = inn == 1
    inward = rank + 1 - 2 * mir
    outward = rank - 1 + 2 * mir
    far = 3 - 3 * mir
    bf = jnp.bfloat16
    f32 = jnp.float32

    def greet(**where):
        pl.semaphore_signal(barrier, inc=1, device_id=where, device_id_type=MESH)

    barrier = pltpu.get_barrier_semaphore()
    greet(seq=inward)

    @pl.when(inner)
    def _():
        greet(seq=outward)

    @pl.when(inn == 0)
    def _():
        greet(seq=2 - mir)

    @pl.when(rank > 0)
    def _():
        greet(groups=1 - group)

    loads = [
        pltpu.make_async_copy(feat_hbm, xf, ld.at[0]),
        pltpu.make_async_copy(taps_hbm, taps_v, ld.at[1]),
        pltpu.make_async_copy(skip_hbm, skip_v, ld.at[2]),
        pltpu.make_async_copy(dout_hbm, xd, ld.at[3]),
        pltpu.make_async_copy(filt_hbm, h_all.at[rank], ld.at[4]),
        pltpu.make_async_copy(there_hbm.at[0], wh, ld.at[5]),
        pltpu.make_async_copy(there_hbm.at[mir], wsig, ld.at[6]),
        pltpu.make_async_copy(back_hbm.at[mir], winv, ld.at[7]),
        pltpu.make_async_copy(lengths_hbm, lengths_ref, ld.at[8]),
    ]
    for load in loads:
        load.start()

    def rows_of(i):
        c = lax.rem(half * group + i, count)
        return c, pl.ds(pl.multiple_of(c * CH, CH), CH)

    def remote(src, dst, ss, rs, where):
        return pltpu.make_async_remote_copy(
            src_ref=src, dst_ref=dst, send_sem=ss, recv_sem=rs, device_id=where, device_id_type=MESH
        )

    def h_own_copy(i):
        c, rows = rows_of(i)
        return remote(filt_hbm.at[rows], h_all.at[rank, rows], h_zs.at[0, i], h_rs.at[rank, c], {"seq": inward})

    def h_on_copy(i):
        c, rows = rows_of(i)
        return remote(h_all.at[outward, rows], h_all.at[outward, rows], h_zs.at[1, i], h_rs.at[outward, c], {"seq": inward})

    def h_back_copy(i):
        c, rows = rows_of(i)
        return remote(h_all.at[0, rows], h_all.at[0, rows], h_bs.at[i], h_rs.at[0, c], {"seq": 3})

    def h_over_copy(which, slot, i):
        c, rows = rows_of(i)
        return remote(
            h_all.at[slot, rows], h_all.at[slot, rows], h_ys.at[which, i], h_rs.at[slot, c], {"groups": 1 - group}
        )

    def h_arrival(slot, i):
        c, rows = rows_of(i)
        return remote(h_all.at[slot, rows], h_all.at[slot, rows], h_zs.at[0, 0], h_rs.at[slot, c], {"seq": inward})

    def u_copy(i):
        c, rows = rows_of(i)
        return remote(sig.at[0, rows], sig.at[2, rows], u_ss.at[i], u_rs.at[c], {"seq": inward})

    def c_copy(which, i):
        c, rows = rows_of(i)
        direct = (i >= RELAY).astype(jnp.int32)
        slot = (0, 1 - direct, 1)[which]
        where = (inward, inward + (far - inward) * direct, outward)[which]
        return remote(
            c_src.at[which, rows], c_in.at[slot, rows], c_ss.at[which, i], c_rs.at[slot, c], {"seq": where}
        )

    def c_arrival(slot, i):
        c, rows = rows_of(i)
        return remote(c_in.at[slot, rows], c_in.at[slot, rows], c_ss.at[0, i], c_rs.at[slot, c], {"seq": inward})

    def mini_copy(i):
        c, _ = rows_of(i)
        where = (2 - 2 * mir) * (i >= RELAY).astype(jnp.int32)
        return remote(mini_src.at[c], mini.at[c], mini_ss.at[i], mini_rs.at[c], {"seq": where})

    def rim_copy():
        return remote(rim_src, rim, rim_ss, rim_rs, {"seq": jnp.minimum(rank + 1, 3)})

    def hal_copy(i):
        c, _ = rows_of(i)
        return remote(hal_src.at[c], hal.at[c], hal_ss.at[i], hal_rs.at[c], {"seq": jnp.maximum(rank - 1, 0)})

    @pl.when(rank == 0)
    def _():
        rim[...] = jnp.zeros_like(rim)

    @pl.when(rank == 3)
    def _():
        hal[...] = jnp.zeros_like(hal)

    @pl.when(lax.rem(rank, 2) == 1)
    def _():
        mini[...] = jnp.zeros_like(mini)

    @pl.when(rank == 2)
    def _():
        for i in range(min(RELAY, count)):
            mini[rows_of(i)[0]] = jnp.zeros((16, CH), bf)

    @pl.when(inn == 0)
    def _():
        mini_own[...] = jnp.zeros_like(mini_own)

    pl.semaphore_wait(barrier, 1 + 3 * inn + rank // 3)

    h_own_copy(0).start()

    loads[0].wait()
    r_id = lax.broadcasted_iota(jnp.int32, (16, 128), 0)
    p_id = lax.broadcasted_iota(jnp.int32, (16, 128), 1)
    total = None
    for part in range(2):
        for a in range(3):
            first = 8 * part + 2 * a
            hit = ((r_id == first) & (p_id == 126)) | ((r_id == first + 1) & (p_id == 127))
            edge = xf[a, part * half * CH : (part + 1) * half * CH, span - 128 :]
            term = mm(jnp.where(hit, 1.0, 0.0).astype(bf), edge, NT)
            total = term if total is None else total + term
    rim_src[...] = total.astype(bf)

    @pl.when(rank < 3)
    def _():
        rim_copy().start()

    for i in range(1, max(half - 1, 1)):
        h_own_copy(i).start()

    @pl.when(inn == 0)
    def _():
        for i in range(max(half - 1, 1), half):
            h_own_copy(i).start()

    loads[8].wait()

    def keeps(ahead, least):
        position = rank * span + ahead + lax.broadcasted_iota(jnp.int32, (8, span), 1)
        offset = position
        end = jnp.int32(0)
        for g in range(lengths_ref.shape[0]):
            one = lengths_ref[g]
            end = end + one
            offset = offset - jnp.where(end <= position, one, 0)
        return jnp.where(offset >= least, 1.0, 0.0)

    for j in (1, 2):
        keep_f[j - 1] = keeps(0, j)
        keep_b[j - 1] = keeps(j, j)

    loads[1].wait()
    loads[2].wait()
    flat = jnp.concatenate(
        [taps_v[0], taps_v[1], taps_v[2], skip_v[...], jnp.zeros((6, channels), f32)], axis=0
    )
    for c in range(count):
        par[c * CH : (c + 1) * CH, 0:16] = flat[:, c * CH : (c + 1) * CH].T
    for load in loads[3:8]:
        load.wait()

    def pass_on(i):
        h_arrival(outward, i).wait_recv()
        h_on_copy(i).start()
        h_over_copy(0, outward, i).start()

    @pl.when(inner)
    def _():
        for i in range(min(2, half)):
            pass_on(i)
            if i == 0:
                for k in range(max(half - 1, 1), half):
                    h_own_copy(k).start()

    @pl.when(rank > 0)
    def _():
        rim_copy().wait_recv()

    rr = lax.broadcasted_iota(jnp.int32, (16, 384), 0)
    cc = lax.broadcasted_iota(jnp.int32, (16, 384), 1)

    def spread(first, above=0):
        hit = None
        for a in range(3):
            row = 2 * a + above
            one = ((rr == row) & (cc == 128 * a + first)) | ((rr == row + 1) & (cc == 128 * a + first + 1))
            hit = one if hit is None else hit | one
        return jnp.where(hit, 1.0, 0.0).astype(bf)

    def prepare(i):
        c, rows = rows_of(i)
        upper = c // half
        cols = pl.ds(pl.multiple_of((c - half * upper) * CH, CH), CH)
        edge = mm(rim[:, cols], spread(126, 8 * upper), TN)
        tap = par[rows, :]
        result = []
        for a in range(3):
            here = xf[a, rows, :].astype(f32)
            wide = jnp.concatenate([edge[:, 128 * a : 128 * a + 128], here], axis=1)
            acc = tap[:, 3 * a : 3 * a + 1] * here
            for j in (1, 2):
                moved = pltpu.roll(wide, j, 1)[:, 128:]
                acc = acc + tap[:, 3 * a + j : 3 * a + j + 1] * (moved * keep_f[j - 1, 0:1, :])
            result.append(acc.astype(bf))
        q, k, v = result
        q_s[rows, :] = q
        k_s[rows, :] = k
        v_s[rows, :] = v
        sig[mir, rows, :] = (k.astype(f32) * v.astype(f32)).astype(bf)
        sig[1 - mir, rows, :] = (xd[rows, :].astype(f32) * q.astype(f32)).astype(bf)

        @pl.when(inn == 0)
        def _():
            u_copy(i).start()

        @pl.when(inner & (i + 2 < half))
        def _():
            pass_on(i + 2)

    def pick(block, rows_at):
        hit = None
        for first, lane in rows_at:
            one = ((r_id == first) & (p_id == lane)) | ((r_id == first + 1) & (p_id == lane + 1))
            hit = one if hit is None else hit | one
        return mm(jnp.where(hit, 1.0, 0.0).astype(bf), block, NT)

    def keep_local(rows, value):
        skip = par[rows, 9:10]
        yd[0, rows, :] = (value[0:CH] + skip * sig[0, rows, :].astype(f32)).astype(bf)
        other = value[CH : 2 * CH] + skip * sig[1, rows, :].astype(f32)
        w_loc[rows, :] = other
        yd[1, rows, :] = other.astype(bf)

    def products(terms_of):
        def block(b, carry):
            first = pl.multiple_of(b * 16, 16)

            def pair(ref, k):
                at = pl.ds(k * CH + first, 16)
                return ref[at, 0:span], ref[at, span:]

            for k, terms in enumerate(terms_of(lambda n: pair(spec_h, n), lambda n: pair(spec_s, n))):
                re = im = None
                for (tc, ts), (xc, xs), sign in terms:
                    if sign > 0:
                        new_re, new_im = tc * xc - ts * xs, tc * xs + ts * xc
                    else:
                        new_re, new_im = tc * xc + ts * xs, tc * xs - ts * xc
                    re = new_re if re is None else re + new_re
                    im = new_im if im is None else im + new_im
                at = pl.ds(k * CH + first, 16)
                prod[at, 0:span] = re.astype(bf)
                prod[at, span:] = im.astype(bf)
            return carry

        lax.fori_loop(0, CH // 16, block, 0, unroll=8)

    def inner_terms(h, s):
        hs = [h(k) for k in range(4)]
        t = [hs[0]] + [(hs[k][0] + hs[k - 1][1], hs[k][1] - hs[k - 1][0]) for k in (1, 2, 3)]
        own, other, near = [s(k) for k in range(3)]
        return [
            [(t[0], own, 1), (t[1], near, 1)],
            [(t[0], other, -1)],
            [(t[1], own, 1), (t[2], near, 1)],
            [(t[2], own, 1), (t[3], near, 1)],
            [(t[1], other, -1)],
        ]

    def outer_terms(h, s):
        return [[(h(0), s(0), 1)], [(h(0), s(1), -1)]]

    def main_inner(i):
        c, rows = rows_of(i)

        @pl.when(i < half)
        def _():
            h_arrival(inward, i).wait_recv()
            h_over_copy(1, inward, i).start()
            h_arrival(far, i).wait_recv()
            h_over_copy(2, far, i).start()

            @pl.when(rank == 2)
            def _():
                h_back_copy(i).start()

        @pl.when(i >= half)
        def _():
            h_arrival(outward, i).wait_recv()
            h_arrival(inward, i).wait_recv()
            h_arrival(far, i).wait_recv()

        u_copy(i).wait_recv()
        spec_h[...] = mm(h_all[:, rows, :].reshape(4 * CH, span), wh[...])
        spec_s[...] = mm(sig[:, rows, :].reshape(3 * CH, span), wsig[...])
        products(inner_terms)
        value = mm(prod[...], winv[...])
        for which in range(3):
            c_src[which, rows, :] = value[(2 + which) * CH : (3 + which) * CH].astype(bf)

        @pl.when(i >= RELAY)
        def _():
            mini_src[c] = pick(c_src[1 - mir, rows, 0:128], [(8 - 6 * mir, 0), (8 - 4 * mir, 0)]).astype(bf)
            mini_copy(i).start()

        c_copy(1, i).start()

        @pl.when(i >= RELAY)
        def _():
            c_copy(2, i).start()

        keep_local(rows, value)
        halo(i)
        c_copy(0, i).start()

        @pl.when((rank == 1) | (i >= RELAY))
        def _():
            mini_own[c] = pick(c_src[2 * mir, rows, 0:128], [(8, 0)]).astype(bf)

    def relay(i):
        c, rows = rows_of(i)
        c_arrival(1, i).wait_recv()
        c_src[2, rows, :] = (c_src[2, rows, :].astype(f32) + c_in[1, rows, :].astype(f32)).astype(bf)
        c_copy(2, i).start()
        c_arrival(0, i).wait_recv()

        @pl.when(rank == 1)
        def _():
            mini_src[c] = pick(c_in[0, rows, 0:128], [(2, 0), (4, 0)]).astype(bf)
            mini_copy(i).start()

        @pl.when(rank == 2)
        def _():
            mini_own[c] = pick(c_src[2, rows, 0:128], [(8, 0)]).astype(bf)

    def main_outer(i):
        c, rows = rows_of(i)

        @pl.when(rank == 3)
        def _():
            h_arrival(0, i).wait_recv()

            @pl.when(i < half)
            def _():
                h_over_copy(0, 0, i).start()

        spec_h[0:CH] = mm(h_all[0, rows, :], wh[...])
        spec_s[0 : 2 * CH] = mm(sig[0:2, rows, :].reshape(2 * CH, span), wsig[...])
        products(outer_terms)
        keep_local(rows, mm(prod[0 : 2 * CH], winv[...]))

    def grad_of(a, rows):
        if a == 0:
            return xd[rows, :].astype(f32) * yd[mir, rows, :].astype(f32)
        other = v_s if a == 1 else k_s
        return yd[1 - mir, rows, :].astype(f32) * other[rows, :].astype(f32)

    def halo(i):
        c, rows = rows_of(i)
        first = slice(0, 128)
        edge = pick(xd[rows, first], [(0, 0)]) + pick(yd[1 - mir, rows, first], [(2, 0), (4, 0)])
        edge = edge + pick(yd[mir, rows, first], [(8, 0)])
        edge = edge + pick(v_s[rows, first], [(10, 0)]) + pick(k_s[rows, first], [(12, 0)])
        hal_src[c] = edge.astype(bf)
        hal_copy(i).start()

    def gates(rows, edges, arrays):
        tap = par[rows, :]
        first_grads = jnp.concatenate([edges[0:8] * edges[8:16], jnp.zeros((8, CH), f32)], axis=0)
        edge = mm(first_grads.astype(bf), spread(0), TN)
        if 0 in arrays:
            out_ref[rows, :] = (q_s[rows, :].astype(f32) * yd[mir, rows, :].astype(f32)).astype(bf)
        for a in arrays:
            grad = grad_of(a, rows)
            wide = jnp.concatenate([grad, edge[:, 128 * a : 128 * a + 128]], axis=1)
            acc = tap[:, 3 * a : 3 * a + 1] * grad
            for j in (1, 2):
                moved = pltpu.roll(wide, span + 128 - j, 1)[:, :span]
                acc = acc + tap[:, 3 * a + j : 3 * a + j + 1] * (moved * keep_b[j - 1, 0:1, :])
            df_ref[a, rows, :] = acc.astype(bf)

    def early(i):
        c, rows = rows_of(i)

        @pl.when(rank < 3)
        def _():
            hal_copy(i).wait_recv()

        edges = hal[c].astype(f32) + mini_own[c].astype(f32)

        @pl.when(mir == 0)
        def _():
            gates(rows, edges, (0,))

        @pl.when(mir == 1)
        def _():
            gates(rows, edges, (1, 2))

    def late(i):
        c, rows = rows_of(i)

        @pl.when(i >= RELAY)
        def _():
            c_arrival(0, i).wait_recv()

        @pl.when(inner)
        def _():
            yd[1, rows, :] = (w_loc[rows, :] + c_in[0, rows, :].astype(f32)).astype(bf)

        @pl.when((inn == 0) & (i >= RELAY))
        def _():
            c_arrival(1, i).wait_recv()
            cross = c_in[0, rows, :].astype(f32) + c_in[1, rows, :].astype(f32)
            yd[1, rows, :] = (w_loc[rows, :] + cross).astype(bf)

        @pl.when((inn == 0) & (i < RELAY))
        def _():
            c_arrival(1, i).wait_recv()
            yd[1, rows, :] = (w_loc[rows, :] + c_in[1, rows, :].astype(f32)).astype(bf)

        @pl.when((rank == 0) | ((rank == 2) & (i >= RELAY)))
        def _():
            mini_copy(i).wait_recv()

        edges = hal[c].astype(f32) + mini[c].astype(f32) + mini_own[c].astype(f32)

        @pl.when(mir == 0)
        def _():
            gates(rows, edges, (1, 2))

        @pl.when(mir == 1)
        def _():
            gates(rows, edges, (0,))

    def first_steps(s, carry):
        prepare(s)
        return carry

    lax.fori_loop(0, count, first_steps, 0)

    def step(s, carry):
        main = s < count

        @pl.when(inner & main)
        def _():
            main_inner(s)

        @pl.when((inn == 0) & main)
        def _():
            main_outer(s)

        @pl.when((rank == 3) & main)
        def _():
            halo(s)

        @pl.when(inner & (s >= HOLD) & (s < RELAY + HOLD) & (s < count + HOLD))
        def _():
            relay(s - HOLD)

        return carry

    lax.fori_loop(0, max(count, min(RELAY, count) + HOLD), step, 0)

    def last_steps(s, carry):
        @pl.when(s < count)
        def _():
            early(s)

        @pl.when(s >= BACK)
        def _():
            late(s - BACK)

        return carry

    lax.fori_loop(0, count + BACK, last_steps, 0)

    @pl.when(rank < 3)
    def _():
        rim_copy().wait_send()

    def drain(i, carry):
        @pl.when(inn == 0)
        def _():
            u_copy(i).wait_send()

        @pl.when(rank > 0)
        def _():
            hal_copy(i).wait_send()

        @pl.when(inner)
        def _():
            for which in range(3):
                c_copy(which, i).wait_send()

        @pl.when((rank == 1) | ((rank == 2) & (i >= RELAY)))
        def _():
            mini_copy(i).wait_send()

        @pl.when(i < half)
        def _():
            h_own_copy(i).wait_send()

            @pl.when(inner)
            def _():
                h_on_copy(i).wait_send()
                h_over_copy(0, outward, i).wait_send()
                h_over_copy(1, inward, i).wait_send()
                h_over_copy(2, far, i).wait_send()

            @pl.when(rank == 2)
            def _():
                h_back_copy(i).wait_send()

            @pl.when(rank == 3)
            def _():
                h_over_copy(0, 0, i).wait_send()

        return carry

    lax.fori_loop(0, count, drain, 0)


def local_kernel(features, dout, filters, taps, skip, lengths):
    channels, span = dout.shape
    count = channels // CH
    bf = jnp.bfloat16
    f32 = jnp.float32
    there, back = block_tables(span)
    operands = [lengths, features, dout, filters, taps, skip[None], jnp.asarray(there), jnp.asarray(back)]
    vmem = pl.BlockSpec(memory_space=pltpu.VMEM)
    hbm = pl.BlockSpec(memory_space=pltpu.HBM)
    dma = pltpu.SemaphoreType.DMA
    return pl.pallas_call(
        mixer_kernel,
        out_shape=(pltpu.VMEM(dout.shape, bf), pltpu.VMEM(features.shape, bf)),
        in_specs=[hbm] * 8,
        out_specs=(vmem, vmem),
        scratch_shapes=[
            pltpu.SMEM(lengths.shape, jnp.int32),
            pltpu.VMEM((3, channels, span), bf),
            pltpu.VMEM((channels, span), bf),
            pltpu.VMEM((3, 3, channels), f32),
            pltpu.VMEM((1, channels), f32),
            pltpu.VMEM((channels, 128), f32),
            pltpu.VMEM((span, 2 * span), bf),
            pltpu.VMEM((span, 2 * span), bf),
            pltpu.VMEM((2 * span, span), bf),
            pltpu.VMEM((2, 8, span), f32),
            pltpu.VMEM((2, 8, span), f32),
            pltpu.VMEM((16, channels // 2), bf),
            pltpu.VMEM((16, channels // 2), bf),
            pltpu.VMEM((4, channels, span), bf),
            pltpu.VMEM((3, channels, span), bf),
            pltpu.VMEM((channels, span), bf),
            pltpu.VMEM((channels, span), bf),
            pltpu.VMEM((channels, span), bf),
            pltpu.VMEM((2, channels, span), bf),
            pltpu.VMEM((channels, span), f32),
            pltpu.VMEM((3, channels, span), bf),
            pltpu.VMEM((2, channels, span), bf),
            pltpu.VMEM((count, 16, CH), bf),
            pltpu.VMEM((count, 16, CH), bf),
            pltpu.VMEM((count, 16, CH), bf),
            pltpu.VMEM((count, 16, CH), bf),
            pltpu.VMEM((count, 16, CH), bf),
            pltpu.VMEM((3 * CH, 2 * span), f32),
            pltpu.VMEM((4 * CH, 2 * span), f32),
            pltpu.VMEM((5 * CH, 2 * span), bf),
            dma((9,)), dma, dma,
            dma((2, count)), dma((3, count)), dma((count,)), dma((4, count)),
            dma((count,)), dma((count,)), dma((3, count)), dma((2, count)),
            dma((count,)), dma((count,)), dma((count,)), dma((count,)),
        ],
        compiler_params=pltpu.CompilerParams(
            collective_id=0, has_side_effects=True, vmem_limit_bytes=32 * 1024 * 1024
        ),
    )(*[pltpu.with_memory_space_constraint(x, pltpu.HBM) for x in operands])


def local(features, dout, filters, taps, skip, lengths):
    channels, span = dout.shape
    fits = lax.axis_size("seq") == 4 and lax.axis_size("groups") == 2 and taps.shape[:2] == (3, 3)
    if fits and span == 256 and channels % (2 * CH) == 0:
        return local_kernel(features, dout, filters, taps, skip, lengths)
    return local_general(features, dout, filters, taps, skip, lengths)


def solution(mesh):
    in_specs = (
        P(None, ("chan", "sub"), ("groups", "seq")),
        P(("chan", "sub"), ("groups", "seq")),
        P(("chan", "sub"), "seq"),
        P(None, None, ("chan", "sub")),
        P(("chan", "sub")),
        P("groups"),
    )
    out_specs = (P(("chan", "sub"), ("groups", "seq")), P(None, ("chan", "sub"), ("groups", "seq")))
    return jax.shard_map(local, mesh=mesh, in_specs=in_specs, out_specs=out_specs, check_vma=False)
```
